32 devices in a mesh: ctx: 8 (over y, x, core), fsdp: 4 (over z).
Axes of the slice: x: 2, y: 2, z: 4, core: 2. Of those that a mesh axis runs over, the one named last changes fastest.
Arguments:
- inputs: bfloat16 [2048, 8, 1024], P('ctx', 'fsdp'), may hold values from -6 to 6
- w_query: bfloat16 [1024, 1024], P('fsdp'), may hold values from -0.25 to 0.25
- w_key: bfloat16 [1024, 1024], P('fsdp'), may hold values from -0.25 to 0.25
- w_value: bfloat16 [1024, 1024], P('fsdp'), may hold values from -0.1875 to 0.1875
- w_out: bfloat16 [1024, 1024], P('fsdp'), may hold values from -0.75 to 0.75
- w_gate: bfloat16 [1024, 4096], P('fsdp'), may hold values from -0.1875 to 0.1875
- w_up: bfloat16 [1024, 4096], P('fsdp'), may hold values from -0.1875 to 0.1875
- w_down: bfloat16 [4096, 1024], P('fsdp'), may hold values from -0.125 to 0.125
- gain_attn: bfloat16 [1024], P('fsdp'), may hold values from 0.25 to 1.75
- gain_ffn: bfloat16 [1024], P('fsdp'), may hold values from 0.25 to 1.75
- segments: int32 [2048, 8], P(None, 'fsdp'), may hold values from 0 to 2047
- deal_order: int32 [16], replicated, may hold values from 0 to 15, as said below
- cotangent: bfloat16 [2048, 8, 1024], P('ctx', 'fsdp'), may hold values from -6 to 6
Outputs:
- output: bfloat16 [2048, 8, 1024], P('ctx', 'fsdp')
- grad_inputs: bfloat16 [2048, 8, 1024], P('ctx', 'fsdp')
- grad_w_query: float32 [1024, 1024], P('fsdp')
- grad_w_key: float32 [1024, 1024], P('fsdp')
- grad_w_value: float32 [1024, 1024], P('fsdp')
- grad_w_out: float32 [1024, 1024], P('fsdp')
- grad_w_gate: float32 [1024, 4096], P('fsdp')
- grad_w_up: float32 [1024, 4096], P('fsdp')
- grad_w_down: float32 [4096, 1024], P('fsdp')
- grad_gain_attn: float32 [1024], P('fsdp')
- grad_gain_ffn: float32 [1024], P('fsdp')
The draws below stay inside these ranges and needn't reach their ends.
Inputs may be any that keep to these rules, and one draw needn't show every extreme that they name: deal_order is a permutation of the 16 blocks in which entries 2c and 2c + 1 are some p and 15 - p.
All inputs are finite; a program needn't handle non-finite values.
Results may differ from the reference program's by a relative error of at most 0.023.
Values may be sent and summed in bfloat16 or wider, within the bound.
No kernel may reach another device: no remote copies, remote signals or barrier semaphores. Data moves between devices by JAX's collectives and lax.ppermute only.
A program may use at most 320 MiB of HBM per device.

```python
import jax
import jax.numpy as jnp
from jax import lax

HEADS = 16
HEAD_DIM = 64
D = 1024
FF = 4096
BLK = 128
DOC_MIN = 200
DOC_MAX = 2000
SEQ = 2048
SEQS = 8


def dealt_blocks(key):
    pairs_count = SEQ // (2 * BLK)
    chosen = jax.random.permutation(jax.random.fold_in(key, 11), pairs_count).astype(jnp.int32)
    mirrored = 2 * pairs_count - 1 - chosen
    return jnp.stack([chosen, mirrored], axis=1).reshape(2 * pairs_count).astype(jnp.int32)


def draw_deal_order(key, part):
    return dealt_blocks(key)


def last_rows(number_row):
    return (jnp.searchsorted(number_row, number_row, side='right') - 1).astype(jnp.int32)


def draw_segments(key, part):
    block_order = dealt_blocks(key)
    doc_count = SEQ // DOC_MIN + 2
    lengths = jax.random.randint(jax.random.fold_in(key, 13), (SEQS, doc_count), DOC_MIN, DOC_MAX + 1)
    side_pick = jax.random.randint(jax.random.fold_in(key, 17), (SEQS,), 0, 2)
    first_len = jnp.where(side_pick == 0, DOC_MAX, lengths[:, 0])
    lengths = jnp.concatenate([first_len[:, None], lengths[:, 1:]], axis=1)
    doc_ends = jnp.cumsum(lengths, axis=1)
    places = jnp.arange(SEQ, dtype=jnp.int32)
    numbers = jnp.sum(places[None, :, None] >= doc_ends[:, None, :], axis=2).astype(jnp.int32)
    border = SEQ - DOC_MAX
    before_id = jnp.sum(doc_ends <= border - 1, axis=1).astype(jnp.int32)
    at_tail = (places[None, :] >= border) & (side_pick[:, None] == 1)
    numbers = jnp.where(at_tail, before_id[:, None] + 1, numbers).astype(jnp.int32)
    labels = jax.vmap(last_rows)(numbers)
    slot_places = (block_order[:, None] * BLK + jnp.arange(BLK, dtype=jnp.int32)[None, :]).reshape(SEQ)
    return jnp.take(labels, slot_places, axis=1).T.astype(jnp.int32)


def steps_of(rng, dims, split, low, largest):
    factor_of = 1.0
    for dim, blocks in split:
        heights = jax.random.uniform(jax.random.fold_in(jax.random.fold_in(rng, 6), dim), (blocks,), jnp.float32, low / len(split), largest / len(split))
        factor_of = factor_of * jnp.repeat(jnp.exp(heights), dims[dim] // blocks).reshape((-1,) + (1,) * (len(dims) - 1 - dim))
    return factor_of


def scatter_about(own_key, extent, width, bound, cuts=(), kind=jnp.bfloat16):
    loudness = steps_of(own_key, extent, cuts, -0.22, 0.18) if cuts else 1.0
    array = jax.random.normal(own_key, extent, jnp.float32) * width * loudness
    return jnp.minimum(jnp.maximum(array, -bound), bound).astype(kind)


def setup_inputs(seed: int = 0) -> dict:
    splits = jax.random.split(jax.random.key(seed), 14)
    return {
        "inputs": scatter_about(splits[0], (SEQ, SEQS, D), 1.0, 6.0, ((0, 8), (1, 4))),
        "w_query": scatter_about(splits[1], (D, D), (D // 2) ** -0.5, 0.25, ((0, 4),)),
        "w_key": scatter_about(splits[2], (D, D), (D // 2) ** -0.5, 0.25, ((0, 4),)),
        "w_value": scatter_about(splits[3], (D, D), D ** -0.5, 0.1875, ((0, 4),)),
        "w_out": scatter_about(splits[4], (D, D), (D // 16) ** -0.5, 0.75, ((0, 4),)),
        "w_gate": scatter_about(splits[5], (D, FF), D ** -0.5, 0.1875, ((0, 4),)),
        "w_up": scatter_about(splits[6], (D, FF), D ** -0.5, 0.1875, ((0, 4),)),
        "w_down": scatter_about(splits[7], (FF, D), (FF // 2) ** -0.5, 0.125, ((0, 4),)),
        "gain_attn": jnp.clip(1.0 + 0.15 * jax.random.normal(splits[8], (D,), jnp.float32), 0.25, 1.75).astype(jnp.bfloat16),
        "gain_ffn": jnp.clip(1.0 + 0.15 * jax.random.normal(splits[9], (D,), jnp.float32), 0.25, 1.75).astype(jnp.bfloat16),
        "segments": draw_segments(jax.random.fold_in(splits[13], 71), 0),
        "deal_order": draw_deal_order(jax.random.fold_in(splits[13], 71), 0),
        "cotangent": scatter_about(splits[12], (SEQ, SEQS, D), 1.0, 6.0, ((0, 8), (1, 4))),
    }


epsilon = 1e-05
highest = lax.Precision.HIGHEST

@jax.custom_vjp
def low(v):
    return lax.optimization_barrier(v.astype(jnp.bfloat16)).astype(jnp.float32)

@jax.custom_vjp
def low_back(v):
    return v

def low_keep(v):
    return (low(v), None)

def low_pass(kept, grad):
    return (grad,)

def back_keep(v):
    return (v, None)

def back_low(kept, grad):
    return (low(grad),)
low.defvjp(low_keep, low_pass)
low_back.defvjp(back_keep, back_low)

def matmul(left_op, right_op):
    return jnp.dot(left_op, right_op, precision=highest, preferred_element_type=jnp.float32)

def norm_rows(values, gain):
    return values * lax.rsqrt(lax.optimization_barrier(jnp.mean(values * values, axis=-1, keepdims=True)) + epsilon) * gain

def attend_block(queries, q_pos, q_seg, key_rows, values, k_pos, k_seg):
    scores = jnp.einsum('qhd,khd->hqk', queries, key_rows, precision=highest) * HEAD_DIM ** (-0.5)
    scores = low_back(scores)
    allowed = (q_seg[:, None] == k_seg[None, :]) & (k_pos[None, :] <= q_pos[:, None])
    scores = jnp.where(allowed[None], scores, -1e+30)
    prob_rows = jax.nn.softmax(scores, axis=-1)
    return jnp.einsum('hqk,khd->qhd', low(prob_rows), values, precision=highest)

def layer_sequence(seq_rows, seq_segs, positions, params):
    w_query, w_key, w_value, w_out, w_gate, w_up, w_down, gain_attn, gain_ffn = params
    block_rows = min(512, SEQ)
    block_count = SEQ // block_rows
    normed_in = low(norm_rows(seq_rows, gain_attn))
    query_rows = low(low_back(matmul(normed_in, w_query))).reshape(SEQ, HEADS, HEAD_DIM)
    key_rows = low(low_back(matmul(normed_in, w_key))).reshape(SEQ, HEADS, HEAD_DIM)
    value_rows = low(low_back(matmul(normed_in, w_value))).reshape(SEQ, HEADS, HEAD_DIM)
    attend_saved = jax.checkpoint(attend_block)
    attended = lax.map(lambda piece_set: attend_saved(piece_set[0], piece_set[1], piece_set[2], key_rows, value_rows, positions, seq_segs), (query_rows.reshape(block_count, block_rows, HEADS, HEAD_DIM), positions.reshape(block_count, block_rows), seq_segs.reshape(block_count, block_rows)))
    attended = low(low_back(attended.reshape(SEQ, D)))
    middle = seq_rows + low_back(matmul(attended, w_out))
    normed_mid = low(norm_rows(middle, gain_ffn))
    gate_pre = low_back(matmul(normed_mid, w_gate))
    up_pre = low_back(matmul(normed_mid, w_up))
    hidden = low(jax.nn.silu(gate_pre) * up_pre)
    return middle + matmul(hidden, w_down)

def reference(inputs, w_query, w_key, w_value, w_out, w_gate, w_up, w_down, gain_attn, gain_ffn, segments, deal_order, cotangent):
    offsets = jnp.arange(BLK, dtype=jnp.int32)
    positions = (deal_order[:, None] * BLK + offsets[None, :]).reshape(SEQ).astype(jnp.int32)
    params = tuple((weight.astype(jnp.float32) for weight in (w_query, w_key, w_value, w_out, w_gate, w_up, w_down, gain_attn, gain_ffn)))

    def forward(inputs_f, params_f):

        def seq_step(carried, seq_item):
            return (carried, layer_sequence(seq_item[0], seq_item[1], positions, params_f))
        _, outputs = lax.scan(seq_step, jnp.zeros((), jnp.float32), (jnp.swapaxes(inputs_f, 0, 1), jnp.swapaxes(segments, 0, 1)))
        return jnp.swapaxes(outputs, 0, 1)
    output, pullback = jax.vjp(forward, inputs.astype(jnp.float32), params)
    grad_inputs, grad_all = pullback(cotangent.astype(jnp.float32))
    return (output.astype(jnp.bfloat16), grad_inputs.astype(jnp.bfloat16), grad_all[0], grad_all[1], grad_all[2], grad_all[3], grad_all[4], grad_all[5], grad_all[6], grad_all[7], grad_all[8])
```

```python
import functools

import jax
import jax.numpy as jnp
from jax import lax
from jax.experimental import pallas as pl
from jax.experimental.pallas import tpu as pltpu
from jax.sharding import Mesh, PartitionSpec as P

HEAD_DIM = 64
EPSILON = 1e-05
MASKED = -1e30
TILE = 256
PLANE = ("chip", "core")

bf16 = jnp.bfloat16
f32 = jnp.float32


def dot_nn(left_op, right_op):
    return lax.dot_general(left_op, right_op, (((1,), (0,)), ((), ())), preferred_element_type=f32)


def dot_nt(left_op, right_op):
    return lax.dot_general(left_op, right_op, (((1,), (1,)), ((), ())), preferred_element_type=f32)


def dot_tn(left_op, right_op):
    return lax.dot_general(left_op, right_op, (((0,), (0,)), ((), ())), preferred_element_type=f32)


def row_scale(values):
    return lax.rsqrt(jnp.mean(values * values, axis=-1, keepdims=True) + EPSILON)


def swap_core(value):
    return lax.ppermute(value, "core", [(0, 1), (1, 0)])


def swap_chip(value, mask):
    count = lax.axis_size("chip")
    return lax.ppermute(value, "chip", [(i, i ^ mask) for i in range(count)])


def plane_gather(value):
    count = lax.axis_size("chip")
    if count != 4:
        return jnp.stack([value] + [swap_chip(value, r) for r in range(1, count)])
    half = value.shape[0] // 2
    top, low = value[:half], value[half:]
    top_x = swap_chip(top, 1)
    low_y = swap_chip(low, 2)
    top_y = swap_chip(jnp.stack([top, top_x]), 2)
    low_x = swap_chip(jnp.stack([low, low_y]), 1)
    tops = jnp.stack([top, top_x, top_y[0], top_y[1]])
    lows = jnp.stack([low, low_x[0], low_y, low_x[1]])
    return jnp.concatenate([tops, lows], axis=1)


def gather_all(value):
    near = plane_gather(value)
    return near, swap_core(near)


def plane_reduce(own, other):
    count = lax.axis_size("chip")
    total = (own.astype(f32) + swap_core(other).astype(f32)).astype(bf16)
    if count != 4:
        result = total[0].astype(f32)
        for r in range(1, count):
            result = result + swap_chip(total[r], r).astype(f32)
        return result
    half = own.shape[1] // 2
    top, low = total[:, :half], total[:, half:]
    got_x = swap_chip(jnp.stack([top[1], top[3]]), 1)
    got_y = swap_chip(jnp.stack([low[2], low[3]]), 2)
    top_two = (top[2].astype(f32) + got_x[1].astype(f32)).astype(bf16)
    low_one = (low[1].astype(f32) + got_y[1].astype(f32)).astype(bf16)
    last_y = swap_chip(top_two, 2)
    last_x = swap_chip(low_one, 1)
    return jnp.concatenate(
        [
            top[0].astype(f32) + got_x[0].astype(f32) + last_y.astype(f32),
            low[0].astype(f32) + got_y[0].astype(f32) + last_x.astype(f32),
        ]
    )


def head_masks(rows, width):
    lanes = lax.broadcasted_iota(jnp.int32, (rows, width), 1) // HEAD_DIM
    return [lanes == h for h in range(width // HEAD_DIM)]


def stack_heads(values, masks):
    zero = jnp.zeros_like(values)
    return jnp.concatenate([jnp.where(mask, values, zero) for mask in masks], axis=0)


def merge_heads(stacked, masks, rows):
    merged = stacked[:rows]
    for h in range(1, len(masks)):
        merged = jnp.where(masks[h], stacked[h * rows : (h + 1) * rows], merged)
    return merged


def forward_kernel(
    rel, send, first, full, x_near, x_far, weight, gain, start,
    query, key, value, normed, attended, fine, logsum,
    scores, top, total,
):
    width = query.shape[1]
    seq_len = query.shape[0]
    heads = width // HEAD_DIM
    blk = TILE // 2
    tiles = x_near.shape[0] // TILE
    gain_row = gain[...].astype(f32)
    for s, source in ((0, x_near), (1, x_far)):

        def project(t, _, s=s, source=source):
            rows = pl.ds(pl.multiple_of(t * TILE, TILE), TILE)
            rows_in = source[rows, :].astype(f32)
            tile = (rows_in * row_scale(rows_in) * gain_row).astype(bf16)
            normed[s, rows, :] = tile
            mixed = dot_nn(tile, weight[...])
            for h in range(2):
                place = rel[(s * tiles + t) * 2 + h]
                where = pl.ds(pl.multiple_of(place * blk, blk), blk)
                part = mixed[h * blk : (h + 1) * blk]
                query[where, :] = (part[:, :width].astype(bf16) * 0.125).astype(bf16)
                key[where, :] = part[:, width : 2 * width].astype(bf16)
                value[where, :] = part[:, 2 * width :].astype(bf16)
            return 0

        lax.fori_loop(0, tiles, project, 0)

    masks = head_masks(TILE, width)
    big = heads * TILE

    def query_tile(qb, _):
        rows = pl.ds(pl.multiple_of(qb * TILE, TILE), TILE)
        stacked = stack_heads(query[rows, :], masks)
        top[...] = jnp.full_like(top, MASKED)
        begin = jnp.concatenate([start[rows, :]] * heads, axis=0)

        def score(kb, masked):
            keys = key[pl.ds(pl.multiple_of(kb * TILE, TILE), TILE), :]
            raw = dot_nt(stacked, keys)
            if masked:
                k_pos = kb * TILE + lax.broadcasted_iota(jnp.int32, (big, TILE), 1)
                q_row = lax.broadcasted_iota(jnp.int32, (big, TILE), 0) & (TILE - 1)
                allowed = (k_pos >= begin) & (k_pos <= qb * TILE + q_row)
                raw = jnp.where(allowed, raw, MASKED)
            scores[kb] = raw
            best = raw[:, :128]
            for c in range(1, TILE // 128):
                best = jnp.maximum(best, raw[:, c * 128 : (c + 1) * 128])
            top[...] = jnp.maximum(top[...], best)

        def masked_step(kb, _):
            score(kb, True)
            return 0

        def plain_step(kb, _):
            score(kb, False)
            return 0

        lax.fori_loop(first[qb], full[qb], masked_step, 0)
        lax.fori_loop(full[qb], qb, plain_step, 0)
        score(qb, True)
        peak = jnp.max(top[...], axis=1, keepdims=True)
        top[...] = jnp.broadcast_to(peak, top.shape)
        total[...] = jnp.zeros_like(total)

        def weigh(kb, carry):
            vals = value[pl.ds(pl.multiple_of(kb * TILE, TILE), TILE), :]
            pieces = []
            summed = total[...]
            for c in range(TILE // 128):
                piece = jnp.exp(scores[kb, :, c * 128 : (c + 1) * 128] - top[...])
                summed = summed + piece
                pieces.append(piece.astype(bf16))
            total[...] = summed
            return carry + dot_nn(jnp.concatenate(pieces, axis=1), vals)

        gathered = lax.fori_loop(first[qb], qb + 1, weigh, jnp.zeros((big, width), f32))
        denom = jnp.sum(total[...], axis=1, keepdims=True)
        fine[rows, :] = merge_heads(gathered / denom, masks, TILE)
        logs = jnp.broadcast_to(peak + jnp.log(denom), (big, width))
        logsum[rows, :] = merge_heads(logs, masks, TILE)
        return 0

    lax.fori_loop(0, seq_len // TILE, query_tile, 0)

    def emit(j, _):
        where = pl.ds(pl.multiple_of(send[j] * blk, blk), blk)
        attended[pl.ds(pl.multiple_of(j * blk, blk), blk), :] = fine[where, :].astype(bf16)
        return 0

    lax.fori_loop(0, seq_len // blk, emit, 0)


def backward_kernel(
    rel, send, first, full, query, key, value, fine, logsum, grad_in, weight, start,
    partial, grads,
    grad_at, grad_q, grad_k, grad_v, grad_q2,
):
    seq_len, width = query.shape
    heads = width // HEAD_DIM
    blk = TILE // 2
    big = heads * TILE

    def place(j, _):
        where = pl.ds(pl.multiple_of(send[j] * blk, blk), blk)
        grad_at[where, :] = grad_in[pl.ds(pl.multiple_of(j * blk, blk), blk), :]
        return 0

    lax.fori_loop(0, seq_len // blk, place, 0)
    grad_k[...] = jnp.zeros_like(grad_k)
    grad_v[...] = jnp.zeros_like(grad_v)
    masks = head_masks(TILE, width)

    def flip(values):
        if width < 128:
            values = jnp.concatenate([values, jnp.zeros((TILE, 128 - width), f32)], axis=1)
        return values.T

    def query_tile(qb, _):
        rows = pl.ds(pl.multiple_of(qb * TILE, TILE), TILE)
        stacked = stack_heads(query[rows, :], masks)
        grad_rows = grad_at[rows, :]
        grad_stacked = stack_heads(grad_rows, masks)
        products = flip(grad_rows.astype(f32) * fine[rows, :])
        logs = flip(logsum[rows, :])
        delta = jnp.concatenate(
            [
                jnp.sum(products[h * HEAD_DIM : (h + 1) * HEAD_DIM], axis=0, keepdims=True)
                for h in range(heads)
            ],
            axis=1,
        )
        log_row = jnp.concatenate(
            [logs[h * HEAD_DIM : h * HEAD_DIM + 1] for h in range(heads)], axis=1
        )
        begin = jnp.concatenate([start[qb]] * heads, axis=1)
        grad_q2[...] = jnp.zeros_like(grad_q2)

        def step(kb, masked):
            where = pl.ds(pl.multiple_of(kb * TILE, TILE), TILE)
            keys = key[where, :]
            probs = jnp.exp(dot_nt(keys, stacked) - log_row)
            if masked:
                k_pos = kb * TILE + lax.broadcasted_iota(jnp.int32, (TILE, big), 0)
                q_row = lax.broadcasted_iota(jnp.int32, (TILE, big), 1) & (TILE - 1)
                allowed = (k_pos >= begin) & (k_pos <= qb * TILE + q_row)
                probs = jnp.where(allowed, probs, 0.0)
            slope = (probs * (dot_nt(value[where, :], grad_stacked) - delta)).astype(bf16)
            grad_v[where, :] += dot_nn(probs.astype(bf16), grad_stacked)
            grad_k[where, :] += dot_nn(slope, stacked)
            grad_q2[...] += dot_tn(slope, keys)

        def masked_step(kb, _):
            step(kb, True)
            return 0

        def plain_step(kb, _):
            step(kb, False)
            return 0

        lax.fori_loop(first[qb], full[qb], masked_step, 0)
        lax.fori_loop(full[qb], qb, plain_step, 0)
        step(qb, True)
        grad_q[rows, :] = (merge_heads(grad_q2[...], masks, TILE) * 0.125).astype(bf16)
        return 0

    lax.fori_loop(0, seq_len // TILE, query_tile, 0)

    tiles = seq_len // TILE

    def project(t, _):
        rows = pl.ds(pl.multiple_of(t * TILE, TILE), TILE)
        for h in range(2):
            where = pl.ds(pl.multiple_of(rel[t * 2 + h] * blk, blk), blk)
            here = pl.ds(pl.multiple_of(t * TILE + h * blk, blk), blk)
            grads[here, :width] = grad_q[where, :]
            grads[here, width : 2 * width] = grad_k[where, :].astype(bf16)
            grads[here, 2 * width :] = grad_v[where, :].astype(bf16)
        partial[rows, :] = dot_nt(grads[rows, :], weight[...]).astype(bf16)
        return 0

    lax.fori_loop(0, tiles, project, 0)


def smem():
    return pl.BlockSpec(memory_space=pltpu.SMEM)


def vmem():
    return pl.BlockSpec(memory_space=pltpu.VMEM)


LIMIT = pltpu.CompilerParams(vmem_limit_bytes=56 * 2**20)


def attend_forward(tables, x_near, x_far, weight, gain, start, width):
    half_rows, feats = x_near.shape
    seq_len = 2 * half_rows
    big = (width // HEAD_DIM) * TILE
    shape = jax.ShapeDtypeStruct
    narrow = shape((seq_len, width), bf16)
    wide = shape((seq_len, width), f32)
    pairs = seq_len * seq_len * width // 2
    return pl.pallas_call(
        forward_kernel,
        out_shape=(narrow, narrow, narrow, shape((2, half_rows, feats), bf16), narrow, wide, wide),
        in_specs=[smem()] * 4 + [vmem()] * 5,
        out_specs=[vmem()] * 7,
        scratch_shapes=[
            pltpu.VMEM((seq_len // TILE, big, TILE), f32),
            pltpu.VMEM((big, 128), f32),
            pltpu.VMEM((big, 128), f32),
        ],
        compiler_params=LIMIT,
        cost_estimate=pl.CostEstimate(
            flops=6 * seq_len * feats * width + 16 * pairs,
            bytes_accessed=6 * seq_len * feats,
            transcendentals=pairs // HEAD_DIM,
        ),
        name="attend_forward",
    )(*tables, x_near, x_far, weight, gain, start)


def attend_backward(tables, saved, grad_in, weight, start):
    query = saved[0]
    seq_len, width = query.shape
    feats = weight.shape[0]
    big = (width // HEAD_DIM) * TILE
    shape = jax.ShapeDtypeStruct
    pairs = seq_len * seq_len * width // 2
    return pl.pallas_call(
        backward_kernel,
        out_shape=(shape((seq_len, feats), bf16), shape((seq_len, 3 * width), bf16)),
        in_specs=[smem()] * 4 + [vmem()] * 8,
        out_specs=[vmem()] * 2,
        scratch_shapes=[
            pltpu.VMEM((seq_len, width), bf16),
            pltpu.VMEM((seq_len, width), bf16),
            pltpu.VMEM((seq_len, width), f32),
            pltpu.VMEM((seq_len, width), f32),
            pltpu.VMEM((big, width), f32),
        ],
        compiler_params=LIMIT,
        cost_estimate=pl.CostEstimate(
            flops=6 * seq_len * feats * width + 32 * pairs,
            bytes_accessed=4 * seq_len * feats,
            transcendentals=pairs // HEAD_DIM,
        ),
        name="attend_backward",
    )(*tables, *saved, grad_in, weight, start)


def per_device(
    inputs, w_query, w_key, w_value, w_out, w_gate, w_up, w_down,
    gain_attn, gain_ffn, segments, deal_order, cotangent,
):
    rows, seqs, feats = inputs.shape
    chips = lax.axis_size("chip")
    groups = 2 * chips
    shards = lax.axis_size("fsdp")
    chip = lax.axis_index("chip")
    core = lax.axis_index("core")
    rank = chip * 2 + core
    width = feats // groups
    hidden_width = w_gate.shape[1] // groups
    per_shard = hidden_width // shards
    seq_len = rows * groups
    blocks = deal_order.shape[0]
    blk = rows // 2
    tokens = chips * rows

    near_ids = jnp.arange(chips, dtype=jnp.int32) ^ chip
    pair = jnp.arange(2, dtype=jnp.int32)
    rel_dev = (near_ids[None, :] * 2) + (pair[:, None] ^ core)
    rel_slot = (rel_dev[:, :, None] * 2 + pair[None, None, :]).reshape(-1)
    send_dev = jnp.arange(chips, dtype=jnp.int32)[:, None] * 2 + (pair[None, :] ^ core)
    send_slot = (send_dev[:, :, None] * 2 + pair[None, None, :]).reshape(-1)
    ids = jnp.arange(blocks, dtype=jnp.int32)

    def look_up(slots):
        return jnp.sum(
            jnp.where(slots[:, None] == ids[None, :], deal_order[None, :], 0), axis=1
        ).astype(jnp.int32)

    rel_table = look_up(rel_slot)
    send_table = look_up(send_slot)
    earlier = (segments[None, :, :] < segments[:, None, :]).astype(jnp.int32)
    slot_start = jnp.sum(earlier, axis=1).astype(jnp.int32).reshape(blocks, blk, seqs)
    start = jnp.sum(
        jnp.where((deal_order[None, :] == ids[:, None])[:, :, None, None], slot_start[None], 0),
        axis=1,
    ).astype(jnp.int32)
    start = start.transpose(2, 0, 1).reshape(seqs, seq_len)
    tiles = seq_len // TILE
    tiled = start.reshape(seqs, tiles, TILE)
    first = tiled[:, :, 0] // TILE
    full = jnp.minimum(
        jnp.arange(tiles, dtype=jnp.int32)[None, :], (tiled[:, :, -1] + TILE - 1) // TILE
    )

    def take(weight, axis, index, size):
        return lax.dynamic_slice_in_dim(weight, index * size, size, axis)

    own_qkv = jnp.concatenate([take(w, 1, rank, width) for w in (w_query, w_key, w_value)], axis=1)

    def hidden_columns(weight):
        grid = weight.reshape(weight.shape[0], shards, groups, per_shard)
        return take(grid, 2, rank, 1).reshape(weight.shape[0], hidden_width)

    own_gate_up = jnp.concatenate([hidden_columns(w_gate), hidden_columns(w_up)], axis=1)
    own_down = take(w_down, 0, rank, per_shard)
    out_grid = w_out.reshape(-1, 2, width, feats)
    own_out = take(out_grid, 1, core, 1).reshape(-1, feats)

    def gather_rows(value):
        return lax.all_gather(value, "fsdp", axis=0, tiled=True)

    gains = gather_rows(jnp.stack([gain_attn, gain_ffn], axis=1))
    gain_one, gain_two = gains[:, 0][None, :], gains[:, 1][None, :]
    qkv = gather_rows(own_qkv)
    out_half = gather_rows(own_out)
    gate_up = gather_rows(own_gate_up)
    down = gather_rows(own_down)

    outputs, grad_inputs = [], []
    grad_qkv = grad_gate_up = grad_down = grad_out = 0.0
    gain_sums_one = gain_sums_two = 0.0
    kept = []
    for b in range(seqs):
        x_own = inputs[:, b]
        x_near, x_far = gather_all(x_own)
        tables = (rel_table, send_table, first[b], full[b])
        query, key, value, normed, sent, fine, logsum = attend_forward(
            tables,
            x_near.reshape(tokens, feats),
            x_far.reshape(tokens, feats),
            qkv,
            gain_one,
            start[b][:, None],
            width,
        )
        got = lax.all_to_all(sent.reshape(chips, 2 * rows, width), "chip", 0, 0)
        attended = got.transpose(1, 0, 2).reshape(2 * rows, chips * width)
        mixed = dot_nn(attended, out_half)
        middle = x_own.astype(f32) + mixed[:rows] + swap_core(mixed[rows:])
        scale_two = row_scale(middle)
        unit_two = middle * scale_two
        normed_mid = (unit_two * gain_two.astype(f32)).astype(bf16)
        kept.append((x_own, query, key, value, normed, fine, logsum, attended, middle,
                     scale_two, unit_two, normed_mid, tables))

    for b in range(seqs):
        (x_own, query, key, value, normed, fine, logsum, attended, middle,
         scale_two, unit_two, normed_mid, tables) = kept[b]
        cot_own = cotangent[:, b]
        cots = gather_all(cot_own)
        mids = gather_all(normed_mid)
        out_parts, mid_parts = [], []
        for cot, mid in zip(cots, mids):
            cot = cot.reshape(tokens, feats)
            mid = mid.reshape(tokens, feats)
            pre = dot_nn(mid, gate_up)
            gate_pre, up_pre = pre[:, :hidden_width], pre[:, hidden_width:]
            sigma = jax.nn.sigmoid(gate_pre)
            active = gate_pre * sigma
            hidden = (active * up_pre).astype(bf16)
            out_parts.append(dot_nn(hidden, down).astype(bf16).reshape(chips, rows, feats))
            grad_hidden = dot_nt(cot, down)
            grad_gate = grad_hidden * up_pre * sigma * (1.0 + gate_pre * (1.0 - sigma))
            grad_up = grad_hidden * active
            grad_pre = jnp.concatenate([grad_gate, grad_up], axis=1).astype(bf16)
            mid_parts.append(dot_nt(grad_pre, gate_up).astype(bf16).reshape(chips, rows, feats))
            grad_gate_up = grad_gate_up + dot_tn(mid, grad_pre)
            grad_down = grad_down + dot_tn(hidden, cot)
        grad_normed_mid = plane_reduce(*mid_parts)
        outputs.append((middle + plane_reduce(*out_parts)).astype(bf16))
        gain_sums_two = gain_sums_two + jnp.sum(grad_normed_mid * unit_two, axis=0)
        scaled_two = grad_normed_mid * gain_two.astype(f32)
        grad_middle = cot_own.astype(f32) + scale_two * (
            scaled_two - unit_two * jnp.mean(scaled_two * unit_two, axis=-1, keepdims=True)
        )
        branch_own = grad_middle.astype(bf16)
        branch = jnp.concatenate([branch_own, swap_core(branch_own)])
        grad_att = dot_nt(branch, out_half).astype(bf16)
        grad_out = grad_out + dot_tn(attended.astype(bf16), branch)
        grad_sent = lax.all_to_all(
            grad_att.reshape(2 * rows, chips, width).transpose(1, 0, 2), "chip", 0, 0
        )
        partial, grads = attend_backward(
            tables,
            (query, key, value, fine, logsum),
            grad_sent.reshape(seq_len, width),
            qkv,
            tiled[b][:, None, :],
        )
        grad_qkv = grad_qkv + dot_tn(normed.reshape(seq_len, feats), grads)
        parts = partial.reshape(2, chips, rows, feats)
        grad_normed_in = plane_reduce(parts[0], parts[1])
        flat_in = x_own.astype(f32)
        scale_one = row_scale(flat_in)
        unit_one = flat_in * scale_one
        gain_sums_one = gain_sums_one + jnp.sum(grad_normed_in * unit_one, axis=0)
        scaled_one = grad_normed_in * gain_one.astype(f32)
        grad_inputs.append(
            (
                grad_middle
                + scale_one
                * (scaled_one - unit_one * jnp.mean(scaled_one * unit_one, axis=-1, keepdims=True))
            ).astype(bf16)
        )

    def to_shard(value):
        return lax.psum_scatter(value.astype(bf16), "fsdp", scatter_dimension=0, tiled=True)

    def collect(value):
        return lax.all_gather(value, PLANE, axis=0)

    own_rows = feats // shards
    s_gate_up = collect(to_shard(grad_gate_up))
    s_gate_up = s_gate_up.reshape(groups, own_rows, 2, shards, per_shard)
    g_gate_up = s_gate_up.transpose(2, 1, 3, 0, 4).reshape(2, own_rows, -1).astype(f32)
    g_down = collect(to_shard(grad_down)).reshape(-1, feats).astype(f32)
    s_qkv = collect(to_shard(grad_qkv)).reshape(groups, own_rows, 3, width)
    g_qkv = s_qkv.transpose(2, 1, 0, 3).reshape(3, own_rows, feats).astype(f32)
    part_out = lax.psum(to_shard(grad_out), "chip")
    s_out = lax.all_gather(part_out.reshape(-1, width, feats), "core", axis=1)
    g_out = s_out.reshape(own_rows, feats).astype(f32)
    gain_sums = lax.psum(jnp.stack([gain_sums_one, gain_sums_two]), PLANE + ("fsdp",))
    g_gains = lax.dynamic_slice_in_dim(gain_sums, lax.axis_index("fsdp") * own_rows, own_rows, 1)

    return (
        jnp.stack(outputs, axis=1),
        jnp.stack(grad_inputs, axis=1),
        g_qkv[0],
        g_qkv[1],
        g_qkv[2],
        g_out,
        g_gate_up[0],
        g_gate_up[1],
        g_down,
        g_gains[0],
        g_gains[1],
    )


def solution(mesh):
    names = mesh.axis_names
    ctx, shards = mesh.shape[names[0]], mesh.shape[names[1]]
    fine_mesh = Mesh(mesh.devices.reshape(ctx // 2, 2, shards), ("chip", "core", "fsdp"))
    by_row = P("fsdp", None)
    by_token = P(PLANE, "fsdp", None)
    return jax.shard_map(
        per_device,
        mesh=fine_mesh,
        in_specs=(by_token,) + (by_row,) * 7 + (P("fsdp"), P("fsdp"), P(None, "fsdp"), P(), by_token),
        out_specs=(by_token, by_token) + (by_row,) * 7 + (P("fsdp"), P("fsdp")),
        check_vma=False,
    )
```

```python
import functools

import jax
import jax.numpy as jnp
from jax import lax
from jax.experimental import pallas as pl
from jax.experimental.pallas import tpu as pltpu
from jax.sharding import Mesh, PartitionSpec as P

HEAD_DIM = 64
EPSILON = 1e-05
MASKED = -1e30
TILE = 256
PLANE = ("chip", "core")

bf16 = jnp.bfloat16
f32 = jnp.float32


def dot_nn(left_op, right_op):
    return lax.dot_general(left_op, right_op, (((1,), (0,)), ((), ())), preferred_element_type=f32)


def dot_nt(left_op, right_op):
    return lax.dot_general(left_op, right_op, (((1,), (1,)), ((), ())), preferred_element_type=f32)


def dot_tn(left_op, right_op):
    return lax.dot_general(left_op, right_op, (((0,), (0,)), ((), ())), preferred_element_type=f32)


def row_scale(values):
    return lax.rsqrt(jnp.mean(values * values, axis=-1, keepdims=True) + EPSILON)


def swap_core(value):
    return lax.ppermute(value, "core", [(0, 1), (1, 0)])


def swap_chip(value, mask):
    count = lax.axis_size("chip")
    return lax.ppermute(value, "chip", [(i, i ^ mask) for i in range(count)])


def swap_shard(value, mask):
    count = lax.axis_size("fsdp")
    return lax.ppermute(value, "fsdp", [(i, i ^ mask) for i in range(count)])


def hold(value, *deps):
    return lax.optimization_barrier((value, deps))[0]


def spread(value):
    count = lax.axis_size("chip")
    return exchange(jnp.broadcast_to(value, (count,) + value.shape))


def exchange(value):
    return lax.all_to_all(value, "chip", 0, 0)


def core_sum(own, swapped):
    return (own.astype(f32) + swapped.astype(f32)).astype(bf16)


def last_sum(value):
    return jnp.sum(value.astype(f32), axis=0)


def shard_pieces(value):
    return [value] + [swap_shard(value, r) for r in range(1, lax.axis_size("fsdp"))]


def shard_sum(pieces):
    return add_pieces(pieces[0], send_pieces(pieces))


def send_pieces(pieces):
    return [swap_shard(pieces[r], r) for r in range(1, len(pieces))]


def add_pieces(own, received):
    total = own.astype(f32)
    for piece in received:
        total = total + piece.astype(f32)
    return total.astype(bf16)


def head_masks(rows, width):
    lanes = lax.broadcasted_iota(jnp.int32, (rows, width), 1) // HEAD_DIM
    return [lanes == h for h in range(width // HEAD_DIM)]


def stack_heads(values, masks):
    zero = jnp.zeros_like(values)
    return jnp.concatenate([jnp.where(mask, values, zero) for mask in masks], axis=0)


def merge_heads(stacked, masks, rows):
    merged = stacked[:rows]
    for h in range(1, len(masks)):
        merged = jnp.where(masks[h], stacked[h * rows : (h + 1) * rows], merged)
    return merged


def forward_kernel(
    rel, send, first, full, x_near, x_far, weight, gain, start,
    query, key, value, normed, attended, fine, logsum,
    scores, top, total,
):
    width = query.shape[1]
    seq_len = query.shape[0]
    heads = width // HEAD_DIM
    blk = TILE // 2
    tiles = x_near.shape[0] // TILE
    gain_row = gain[...].astype(f32)
    for s, source in ((0, x_near), (1, x_far)):

        def project(t, _, s=s, source=source):
            rows = pl.ds(pl.multiple_of(t * TILE, TILE), TILE)
            rows_in = source[rows, :].astype(f32)
            tile = (rows_in * row_scale(rows_in) * gain_row).astype(bf16)
            normed[s, rows, :] = tile
            mixed = dot_nn(tile, weight[:, : 3 * width])
            for h in range(2):
                place = rel[(s * tiles + t) * 2 + h]
                where = pl.ds(pl.multiple_of(place * blk, blk), blk)
                part = mixed[h * blk : (h + 1) * blk]
                query[where, :] = (part[:, :width].astype(bf16) * 0.125).astype(bf16)
                key[where, :] = part[:, width : 2 * width].astype(bf16)
                value[where, :] = part[:, 2 * width :].astype(bf16)
            return 0

        lax.fori_loop(0, tiles, project, 0)

    masks = head_masks(TILE, width)
    big = heads * TILE

    def query_tile(qb, _):
        rows = pl.ds(pl.multiple_of(qb * TILE, TILE), TILE)
        stacked = stack_heads(query[rows, :], masks)
        top[...] = jnp.full_like(top, MASKED)
        begin = jnp.concatenate([start[rows, :]] * heads, axis=0)

        def score(kb, masked):
            keys = key[pl.ds(pl.multiple_of(kb * TILE, TILE), TILE), :]
            raw = dot_nt(stacked, keys)
            if masked:
                k_pos = kb * TILE + lax.broadcasted_iota(jnp.int32, (big, TILE), 1)
                q_row = lax.broadcasted_iota(jnp.int32, (big, TILE), 0) & (TILE - 1)
                allowed = (k_pos >= begin) & (k_pos <= qb * TILE + q_row)
                raw = jnp.where(allowed, raw, MASKED)
            scores[kb] = raw
            best = raw[:, :128]
            for c in range(1, TILE // 128):
                best = jnp.maximum(best, raw[:, c * 128 : (c + 1) * 128])
            top[...] = jnp.maximum(top[...], best)

        def masked_step(kb, _):
            score(kb, True)
            return 0

        def plain_step(kb, _):
            score(kb, False)
            return 0

        lax.fori_loop(first[qb], full[qb], masked_step, 0)
        lax.fori_loop(full[qb], qb, plain_step, 0)
        score(qb, True)
        peak = jnp.max(top[...], axis=1, keepdims=True)
        top[...] = jnp.broadcast_to(peak, top.shape)
        total[...] = jnp.zeros_like(total)

        def weigh(kb, carry):
            vals = value[pl.ds(pl.multiple_of(kb * TILE, TILE), TILE), :]
            pieces = []
            summed = total[...]
            for c in range(TILE // 128):
                piece = jnp.exp(scores[kb, :, c * 128 : (c + 1) * 128] - top[...])
                summed = summed + piece
                pieces.append(piece.astype(bf16))
            total[...] = summed
            return carry + dot_nn(jnp.concatenate(pieces, axis=1), vals)

        gathered = lax.fori_loop(first[qb], qb + 1, weigh, jnp.zeros((big, width), f32))
        denom = jnp.sum(total[...], axis=1, keepdims=True)
        fine[rows, :] = merge_heads(gathered / denom, masks, TILE)
        logs = jnp.broadcast_to(peak + jnp.log(denom), (big, width))
        logsum[rows, :] = merge_heads(logs, masks, TILE)
        return 0

    lax.fori_loop(0, seq_len // TILE, query_tile, 0)

    def emit(j, _):
        where = pl.ds(pl.multiple_of(send[j] * blk, blk), blk)
        attended[pl.ds(pl.multiple_of(j * blk, blk), blk), :] = fine[where, :].astype(bf16)
        return 0

    lax.fori_loop(0, seq_len // blk, emit, 0)


def backward_kernel(
    rel, send, first, full, query, key, value, fine, logsum, grad_in, weight, start,
    part_near, part_far, grads,
    grad_at, grad_q, grad_k, grad_v, grad_q2,
):
    seq_len, width = query.shape
    heads = width // HEAD_DIM
    blk = TILE // 2
    big = heads * TILE

    def place(j, _):
        where = pl.ds(pl.multiple_of(send[j] * blk, blk), blk)
        grad_at[where, :] = grad_in[pl.ds(pl.multiple_of(j * blk, blk), blk), :]
        return 0

    lax.fori_loop(0, seq_len // blk, place, 0)
    grad_k[...] = jnp.zeros_like(grad_k)
    grad_v[...] = jnp.zeros_like(grad_v)
    masks = head_masks(TILE, width)

    def flip(values):
        if width < 128:
            values = jnp.concatenate([values, jnp.zeros((TILE, 128 - width), f32)], axis=1)
        return values.T

    def query_tile(qb, _):
        rows = pl.ds(pl.multiple_of(qb * TILE, TILE), TILE)
        stacked = stack_heads(query[rows, :], masks)
        grad_rows = grad_at[rows, :]
        grad_stacked = stack_heads(grad_rows, masks)
        products = flip(grad_rows.astype(f32) * fine[rows, :])
        logs = flip(logsum[rows, :])
        delta = jnp.concatenate(
            [
                jnp.sum(products[h * HEAD_DIM : (h + 1) * HEAD_DIM], axis=0, keepdims=True)
                for h in range(heads)
            ],
            axis=1,
        )
        log_row = jnp.concatenate(
            [logs[h * HEAD_DIM : h * HEAD_DIM + 1] for h in range(heads)], axis=1
        )
        begin = jnp.concatenate([start[qb]] * heads, axis=1)
        grad_q2[...] = jnp.zeros_like(grad_q2)

        def step(kb, masked):
            where = pl.ds(pl.multiple_of(kb * TILE, TILE), TILE)
            keys = key[where, :]
            probs = jnp.exp(dot_nt(keys, stacked) - log_row)
            if masked:
                k_pos = kb * TILE + lax.broadcasted_iota(jnp.int32, (TILE, big), 0)
                q_row = lax.broadcasted_iota(jnp.int32, (TILE, big), 1) & (TILE - 1)
                allowed = (k_pos >= begin) & (k_pos <= qb * TILE + q_row)
                probs = jnp.where(allowed, probs, 0.0)
            slope = (probs * (dot_nt(value[where, :], grad_stacked) - delta)).astype(bf16)
            grad_v[where, :] += dot_nn(probs.astype(bf16), grad_stacked)
            grad_k[where, :] += dot_nn(slope, stacked)
            grad_q2[...] += dot_tn(slope, keys)

        def masked_step(kb, _):
            step(kb, True)
            return 0

        def plain_step(kb, _):
            step(kb, False)
            return 0

        lax.fori_loop(first[qb], full[qb], masked_step, 0)
        lax.fori_loop(full[qb], qb, plain_step, 0)
        step(qb, True)
        grad_q[rows, :] = (merge_heads(grad_q2[...], masks, TILE) * 0.125).astype(bf16)
        return 0

    lax.fori_loop(0, seq_len // TILE, query_tile, 0)

    tiles = seq_len // TILE // 2

    def project(t, side, part):
        rows = pl.ds(pl.multiple_of(t * TILE, TILE), TILE)
        base = side * tiles + t
        for h in range(2):
            where = pl.ds(pl.multiple_of(rel[base * 2 + h] * blk, blk), blk)
            here = pl.ds(pl.multiple_of(t * TILE + h * blk, blk), blk)
            grads[side, here, :width] = grad_q[where, :]
            grads[side, here, width : 2 * width] = grad_k[where, :].astype(bf16)
            grads[side, here, 2 * width :] = grad_v[where, :].astype(bf16)
        part[rows, :] = dot_nt(grads[side, rows, :], weight[:, : 3 * width]).astype(bf16)
        return 0

    for side, part in ((0, part_near), (1, part_far)):
        lax.fori_loop(0, tiles, lambda t, _, s=side, p=part: project(t, s, p), 0)


def place_pieces(target, pieces, shard, begin, count):
    for r, piece in enumerate(pieces):
        at = pl.multiple_of((shard ^ r) * count, count)
        target[pl.ds(at, count), :] = piece[begin : begin + count, :]


def mix_kernel(ids, got, *refs):
    pieces, (attended, own, other, weight) = refs[:-4], refs[-4:]
    rows = own.shape[0]
    place_pieces(weight, pieces, ids[1], 0, pieces[0].shape[0])
    joined = jnp.concatenate([got[p] for p in range(got.shape[0])], axis=1)
    attended[...] = joined
    own[...] = dot_nn(joined[:rows], weight[...])
    other[...] = dot_nn(joined[rows:], weight[...])


def unmix_kernel(ids, own, other, attended, *refs):
    pieces, (grad_sent, grad_weight, weight) = refs[:-3], refs[-3:]
    place_pieces(weight, pieces, ids[1], 0, pieces[0].shape[0])
    branch = jnp.concatenate([own[...], other[...]], axis=0)
    spread = dot_nt(branch, weight[...]).astype(bf16)
    width = grad_sent.shape[2]
    for p in range(grad_sent.shape[0]):
        grad_sent[p] = spread[:, p * width : (p + 1) * width]
    grad_weight[...] = dot_tn(attended[...], branch)


def ffn_kernel(ids, x_near, x_far, cot_ref, *refs, split):
    outs = 7 + split
    pieces, out_parts = refs[:-outs], refs[-outs : 1 + split - outs]
    mid_near, mid_far, hidden, grad_pre, gate_up, down = refs[-6:]
    t = pl.program_id(0)
    half = pl.num_programs(0) // 2
    feats, size = gate_up.shape[0], gate_up.shape[1] // 2
    shards = pieces[0].shape[0]
    rows, more = feats // shards, size // shards
    begin = rows if len(pieces) == 1 else 0

    @pl.when(t == 0)
    def _():
        for z in range(shards):
            gate_up[z * rows : (z + 1) * rows, :] = pieces[0][z, :rows, :]
            down[z * more : (z + 1) * more, :] = pieces[-1][z, begin : begin + more, :]

    tile = jnp.where(t < half, x_near[...], x_far[...])
    cot = cot_ref[...].reshape(tile.shape)
    pre = dot_nn(tile, gate_up[...])
    gate_pre, up_pre = pre[:, :size], pre[:, size:]
    sigma = jax.nn.sigmoid(gate_pre)
    active = gate_pre * sigma
    low = (active * up_pre).astype(bf16)
    grad_hidden = dot_nt(cot, down[...])
    hidden[...] = low
    out_part = dot_nn(low, down[...]).astype(bf16)
    grad_gate = grad_hidden * up_pre * sigma * (1.0 + gate_pre * (1.0 - sigma))
    grad_up = grad_hidden * active
    grads = jnp.concatenate([grad_gate.astype(bf16), grad_up.astype(bf16)], axis=1)
    grad_pre[...] = grads
    mid_part = dot_nt(grads, gate_up[...]).astype(bf16)

    if not split:
        out_parts[0][...] = out_part.reshape(out_parts[0].shape)

    @pl.when(t < half)
    def _():
        mid_near[...] = mid_part
        if split:
            out_parts[0][...] = out_part

    @pl.when(t >= half)
    def _():
        mid_far[...] = mid_part
        if split:
            out_parts[1][...] = out_part


def weight_kernel(ids, *refs, streams, shards):
    ins, outs, (wide, down) = refs[: 5 * streams], refs[5 * streams : -2], refs[-2:]
    t = pl.program_id(0)
    per = pl.num_programs(0) // streams

    @pl.when(t == 0)
    def _():
        wide[...] = jnp.zeros_like(wide)
        down[...] = jnp.zeros_like(down)

    for b in range(streams):
        x_near, x_far, cot, hidden, grad_pre = ins[5 * b : 5 * b + 5]

        @pl.when((t >= b * per) & (t < (b + 1) * per))
        def _(b=b, x_near=x_near, x_far=x_far, cot=cot, hidden=hidden, grad_pre=grad_pre):
            tile = jnp.where(t < b * per + per // 2, x_near[...], x_far[...])
            wide[...] += dot_tn(tile, grad_pre[...])
            down[...] += dot_tn(hidden[...], cot[...].reshape(tile.shape))

    @pl.when(t == pl.num_programs(0) - 1)
    def _():
        rows, more = wide.shape[0] // shards, down.shape[0] // shards
        begin = rows if len(outs) == 1 else 0
        for z in range(shards):
            outs[0][z, :rows, :] = wide[z * rows : (z + 1) * rows, :].astype(bf16)
            piece = down[z * more : (z + 1) * more, :]
            outs[-1][z, begin : begin + more, :] = piece.astype(bf16)


def assemble_kernel(*refs, kinds, shards, with_down):
    parts, gain = refs[:2]
    weights = refs[2 : 2 + kinds]
    rest = refs[2 + kinds :]
    if with_down:
        down_part, rest = rest[0], rest[1:]
    outs, gain_out = rest[:kinds], rest[kinds]
    groups, _, size = parts.shape
    pieces = size // kinds
    lanes = pieces // shards
    sums = 0.0
    for k in range(kinds):
        columns = []
        for z in range(shards):
            for i in range(groups):
                at = k * pieces + z * lanes
                columns.append(parts[i, :, at : at + lanes].astype(f32))
        full = jnp.concatenate(columns, axis=1)
        outs[k][...] = full
        sums = sums + jnp.sum(full * weights[k][...].astype(f32), axis=1, keepdims=True)
    gain_out[...] = sums / gain[...].astype(f32)
    if with_down:
        rest[kinds + 1][...] = down_part[...].astype(f32)


def smem():
    return pl.BlockSpec(memory_space=pltpu.SMEM)


def vmem():
    return pl.BlockSpec(memory_space=pltpu.VMEM)


def cost(micros):
    return pl.CostEstimate(flops=micros * 10**9, bytes_accessed=2**20, transcendentals=0)


LIMIT = pltpu.CompilerParams(vmem_limit_bytes=56 * 2**20)


def attend_forward(tables, x_near, x_far, weight, gain, start, width):
    half_rows, feats = x_near.shape
    seq_len = 2 * half_rows
    big = (width // HEAD_DIM) * TILE
    shape = jax.ShapeDtypeStruct
    narrow = shape((seq_len, width), bf16)
    wide = shape((seq_len, width), f32)
    pairs = seq_len * seq_len * width // 2
    return pl.pallas_call(
        forward_kernel,
        out_shape=(narrow, narrow, narrow, shape((2, half_rows, feats), bf16), narrow, wide, wide),
        in_specs=[smem()] * 4 + [vmem()] * 5,
        out_specs=[vmem()] * 7,
        scratch_shapes=[
            pltpu.VMEM((seq_len // TILE, big, TILE), f32),
            pltpu.VMEM((big, 128), f32),
            pltpu.VMEM((big, 128), f32),
        ],
        compiler_params=LIMIT,
        cost_estimate=cost(31),
        name="attend_forward",
    )(*tables, x_near, x_far, weight, gain, start)


def attend_backward(tables, saved, grad_in, weight, start):
    query = saved[0]
    seq_len, width = query.shape
    feats = weight.shape[0]
    big = (width // HEAD_DIM) * TILE
    shape = jax.ShapeDtypeStruct
    pairs = seq_len * seq_len * width // 2
    return pl.pallas_call(
        backward_kernel,
        out_shape=(
            shape((seq_len // 2, feats), bf16),
            shape((seq_len // 2, feats), bf16),
            shape((2, seq_len // 2, 3 * width), bf16),
        ),
        in_specs=[smem()] * 4 + [vmem()] * 8,
        out_specs=[vmem()] * 3,
        scratch_shapes=[
            pltpu.VMEM((seq_len, width), bf16),
            pltpu.VMEM((seq_len, width), bf16),
            pltpu.VMEM((seq_len, width), f32),
            pltpu.VMEM((seq_len, width), f32),
            pltpu.VMEM((big, width), f32),
        ],
        compiler_params=LIMIT,
        cost_estimate=cost(31),
        name="attend_backward",
    )(*tables, *saved, grad_in, weight, start)


def mix(ids, got, pieces):
    chips, doubled, width = got.shape
    feats = pieces[0].shape[1]
    size = chips * width
    shape = jax.ShapeDtypeStruct
    return pl.pallas_call(
        mix_kernel,
        out_shape=(
            shape((doubled, size), bf16),
            shape((doubled // 2, feats), f32),
            shape((doubled // 2, feats), f32),
        ),
        in_specs=[smem()] + [vmem()] * (1 + len(pieces)),
        out_specs=[vmem()] * 3,
        scratch_shapes=[pltpu.VMEM((size, feats), bf16)],
        compiler_params=LIMIT,
        cost_estimate=cost(3),
        name="mix",
    )(ids, got, *pieces)


def unmix(ids, own, other, attended, pieces, chips):
    rows, feats = own.shape
    size = attended.shape[1]
    shape = jax.ShapeDtypeStruct
    return pl.pallas_call(
        unmix_kernel,
        out_shape=(shape((chips, 2 * rows, size // chips), bf16), shape((size, feats), f32)),
        in_specs=[smem()] + [vmem()] * (3 + len(pieces)),
        out_specs=[vmem()] * 2,
        scratch_shapes=[pltpu.VMEM((size, feats), bf16)],
        compiler_params=LIMIT,
        cost_estimate=cost(4),
        name="unmix",
    )(ids, own, other, attended, *pieces)


ROWS = 512


def feed_forward(ids, mids, cot, pieces, size, split):
    tokens, feats = mids[0].shape
    chips, _, rows, _ = cot.shape
    half = tokens // ROWS
    shape = jax.ShapeDtypeStruct
    near = pl.BlockSpec((ROWS, feats), lambda t, ids: (jnp.minimum(t, half - 1), 0))
    far = pl.BlockSpec((ROWS, feats), lambda t, ids: (jnp.maximum(t - half, 0), 0))
    by_device = pl.BlockSpec(
        (ROWS // rows, None, rows, feats),
        lambda t, ids: (lax.rem(t, half), ids[0] ^ lax.div(t, half), 0, 0),
    )

    def tiles(width):
        return pl.BlockSpec((ROWS, width), lambda t, ids: (t, 0))

    side = shape((tokens, feats), bf16)
    return pl.pallas_call(
        functools.partial(ffn_kernel, split=split),
        grid_spec=pltpu.PrefetchScalarGridSpec(
            num_scalar_prefetch=1,
            grid=(2 * half,),
            in_specs=[near, far, by_device]
            + [pl.BlockSpec(piece.shape, lambda t, ids: (0, 0, 0)) for piece in pieces],
            out_specs=([near, far] if split else [by_device])
            + [near, far, tiles(size), tiles(2 * size)],
            scratch_shapes=[
                pltpu.VMEM((feats, 2 * size), bf16),
                pltpu.VMEM((size, feats), bf16),
            ],
        ),
        out_shape=([side, side] if split else [shape(cot.shape, bf16)])
        + [
            side,
            side,
            shape((2 * tokens, size), bf16),
            shape((2 * tokens, 2 * size), bf16),
        ],
        compiler_params=LIMIT,
        cost_estimate=cost(20),
        name="feed_forward",
    )(ids, *mids, cot, *pieces)


def weight_sums(ids, streams, shards):
    tokens, feats = streams[0][0].shape
    size = streams[0][3].shape[1]
    rows = streams[0][2].shape[2]
    half = tokens // ROWS
    per = 2 * half
    shape = jax.ShapeDtypeStruct
    specs = []
    for b in range(len(streams)):

        def local(t, b=b):
            return jnp.clip(t - b * per, 0, per - 1)

        specs += [
            pl.BlockSpec((ROWS, feats), lambda t, ids, f=local: (jnp.minimum(f(t), half - 1), 0)),
            pl.BlockSpec((ROWS, feats), lambda t, ids, f=local: (jnp.maximum(f(t) - half, 0), 0)),
            pl.BlockSpec(
                (ROWS // rows, None, rows, feats),
                lambda t, ids, f=local: (
                    lax.rem(f(t), half),
                    ids[0] ^ lax.div(f(t), half),
                    0,
                    0,
                ),
            ),
            pl.BlockSpec((ROWS, size), lambda t, ids, f=local: (f(t), 0)),
            pl.BlockSpec((ROWS, 2 * size), lambda t, ids, f=local: (f(t), 0)),
        ]
    if 2 * size == feats:
        outs = [(shards, (feats + size) // shards, feats)]
    else:
        outs = [(shards, feats // shards, 2 * size), (shards, size // shards, feats)]
    return pl.pallas_call(
        functools.partial(weight_kernel, streams=len(streams), shards=shards),
        grid_spec=pltpu.PrefetchScalarGridSpec(
            num_scalar_prefetch=1,
            grid=(per * len(streams),),
            in_specs=specs,
            out_specs=[pl.BlockSpec(out, lambda t, ids: (0, 0, 0)) for out in outs],
            scratch_shapes=[pltpu.VMEM((feats, 2 * size), f32), pltpu.VMEM((size, feats), f32)],
        ),
        out_shape=[shape(out, bf16) for out in outs],
        compiler_params=LIMIT,
        cost_estimate=cost(23),
        name="weight_sums",
    )(ids, *[value for stream in streams for value in stream])


STEPS = 4


def assemble(parts, gain, weights, shards, downs=None, begin=0, down_rows=0):
    rows, columns = weights[0].shape
    step = rows // STEPS
    shape = jax.ShapeDtypeStruct
    groups, _, size = parts.shape
    row_block = pl.BlockSpec((step, columns), lambda t: (t, 0))
    thin = pl.BlockSpec((step, 1), lambda t: (t, 0))
    count = len(weights)
    args = [parts, gain[:, None], *weights]
    in_specs = [pl.BlockSpec((groups, step, size), lambda t: (0, t, 0)), thin] + [row_block] * count
    out_shape = [shape((rows, columns), f32)] * count + [shape((rows, 1), f32)]
    out_specs = [row_block] * count + [thin]
    if down_rows:
        share, feats = groups // STEPS, downs.shape[2]
        args.append(downs)
        in_specs.append(
            pl.BlockSpec((share, down_rows, feats), lambda t: (t, begin // down_rows, 0))
        )
        out_shape.append(shape((groups, down_rows, feats), f32))
        out_specs.append(pl.BlockSpec((share, down_rows, feats), lambda t: (t, 0, 0)))
    outs = pl.pallas_call(
        functools.partial(
            assemble_kernel, kinds=count, shards=shards, with_down=bool(down_rows)
        ),
        grid=(STEPS,),
        out_shape=out_shape,
        in_specs=in_specs,
        out_specs=out_specs,
        compiler_params=LIMIT,
        name="assemble",
    )(*args)
    return outs[:count], outs[count][:, 0], outs[count + 1 :]


def per_device(
    inputs, w_query, w_key, w_value, w_out, w_gate, w_up, w_down,
    gain_attn, gain_ffn, segments, deal_order, cotangent,
):
    rows, seqs, feats = inputs.shape
    chips = lax.axis_size("chip")
    groups = 2 * chips
    shards = lax.axis_size("fsdp")
    chip = lax.axis_index("chip")
    core = lax.axis_index("core")
    rank = chip * 2 + core
    width = feats // groups
    hidden_width = w_gate.shape[1] // groups
    per_shard = hidden_width // shards
    seq_len = rows * groups
    blocks = deal_order.shape[0]
    blk = rows // 2
    tokens = chips * rows

    ids = jnp.stack([core, lax.axis_index("fsdp")]).astype(jnp.int32)
    pair = jnp.arange(2, dtype=jnp.int32)
    rel_dev = (jnp.arange(chips, dtype=jnp.int32)[None, :] * 2) + (pair[:, None] ^ core)
    rel_slot = (rel_dev[:, :, None] * 2 + pair[None, None, :]).reshape(-1)
    send_dev = jnp.arange(chips, dtype=jnp.int32)[:, None] * 2 + (pair[None, :] ^ core)
    send_slot = (send_dev[:, :, None] * 2 + pair[None, None, :]).reshape(-1)
    spots = jnp.arange(blocks, dtype=jnp.int32)

    def look_up(slots):
        return jnp.sum(
            jnp.where(slots[:, None] == spots[None, :], deal_order[None, :], 0), axis=1
        ).astype(jnp.int32)

    rel_table = look_up(rel_slot)
    send_table = look_up(send_slot)
    earlier = (segments[None, :, :] < segments[:, None, :]).astype(jnp.int32)
    slot_start = jnp.sum(earlier, axis=1).astype(jnp.int32).reshape(blocks, blk, seqs)
    start = jnp.sum(
        jnp.where((deal_order[None, :] == spots[:, None])[:, :, None, None], slot_start[None], 0),
        axis=1,
    ).astype(jnp.int32)
    start = start.transpose(2, 0, 1).reshape(seqs, seq_len)
    tiles = seq_len // TILE
    tiled = start.reshape(seqs, tiles, TILE)
    first = tiled[:, :, 0] // TILE
    full = jnp.minimum(
        jnp.arange(tiles, dtype=jnp.int32)[None, :], (tiled[:, :, -1] + TILE - 1) // TILE
    )

    def take(weight, axis, index, size):
        return lax.dynamic_slice_in_dim(weight, index * size, size, axis)

    both = jnp.stack([gain_attn, gain_ffn], axis=1)
    spare = jnp.zeros((both.shape[0], -(3 * width + 2) % 128), bf16)
    own_qkv = jnp.concatenate(
        [take(w, 1, rank, width) for w in (w_query, w_key, w_value)] + [both, spare], axis=1
    )

    def hidden_columns(weight):
        return [take(weight, 1, rank + z * groups, per_shard) for z in range(shards)]

    own_gate_up = jnp.concatenate(hidden_columns(w_gate) + hidden_columns(w_up), axis=1)
    own_down = take(w_down, 0, rank, per_shard)
    out_grid = w_out.reshape(-1, 2, width, feats)
    own_out = take(out_grid, 1, core, 1).reshape(-1, feats)

    qkv = lax.all_gather(own_qkv, "fsdp", axis=0, tiled=True)
    gain_one, gain_two = qkv[:, 3 * width][None, :], qkv[:, 3 * width + 1][None, :]
    out_pieces = shard_pieces(own_out)
    merged = 2 * hidden_width == feats
    if merged:
        ffn_own = [jnp.concatenate([own_gate_up, own_down])]
    else:
        ffn_own = [own_gate_up, own_down]
    ffn_pieces = [lax.all_gather(value, "fsdp", axis=0) for value in ffn_own]

    def flat(*pair):
        return [value.reshape(tokens, feats) for value in pair]

    def by_chip(value):
        return value.reshape(chips, rows, feats)

    x_zero, x_one = [inputs[:, b] for b in range(seqs)]
    cot_all = [cotangent[:, b] for b in range(seqs)]
    cots = [
        lax.all_gather(c, PLANE, axis=0).reshape(chips, 2, rows, feats) for c in cot_all
    ]
    tables = [(rel_table, send_table, first[b], full[b]) for b in range(seqs)]

    def forward(b, near, far):
        query, key, value, normed, sent, fine, logsum = attend_forward(
            tables[b], *flat(near, far), qkv, gain_one, start[b][:, None], width
        )
        return (query, key, value, fine, logsum), normed, sent.reshape(chips, 2 * rows, width)

    def mid_norm(x_own, own, swapped):
        middle = x_own.astype(f32) + own + swapped
        return middle, (middle * row_scale(middle) * gain_two.astype(f32)).astype(bf16)

    near_zero = spread(x_zero)
    near_one = spread(hold(x_one, near_zero))
    saved_zero, normed_zero, sent_zero = forward(0, near_zero, swap_core(near_zero))
    near_one, out_pieces = hold((near_one, out_pieces), sent_zero)
    got_zero = exchange(sent_zero)
    saved_one, normed_one, sent_one = forward(1, near_one, swap_core(near_one))
    got_zero = hold(got_zero, sent_one)
    got_one = exchange(sent_one)
    att_zero, own, other = mix(ids, got_zero, out_pieces)
    mid_zero, norm_zero = mid_norm(x_zero, own, swap_core(other))
    got_one = hold(got_one, norm_zero)
    near_zero = spread(hold(norm_zero, got_one))
    att_one, own, other = mix(ids, got_one, out_pieces)
    mid_one, norm_one = mid_norm(x_one, own, swap_core(other))
    near_zero = hold(near_zero, norm_one)
    near_one = spread(hold(norm_one, near_zero))

    def ffn(b, near, far, split):
        mids = flat(near, far)
        *out_part, mid_near, mid_far, hidden, grad_pre = feed_forward(
            ids, mids, cots[b], ffn_pieces, hidden_width, split
        )
        return out_part, by_chip(mid_near), by_chip(mid_far), (*mids, cots[b], hidden, grad_pre)

    out_zero, own_zero, far_zero, stream_zero = ffn(0, near_zero, swap_core(near_zero), False)
    near_one = hold(near_one, stream_zero[3])
    total_zero = core_sum(own_zero, swap_core(far_zero))
    near_far = hold((near_one, swap_core(near_one)), total_zero)
    out_one, own_one, far_one, stream_one = ffn(1, *near_far, True)
    sums_zero = hold(exchange(total_zero), stream_one[3])
    total_one = core_sum(own_one, swap_core(far_one))

    out_sum_zero = lax.psum_scatter(
        out_zero[0].reshape(groups * rows, feats), PLANE, scatter_dimension=0, tiled=True
    )

    def mid_backward(b, grad_normed_mid, middle):
        scale_two = row_scale(middle)
        unit_two = middle * scale_two
        scaled_two = grad_normed_mid * gain_two.astype(f32)
        grad_middle = cot_all[b].astype(f32) + scale_two * (
            scaled_two - unit_two * jnp.mean(scaled_two * unit_two, axis=-1, keepdims=True)
        )
        return grad_middle, grad_middle.astype(bf16)

    def backward(b, saved, grad_got):
        return attend_backward(
            tables[b], saved, grad_got.reshape(seq_len, width), qkv, tiled[b][:, None, :]
        )

    def qkv_sums(normed, grads):
        return dot_tn(normed.reshape(seq_len, feats), grads.reshape(seq_len, 3 * width))

    def in_backward(grad_normed_in, grad_middle, x_own):
        flat_in = x_own.astype(f32)
        scale_one = row_scale(flat_in)
        unit_one = flat_in * scale_one
        scaled_one = grad_normed_in * gain_one.astype(f32)
        return (
            grad_middle
            + scale_one
            * (scaled_one - unit_one * jnp.mean(scaled_one * unit_one, axis=-1, keepdims=True))
        ).astype(bf16)

    grad_mid_zero, branch = mid_backward(0, last_sum(sums_zero), mid_zero)
    grad_sent, grad_out_zero = unmix(ids, branch, swap_core(branch), att_zero, out_pieces, chips)
    streams = hold((stream_zero, stream_one), grad_sent)
    ffn_sums = weight_sums(ids, streams, shards)
    grad_got_zero, out_sum_zero = hold((exchange(grad_sent), out_sum_zero), ffn_sums[0])
    grad_got_zero = hold(grad_got_zero, out_sum_zero)
    shares = [lax.psum_scatter(value, "fsdp", scatter_dimension=0) for value in ffn_sums]
    sums_one = exchange(hold(total_one, grad_got_zero))
    part_near, part_far, grads_zero = backward(0, saved_zero, grad_got_zero)
    sums_one = hold(sums_one, grads_zero)
    far_swapped = swap_core(by_chip(part_far))
    grad_mid_one, branch = mid_backward(1, last_sum(sums_one), mid_one)
    grad_sent, grad_out_one = unmix(ids, branch, swap_core(branch), att_one, out_pieces, chips)
    grad_got_one = exchange(grad_sent)
    far_swapped = hold(far_swapped, grad_sent)
    total_zero = core_sum(by_chip(part_near), far_swapped)
    sums_zero = exchange(hold(total_zero, grad_got_one))

    own_rows = feats // shards

    def rel_rows(value):
        value = value.astype(bf16)
        count = value.shape[0] // shards
        return [take(value, 0, ids[1] ^ r, count) for r in range(shards)]

    out_rel = rel_rows(grad_out_zero + grad_out_one)
    out_sent = send_pieces(out_rel)
    grad_got_one, shares = hold((grad_got_one, shares), total_zero)
    full_ffn = [lax.all_gather(share, PLANE, axis=0) for share in shares]
    part_near, part_far, grads_one = backward(1, saved_one, grad_got_one)
    part_near, part_far, grads_one, sums_zero, out_sent = lax.optimization_barrier(
        (part_near, part_far, grads_one, sums_zero, out_sent)
    )
    far_swapped = swap_core(by_chip(part_far))
    grad_qkv = qkv_sums(normed_zero, grads_zero) + qkv_sums(normed_one, grads_one)
    far_swapped = hold(far_swapped, full_ffn)
    sums_one = exchange(core_sum(by_chip(part_near), far_swapped))
    out_near, out_far = [by_chip(part) for part in out_one]
    total_out = hold(core_sum(out_near, swap_core(out_far)), sums_one)
    out_sum_one = last_sum(exchange(total_out))
    share_out = lax.all_gather(add_pieces(out_rel[0], out_sent), PLANE, axis=0).astype(f32)
    full_qkv = lax.all_gather(shard_sum(rel_rows(grad_qkv)), PLANE, axis=0)

    outputs = [
        (mid_zero + out_sum_zero.astype(f32)).astype(bf16),
        (mid_one + out_sum_one).astype(bf16),
    ]
    grad_inputs = [
        in_backward(last_sum(sums_zero), grad_mid_zero, x_zero),
        in_backward(last_sum(sums_one), grad_mid_one, x_one),
    ]
    g_gate_up, g_gain_two, (g_down,) = assemble(
        full_ffn[0],
        gain_ffn,
        (w_gate, w_up),
        shards,
        full_ffn[-1],
        own_rows if merged else 0,
        per_shard,
    )
    g_down = g_down.reshape(-1, feats)
    g_qkv, g_gain_one, _ = assemble(full_qkv, gain_attn, (w_query, w_key, w_value), 1)
    share_out = share_out.reshape(chips, 2, -1, width, feats)
    g_out = jnp.sum(share_out, axis=0).transpose(1, 0, 2, 3).reshape(own_rows, feats)

    return (
        jnp.stack(outputs, axis=1),
        jnp.stack(grad_inputs, axis=1),
        *g_qkv,
        g_out,
        *g_gate_up,
        g_down,
        g_gain_one,
        g_gain_two,
    )


def solution(mesh):
    names = mesh.axis_names
    ctx, shards = mesh.shape[names[0]], mesh.shape[names[1]]
    fine_mesh = Mesh(mesh.devices.reshape(ctx // 2, 2, shards), ("chip", "core", "fsdp"))
    by_row = P("fsdp", None)
    by_token = P(PLANE, "fsdp", None)
    return jax.shard_map(
        per_device,
        mesh=fine_mesh,
        in_specs=(by_token,) + (by_row,) * 7 + (P("fsdp"), P("fsdp"), P(None, "fsdp"), P(), by_token),
        out_specs=(by_token, by_token) + (by_row,) * 7 + (P("fsdp"), P("fsdp")),
        check_vma=False,
    )
```

```python
import functools

import jax
import jax.numpy as jnp
from jax import lax
from jax.experimental import pallas as pl
from jax.experimental.pallas import tpu as pltpu
from jax.sharding import Mesh, PartitionSpec as P

HEAD_DIM = 64
EPSILON = 1e-05
MASKED = -1e30
TILE = 256
PROJ = 512
Q_FORE, K_FORE = 512, 512
Q_BACK, K_BACK = 512, 512
PLANE = ("chip", "core")

bf16 = jnp.bfloat16
f32 = jnp.float32


def dot_nn(left_op, right_op):
    return lax.dot_general(left_op, right_op, (((1,), (0,)), ((), ())), preferred_element_type=f32)


def dot_nt(left_op, right_op):
    return lax.dot_general(left_op, right_op, (((1,), (1,)), ((), ())), preferred_element_type=f32)


def dot_tn(left_op, right_op):
    return lax.dot_general(left_op, right_op, (((0,), (0,)), ((), ())), preferred_element_type=f32)


def row_scale(values):
    return lax.rsqrt(jnp.mean(values * values, axis=-1, keepdims=True) + EPSILON)


def swap_core(value):
    return lax.ppermute(value, "core", [(0, 1), (1, 0)])


def swap_chip(value, mask):
    count = lax.axis_size("chip")
    return lax.ppermute(value, "chip", [(i, i ^ mask) for i in range(count)])


def swap_shard(value, mask):
    count = lax.axis_size("fsdp")
    return lax.ppermute(value, "fsdp", [(i, i ^ mask) for i in range(count)])


def hold(value, *deps):
    return lax.optimization_barrier((value, deps))[0]


def spread(value):
    count = lax.axis_size("chip")
    return exchange(jnp.broadcast_to(value, (count,) + value.shape))


def exchange(value):
    return lax.all_to_all(value, "chip", 0, 0)


def add_kernel(own, other, total):
    total[...] = (own[...].astype(f32) + other[...].astype(f32)).astype(bf16)


def exchange_pieces(pieces):
    return [pieces[0]] + [swap_chip(pieces[r], r) for r in range(1, len(pieces))]


def core_sum(own, swapped):
    chips, rows, width = own.shape
    block = pl.BlockSpec((chips // 2, rows, width), lambda t: (t, 0, 0))
    return pl.pallas_call(
        add_kernel,
        grid=(2,),
        out_shape=jax.ShapeDtypeStruct(own.shape, bf16),
        in_specs=[block, block],
        out_specs=block,
        cost_estimate=cost(3),
        name="core_sum",
    )(own, swapped)


def last_sum(value):
    return jnp.sum(value.astype(f32), axis=0)


def shard_pieces(value):
    return [value] + [swap_shard(value, r) for r in range(1, lax.axis_size("fsdp"))]


def shard_sum(pieces):
    return add_pieces(pieces[0], send_pieces(pieces))


def in_order(pieces, shard):
    stacked = jnp.stack(pieces)
    rows = [lax.dynamic_index_in_dim(stacked, shard ^ z, keepdims=False) for z in range(len(pieces))]
    return jnp.concatenate(rows)


def send_pieces(pieces):
    return [swap_shard(pieces[r], r) for r in range(1, len(pieces))]


def add_pieces(own, received):
    total = own.astype(f32)
    for piece in received:
        total = total + piece.astype(f32)
    return total.astype(bf16)


def head_masks(rows, width):
    lanes = lax.broadcasted_iota(jnp.int32, (rows, width), 1) // HEAD_DIM
    return [lanes == h for h in range(width // HEAD_DIM)]


def stack_heads(values, masks):
    zero = jnp.zeros_like(values)
    return jnp.concatenate([jnp.where(mask, values, zero) for mask in masks], axis=0)


def merge_heads(stacked, masks, rows):
    merged = stacked[:rows]
    for h in range(1, len(masks)):
        merged = jnp.where(masks[h], stacked[h * rows : (h + 1) * rows], merged)
    return merged


def forward_kernel(
    rel, send, first, full, x_near, x_far, weight, gain, start,
    query, key, value, normed, fine, logsum, *refs,
):
    attended, (scores, top, total) = refs[:-3], refs[-3:]
    width = query.shape[1]
    seq_len = query.shape[0]
    heads = width // HEAD_DIM
    blk = TILE // 2
    tiles = x_near.shape[0] // PROJ
    blocks = PROJ // blk
    gain_row = gain[...].astype(f32)
    for s, source in ((0, x_near), (1, x_far)):

        def project(t, _, s=s, source=source):
            rows = pl.ds(pl.multiple_of(t * PROJ, PROJ), PROJ)
            rows_in = source[rows, :].astype(f32)
            tile = (rows_in * row_scale(rows_in) * gain_row).astype(bf16)
            normed[s, rows, :] = tile
            mixed = dot_nn(tile, weight[:, : 3 * width])
            for h in range(blocks):
                place = rel[(s * tiles + t) * blocks + h]
                where = pl.ds(pl.multiple_of(place * blk, blk), blk)
                part = mixed[h * blk : (h + 1) * blk]
                query[where, :] = (part[:, :width].astype(bf16) * 0.125).astype(bf16)
                key[where, :] = part[:, width : 2 * width].astype(bf16)
                value[where, :] = part[:, 2 * width :].astype(bf16)
            return 0

        lax.fori_loop(0, tiles, project, 0)

    masks = head_masks(Q_FORE, width)
    big = heads * Q_FORE

    def query_tile(qb, _):
        rows = pl.ds(pl.multiple_of(qb * Q_FORE, Q_FORE), Q_FORE)
        stacked = stack_heads(query[rows, :], masks)
        top[...] = jnp.full_like(top, MASKED)
        begin = jnp.concatenate([start[rows, :]] * heads, axis=0)
        diagonal = qb * Q_FORE // K_FORE
        last = (qb * Q_FORE + Q_FORE + K_FORE - 1) // K_FORE

        def score(kb, masked):
            keys = key[pl.ds(pl.multiple_of(kb * K_FORE, K_FORE), K_FORE), :]
            raw = dot_nt(stacked, keys)
            if masked:
                k_pos = kb * K_FORE + lax.broadcasted_iota(jnp.int32, (big, K_FORE), 1)
                q_row = lax.broadcasted_iota(jnp.int32, (big, K_FORE), 0) & (Q_FORE - 1)
                allowed = (k_pos >= begin) & (k_pos <= qb * Q_FORE + q_row)
                raw = jnp.where(allowed, raw, MASKED)
            scores[kb] = raw
            best = raw[:, :128]
            for c in range(1, K_FORE // 128):
                best = jnp.maximum(best, raw[:, c * 128 : (c + 1) * 128])
            top[...] = jnp.maximum(top[...], best)

        def masked_step(kb, _):
            score(kb, True)
            return 0

        def plain_step(kb, _):
            score(kb, False)
            return 0

        lax.fori_loop(first[qb], full[qb], masked_step, 0)
        lax.fori_loop(full[qb], diagonal, plain_step, 0)
        lax.fori_loop(diagonal, last, masked_step, 0)
        peak = jnp.max(top[...], axis=1, keepdims=True)
        top[...] = jnp.broadcast_to(peak, top.shape)
        total[...] = jnp.zeros_like(total)

        def weigh(kb, carry):
            vals = value[pl.ds(pl.multiple_of(kb * K_FORE, K_FORE), K_FORE), :]
            pieces = []
            summed = total[...]
            for c in range(K_FORE // 128):
                piece = jnp.exp(scores[kb, :, c * 128 : (c + 1) * 128] - top[...])
                summed = summed + piece
                pieces.append(piece.astype(bf16))
            total[...] = summed
            return carry + dot_nn(jnp.concatenate(pieces, axis=1), vals)

        gathered = lax.fori_loop(first[qb], last, weigh, jnp.zeros((big, width), f32))
        denom = jnp.sum(total[...], axis=1, keepdims=True)
        fine[rows, :] = merge_heads(gathered / denom, masks, Q_FORE)
        logs = jnp.broadcast_to(peak + jnp.log(denom), (big, width))
        logsum[rows, :] = merge_heads(logs, masks, Q_FORE)
        return 0

    lax.fori_loop(0, seq_len // Q_FORE, query_tile, 0)

    count = seq_len // blk // len(attended)
    for r, piece in enumerate(attended):
        for j in range(count):
            where = pl.ds(pl.multiple_of(send[r * count + j] * blk, blk), blk)
            piece[j * blk : (j + 1) * blk, :] = fine[where, :].astype(bf16)


def backward_kernel(
    rel, send, first, full, query, key, value, fine, logsum, weight, start, *refs
):
    grad_in, refs = refs[:-8], refs[-8:]
    part_near, part_far, grads, grad_at, grad_q, grad_k, grad_v, grad_q2 = refs
    seq_len, width = query.shape
    heads = width // HEAD_DIM
    blk = TILE // 2
    big = heads * Q_BACK

    count = seq_len // blk // len(grad_in)
    for r, piece in enumerate(grad_in):
        for j in range(count):
            where = pl.ds(pl.multiple_of(send[r * count + j] * blk, blk), blk)
            grad_at[where, :] = piece[j * blk : (j + 1) * blk, :]
    grad_k[...] = jnp.zeros_like(grad_k)
    grad_v[...] = jnp.zeros_like(grad_v)
    masks = head_masks(Q_BACK, width)

    def flip(values):
        if width < 128:
            values = jnp.concatenate([values, jnp.zeros((Q_BACK, 128 - width), f32)], axis=1)
        return values.T

    def query_tile(qb, _):
        rows = pl.ds(pl.multiple_of(qb * Q_BACK, Q_BACK), Q_BACK)
        stacked = stack_heads(query[rows, :], masks)
        grad_rows = grad_at[rows, :]
        grad_stacked = stack_heads(grad_rows, masks)
        products = flip(grad_rows.astype(f32) * fine[rows, :])
        logs = flip(logsum[rows, :])
        delta = jnp.concatenate(
            [
                jnp.sum(products[h * HEAD_DIM : (h + 1) * HEAD_DIM], axis=0, keepdims=True)
                for h in range(heads)
            ],
            axis=1,
        )
        log_row = jnp.concatenate(
            [logs[h * HEAD_DIM : h * HEAD_DIM + 1] for h in range(heads)], axis=1
        )
        begin = jnp.concatenate([start[qb]] * heads, axis=1)
        grad_q2[...] = jnp.zeros_like(grad_q2)
        diagonal = qb * Q_BACK // K_BACK
        last = (qb * Q_BACK + Q_BACK + K_BACK - 1) // K_BACK

        def step(kb, masked):
            where = pl.ds(pl.multiple_of(kb * K_BACK, K_BACK), K_BACK)
            keys = key[where, :]
            probs = jnp.exp(dot_nt(keys, stacked) - log_row)
            if masked:
                k_pos = kb * K_BACK + lax.broadcasted_iota(jnp.int32, (K_BACK, big), 0)
                q_row = lax.broadcasted_iota(jnp.int32, (K_BACK, big), 1) & (Q_BACK - 1)
                allowed = (k_pos >= begin) & (k_pos <= qb * Q_BACK + q_row)
                probs = jnp.where(allowed, probs, 0.0)
            slope = (probs * (dot_nt(value[where, :], grad_stacked) - delta)).astype(bf16)
            grad_v[where, :] += dot_nn(probs.astype(bf16), grad_stacked)
            grad_k[where, :] += dot_nn(slope, stacked)
            grad_q2[...] += dot_tn(slope, keys)

        def masked_step(kb, _):
            step(kb, True)
            return 0

        def plain_step(kb, _):
            step(kb, False)
            return 0

        lax.fori_loop(first[qb], full[qb], masked_step, 0)
        lax.fori_loop(full[qb], diagonal, plain_step, 0)
        lax.fori_loop(diagonal, last, masked_step, 0)
        grad_q[rows, :] = (merge_heads(grad_q2[...], masks, Q_BACK) * 0.125).astype(bf16)
        return 0

    lax.fori_loop(0, seq_len // Q_BACK, query_tile, 0)

    tiles = seq_len // PROJ // 2
    blocks = PROJ // blk

    def project(t, side, part):
        rows = pl.ds(pl.multiple_of(t * PROJ, PROJ), PROJ)
        base = side * tiles + t
        for h in range(blocks):
            where = pl.ds(pl.multiple_of(rel[base * blocks + h] * blk, blk), blk)
            here = pl.ds(pl.multiple_of(t * PROJ + h * blk, blk), blk)
            grads[side, here, :width] = grad_q[where, :]
            grads[side, here, width : 2 * width] = grad_k[where, :].astype(bf16)
            grads[side, here, 2 * width :] = grad_v[where, :].astype(bf16)
        part[rows, :] = dot_nt(grads[side, rows, :], weight[:, : 3 * width]).astype(bf16)
        return 0

    for side, part in ((0, part_near), (1, part_far)):
        lax.fori_loop(0, tiles, lambda t, _, s=side, p=part: project(t, s, p), 0)


def place_pieces(target, pieces, shard, begin, count):
    for r, piece in enumerate(pieces):
        at = pl.multiple_of((shard ^ r) * count, count)
        target[pl.ds(at, count), :] = piece[begin : begin + count, :]


def near_first(target, source, chip, count):
    for r in range(count):
        rows = target.shape[0] // count
        at = pl.multiple_of((chip ^ r) * rows, rows)
        target[r * rows : (r + 1) * rows, :] = source[pl.ds(at, rows), :]


def mix_kernel(ids, *refs, chips):
    got, pieces, (attended, own, other, whole, weight) = refs[:chips], refs[chips:-5], refs[-5:]
    rows = own.shape[0]
    place_pieces(whole, pieces, ids[1], 0, pieces[0].shape[0])
    near_first(weight, whole, ids[2], chips)
    joined = jnp.concatenate([piece[...] for piece in got], axis=1)
    attended[...] = joined
    own[...] = dot_nn(joined[:rows], weight[...])
    other[...] = dot_nn(joined[rows:], weight[...])


def unmix_kernel(ids, own, other, attended, *refs, chips):
    outs = chips + 3
    pieces, grad_sent, (grad_weight, whole, weight) = refs[:-outs], refs[-outs:-3], refs[-3:]
    place_pieces(whole, pieces, ids[1], 0, pieces[0].shape[0])
    near_first(weight, whole, ids[2], chips)
    branch = jnp.concatenate([own[...], other[...]], axis=0)
    mixed = dot_nt(branch, weight[...]).astype(bf16)
    sums = dot_tn(attended[...], branch)
    width = grad_sent[0].shape[1]
    for r in range(chips):
        grad_sent[r][...] = mixed[:, r * width : (r + 1) * width]
        at = pl.multiple_of((ids[2] ^ r) * width, width)
        grad_weight[pl.ds(at, width), :] = sums[r * width : (r + 1) * width]


def qkv_kernel(ids, *refs):
    normed, grads, before = refs[:3]
    outs, total = refs[3:-1], refs[-1]
    t = pl.program_id(0)

    @pl.when(t == 0)
    def _():
        total[...] = before[...]

    total[...] += dot_tn(normed[...], grads[...])

    @pl.when(t == pl.num_programs(0) - 1)
    def _():
        rows = outs[0].shape[0]
        for r, out in enumerate(outs):
            at = pl.multiple_of((ids[1] ^ r) * rows, rows)
            out[...] = total[pl.ds(at, rows), :].astype(bf16)


def ffn_kernel(ids, x_near, x_far, *refs, split, sides):
    cot_refs, refs = refs[:sides], refs[sides:]
    outs = 7 + split
    pieces, out_parts = refs[:-outs], refs[-outs : 1 + split - outs]
    mid_near, mid_far, hidden, grad_pre, gate_up, down = refs[-6:]
    t = pl.program_id(0)
    half = pl.num_programs(0) // 2
    feats, size = gate_up.shape[0], gate_up.shape[1] // 2
    shards = pieces[0].shape[0]
    rows, more = feats // shards, size // shards
    begin = rows if len(pieces) == 1 else 0

    @pl.when(t == 0)
    def _():
        for z in range(shards):
            gate_up[z * rows : (z + 1) * rows, :] = pieces[0][z, :rows, :]
            down[z * more : (z + 1) * more, :] = pieces[-1][z, begin : begin + more, :]

    tile = jnp.where(t < half, x_near[...], x_far[...])
    cot = cot_refs[0][...].reshape(tile.shape)
    if sides == 2:
        cot = jnp.where(t < half, cot, cot_refs[1][...])
    pre = dot_nn(tile, gate_up[...])
    gate_pre, up_pre = pre[:, :size], pre[:, size:]
    sigma = jax.nn.sigmoid(gate_pre)
    active = gate_pre * sigma
    low = (active * up_pre).astype(bf16)
    grad_hidden = dot_nt(cot, down[...])
    hidden[...] = low
    out_part = dot_nn(low, down[...]).astype(bf16)
    grad_gate = grad_hidden * up_pre * sigma * (1.0 + gate_pre * (1.0 - sigma))
    grad_up = grad_hidden * active
    grads = jnp.concatenate([grad_gate.astype(bf16), grad_up.astype(bf16)], axis=1)
    grad_pre[...] = grads
    mid_part = dot_nt(grads, gate_up[...]).astype(bf16)

    if not split:
        out_parts[0][...] = out_part.reshape(out_parts[0].shape)

    @pl.when(t < half)
    def _():
        mid_near[...] = mid_part
        if split:
            out_parts[0][...] = out_part

    @pl.when(t >= half)
    def _():
        mid_far[...] = mid_part
        if split:
            out_parts[1][...] = out_part


def weight_kernel(ids, *refs, counts, shards):
    streams = len(counts)
    ins, outs, (wide, down) = refs[: sum(counts)], refs[sum(counts) : -2], refs[-2:]
    t = pl.program_id(0)
    per = pl.num_programs(0) // streams

    @pl.when(t == 0)
    def _():
        wide[...] = jnp.zeros_like(wide)
        down[...] = jnp.zeros_like(down)

    for b in range(streams):
        mine = ins[sum(counts[:b]) : sum(counts[: b + 1])]

        @pl.when((t >= b * per) & (t < (b + 1) * per))
        def _(b=b, mine=mine):
            x_near, x_far, hidden, grad_pre = mine[:4]
            near = t < b * per + per // 2
            tile = jnp.where(near, x_near[...], x_far[...])
            cot = mine[4][...].reshape(tile.shape)
            if len(mine) == 6:
                cot = jnp.where(near, cot, mine[5][...])
            wide[...] += dot_tn(tile, grad_pre[...])
            down[...] += dot_tn(hidden[...], cot)

    @pl.when(t == pl.num_programs(0) - 1)
    def _():
        rows, more = wide.shape[0] // shards, down.shape[0] // shards
        begin = rows if len(outs) == 1 else 0
        for z in range(shards):
            outs[0][z, :rows, :] = wide[z * rows : (z + 1) * rows, :].astype(bf16)
            piece = down[z * more : (z + 1) * more, :]
            outs[-1][z, begin : begin + more, :] = piece.astype(bf16)


def assemble_kernel(*refs, kinds, shards, with_down):
    parts, gain = refs[:2]
    weights = refs[2 : 2 + kinds]
    rest = refs[2 + kinds :]
    if with_down:
        down_part, rest = rest[0], rest[1:]
    outs, gain_out = rest[:kinds], rest[kinds]
    groups, _, size = parts.shape
    pieces = size // kinds
    lanes = pieces // shards
    sums = 0.0
    for k in range(kinds):
        columns = []
        for z in range(shards):
            for i in range(groups):
                at = k * pieces + z * lanes
                columns.append(parts[i, :, at : at + lanes].astype(f32))
        full = jnp.concatenate(columns, axis=1)
        outs[k][...] = full
        sums = sums + jnp.sum(full * weights[k][...].astype(f32), axis=1, keepdims=True)
    gain_out[...] = sums / gain[...].astype(f32)
    if with_down:
        rest[kinds + 1][...] = down_part[...].astype(f32)


def smem():
    return pl.BlockSpec(memory_space=pltpu.SMEM)


def vmem():
    return pl.BlockSpec(memory_space=pltpu.VMEM)


def cost(micros):
    return pl.CostEstimate(flops=micros * 10**9, bytes_accessed=2**20, transcendentals=0)


LIMIT = pltpu.CompilerParams(vmem_limit_bytes=56 * 2**20)


def attend_forward(tables, x_near, x_far, weight, gain, start, width, chips):
    half_rows, feats = x_near.shape
    seq_len = 2 * half_rows
    big = (width // HEAD_DIM) * Q_FORE
    shape = jax.ShapeDtypeStruct
    narrow = shape((seq_len, width), bf16)
    wide = shape((seq_len, width), f32)
    pairs = seq_len * seq_len * width // 2
    return pl.pallas_call(
        forward_kernel,
        out_shape=[narrow, narrow, narrow, shape((2, half_rows, feats), bf16), wide, wide]
        + [shape((seq_len // chips, width), bf16)] * chips,
        in_specs=[smem()] * 4 + [vmem()] * 5,
        out_specs=[vmem()] * (6 + chips),
        scratch_shapes=[
            pltpu.VMEM((seq_len // K_FORE, big, K_FORE), f32),
            pltpu.VMEM((big, 128), f32),
            pltpu.VMEM((big, 128), f32),
        ],
        compiler_params=LIMIT,
        cost_estimate=cost(31),
        name="attend_forward",
    )(*tables, x_near, x_far, weight, gain, start)


def attend_backward(tables, saved, grad_in, weight, start):
    query = saved[0]
    seq_len, width = query.shape
    feats = weight.shape[0]
    big = (width // HEAD_DIM) * Q_BACK
    shape = jax.ShapeDtypeStruct
    pairs = seq_len * seq_len * width // 2
    return pl.pallas_call(
        backward_kernel,
        out_shape=(
            shape((seq_len // 2, feats), bf16),
            shape((seq_len // 2, feats), bf16),
            shape((2, seq_len // 2, 3 * width), bf16),
        ),
        in_specs=[smem()] * 4 + [vmem()] * (7 + len(grad_in)),
        out_specs=[vmem()] * 3,
        scratch_shapes=[
            pltpu.VMEM((seq_len, width), bf16),
            pltpu.VMEM((seq_len, width), bf16),
            pltpu.VMEM((seq_len, width), f32),
            pltpu.VMEM((seq_len, width), f32),
            pltpu.VMEM((big, width), f32),
        ],
        compiler_params=LIMIT,
        cost_estimate=cost(31),
        name="attend_backward",
    )(*tables, *saved, weight, start, *grad_in)


def mix(ids, got, pieces):
    chips = len(got)
    doubled, width = got[0].shape
    feats = pieces[0].shape[1]
    size = chips * width
    shape = jax.ShapeDtypeStruct
    return pl.pallas_call(
        functools.partial(mix_kernel, chips=chips),
        out_shape=(
            shape((doubled, size), bf16),
            shape((doubled // 2, feats), f32),
            shape((doubled // 2, feats), f32),
        ),
        in_specs=[smem()] + [vmem()] * (chips + len(pieces)),
        out_specs=[vmem()] * 3,
        scratch_shapes=[pltpu.VMEM((size, feats), bf16)] * 2,
        compiler_params=LIMIT,
        cost_estimate=cost(3),
        name="mix",
    )(ids, *got, *pieces)


def unmix(ids, own, other, attended, pieces, chips):
    rows, feats = own.shape
    size = attended.shape[1]
    shape = jax.ShapeDtypeStruct
    outs = pl.pallas_call(
        functools.partial(unmix_kernel, chips=chips),
        out_shape=[shape((2 * rows, size // chips), bf16)] * chips + [shape((size, feats), f32)],
        in_specs=[smem()] + [vmem()] * (3 + len(pieces)),
        out_specs=[vmem()] * (chips + 1),
        scratch_shapes=[pltpu.VMEM((size, feats), bf16)] * 2,
        compiler_params=LIMIT,
        cost_estimate=cost(4),
        name="unmix",
    )(ids, own, other, attended, *pieces)
    return outs[:-1], outs[-1]


ROWS = 512


def feed_forward(ids, mids, cot, pieces, size, split):
    tokens, feats = mids[0].shape
    rows = ROWS // 2
    chips = tokens // rows
    half = tokens // ROWS
    shape = jax.ShapeDtypeStruct
    near = pl.BlockSpec((ROWS, feats), lambda t, ids: (jnp.minimum(t, half - 1), 0))
    far = pl.BlockSpec((ROWS, feats), lambda t, ids: (jnp.maximum(t - half, 0), 0))
    by_device = pl.BlockSpec(
        (ROWS // rows, None, rows, feats),
        lambda t, ids: (lax.rem(t, half), ids[0] ^ lax.div(t, half), 0, 0),
    )
    cot_specs = [by_device] if len(cot) == 1 else [near, far]

    def tiles(width):
        return pl.BlockSpec((ROWS, width), lambda t, ids: (t, 0))

    side = shape((tokens, feats), bf16)
    return pl.pallas_call(
        functools.partial(ffn_kernel, split=split, sides=len(cot)),
        grid_spec=pltpu.PrefetchScalarGridSpec(
            num_scalar_prefetch=1,
            grid=(2 * half,),
            in_specs=[near, far, *cot_specs]
            + [pl.BlockSpec(piece.shape, lambda t, ids: (0, 0, 0)) for piece in pieces],
            out_specs=([near, far] if split else [by_device])
            + [near, far, tiles(size), tiles(2 * size)],
            scratch_shapes=[
                pltpu.VMEM((feats, 2 * size), bf16),
                pltpu.VMEM((size, feats), bf16),
            ],
        ),
        out_shape=([side, side] if split else [shape((chips, 2, rows, feats), bf16)])
        + [
            side,
            side,
            shape((2 * tokens, size), bf16),
            shape((2 * tokens, 2 * size), bf16),
        ],
        compiler_params=LIMIT,
        cost_estimate=cost(20),
        name="feed_forward",
    )(ids, *mids, *cot, *pieces)


def weight_sums(ids, streams, shards):
    tokens, feats = streams[0][0].shape
    size = streams[0][2].shape[1]
    rows = ROWS // 2
    half = tokens // ROWS
    per = 2 * half
    shape = jax.ShapeDtypeStruct
    specs = []
    for b in range(len(streams)):

        def local(t, b=b):
            return jnp.clip(t - b * per, 0, per - 1)

        near = pl.BlockSpec(
            (ROWS, feats), lambda t, ids, f=local: (jnp.minimum(f(t), half - 1), 0)
        )
        far = pl.BlockSpec(
            (ROWS, feats), lambda t, ids, f=local: (jnp.maximum(f(t) - half, 0), 0)
        )
        by_device = pl.BlockSpec(
            (ROWS // rows, None, rows, feats),
            lambda t, ids, f=local: (lax.rem(f(t), half), ids[0] ^ lax.div(f(t), half), 0, 0),
        )
        specs += [
            near,
            far,
            pl.BlockSpec((ROWS, size), lambda t, ids, f=local: (f(t), 0)),
            pl.BlockSpec((ROWS, 2 * size), lambda t, ids, f=local: (f(t), 0)),
        ]
        specs += [by_device] if len(streams[b]) == 5 else [near, far]
    if 2 * size == feats:
        outs = [(shards, (feats + size) // shards, feats)]
    else:
        outs = [(shards, feats // shards, 2 * size), (shards, size // shards, feats)]
    return pl.pallas_call(
        functools.partial(weight_kernel, counts=[len(v) for v in streams], shards=shards),
        grid_spec=pltpu.PrefetchScalarGridSpec(
            num_scalar_prefetch=1,
            grid=(per * len(streams),),
            in_specs=specs,
            out_specs=[pl.BlockSpec(out, lambda t, ids: (0, 0, 0)) for out in outs],
            scratch_shapes=[pltpu.VMEM((feats, 2 * size), f32), pltpu.VMEM((size, feats), f32)],
        ),
        out_shape=[shape(out, bf16) for out in outs],
        compiler_params=LIMIT,
        cost_estimate=cost(23),
        name="weight_sums",
    )(ids, *[value for stream in streams for value in stream])


def qkv_first(normed, grads):
    tokens, feats = normed.shape
    size = grads.shape[1]

    def kernel(normed_ref, grads_ref, total):
        @pl.when(pl.program_id(0) == 0)
        def _():
            total[...] = jnp.zeros_like(total)

        total[...] += dot_tn(normed_ref[...], grads_ref[...])

    return pl.pallas_call(
        kernel,
        grid=(tokens // ROWS,),
        out_shape=jax.ShapeDtypeStruct((feats, size), f32),
        in_specs=[
            pl.BlockSpec((ROWS, feats), lambda t: (t, 0)),
            pl.BlockSpec((ROWS, size), lambda t: (t, 0)),
        ],
        out_specs=pl.BlockSpec((feats, size), lambda t: (0, 0)),
        compiler_params=LIMIT,
        cost_estimate=cost(6),
        name="qkv_first",
    )(normed, grads)


def qkv_sums(ids, normed, grads, before, shards):
    tokens, feats = normed.shape
    size = grads.shape[1]
    out = (feats // shards, size)
    return pl.pallas_call(
        qkv_kernel,
        grid_spec=pltpu.PrefetchScalarGridSpec(
            num_scalar_prefetch=1,
            grid=(tokens // ROWS,),
            in_specs=[
                pl.BlockSpec((ROWS, feats), lambda t, ids: (t, 0)),
                pl.BlockSpec((ROWS, size), lambda t, ids: (t, 0)),
                pl.BlockSpec((feats, size), lambda t, ids: (0, 0)),
            ],
            out_specs=[pl.BlockSpec(out, lambda t, ids: (0, 0))] * shards,
            scratch_shapes=[pltpu.VMEM((feats, size), f32)],
        ),
        out_shape=[jax.ShapeDtypeStruct(out, bf16)] * shards,
        compiler_params=LIMIT,
        cost_estimate=cost(6),
        name="qkv_sums",
    )(ids, normed, grads, before)


STEPS = 4


def assemble(parts, gain, weights, shards, downs=None, begin=0, down_rows=0):
    rows, columns = weights[0].shape
    step = rows // STEPS
    shape = jax.ShapeDtypeStruct
    groups, _, size = parts.shape
    row_block = pl.BlockSpec((step, columns), lambda t: (t, 0))
    thin = pl.BlockSpec((step, 1), lambda t: (t, 0))
    count = len(weights)
    args = [parts, gain[:, None], *weights]
    in_specs = [pl.BlockSpec((groups, step, size), lambda t: (0, t, 0)), thin] + [row_block] * count
    out_shape = [shape((rows, columns), f32)] * count + [shape((rows, 1), f32)]
    out_specs = [row_block] * count + [thin]
    if down_rows:
        share, feats = groups // STEPS, downs.shape[2]
        args.append(downs)
        in_specs.append(
            pl.BlockSpec((share, down_rows, feats), lambda t: (t, begin // down_rows, 0))
        )
        out_shape.append(shape((groups, down_rows, feats), f32))
        out_specs.append(pl.BlockSpec((share, down_rows, feats), lambda t: (t, 0, 0)))
    outs = pl.pallas_call(
        functools.partial(
            assemble_kernel, kinds=count, shards=shards, with_down=bool(down_rows)
        ),
        grid=(STEPS,),
        out_shape=out_shape,
        in_specs=in_specs,
        out_specs=out_specs,
        compiler_params=LIMIT,
        name="assemble",
    )(*args)
    return outs[:count], outs[count][:, 0], outs[count + 1 :]


def per_device(
    inputs, w_query, w_key, w_value, w_out, w_gate, w_up, w_down,
    gain_attn, gain_ffn, segments, deal_order, cotangent,
):
    rows, seqs, feats = inputs.shape
    chips = lax.axis_size("chip")
    groups = 2 * chips
    shards = lax.axis_size("fsdp")
    chip = lax.axis_index("chip")
    core = lax.axis_index("core")
    rank = chip * 2 + core
    width = feats // groups
    hidden_width = w_gate.shape[1] // groups
    per_shard = hidden_width // shards
    seq_len = rows * groups
    blocks = deal_order.shape[0]
    blk = rows // 2
    tokens = chips * rows

    def take(weight, axis, index, size):
        return lax.dynamic_slice_in_dim(weight, index * size, size, axis)

    x_zero, x_one = [inputs[:, b] for b in range(seqs)]
    x_spread = jnp.broadcast_to(x_zero, (chips,) + x_zero.shape)
    near_zero = exchange(x_spread)
    w_query, w_key, w_value, w_out, w_gate, w_up, w_down, segments, deal_order = hold(
        (w_query, w_key, w_value, w_out, w_gate, w_up, w_down, segments, deal_order), x_spread
    )

    ids = jnp.stack([core, lax.axis_index("fsdp"), chip]).astype(jnp.int32)
    pair = jnp.arange(2, dtype=jnp.int32)
    rel_dev = (jnp.arange(chips, dtype=jnp.int32)[None, :] * 2) + (pair[:, None] ^ core)
    rel_slot = (rel_dev[:, :, None] * 2 + pair[None, None, :]).reshape(-1)
    near_chips = jnp.arange(chips, dtype=jnp.int32) ^ chip
    send_dev = near_chips[:, None] * 2 + (pair[None, :] ^ core)
    send_slot = (send_dev[:, :, None] * 2 + pair[None, None, :]).reshape(-1)
    spots = jnp.arange(blocks, dtype=jnp.int32)

    def look_up(slots):
        return jnp.sum(
            jnp.where(slots[:, None] == spots[None, :], deal_order[None, :], 0), axis=1
        ).astype(jnp.int32)

    rel_table = look_up(rel_slot)
    send_table = look_up(send_slot)
    earlier = (segments[None, :, :] < segments[:, None, :]).astype(jnp.int32)
    slot_start = jnp.sum(earlier, axis=1).astype(jnp.int32).reshape(blocks, blk, seqs)
    start = jnp.sum(
        jnp.where((deal_order[None, :] == spots[:, None])[:, :, None, None], slot_start[None], 0),
        axis=1,
    ).astype(jnp.int32)
    start = start.transpose(2, 0, 1).reshape(seqs, seq_len)

    def ranges(q_rows, k_rows):
        tiled = start.reshape(seqs, seq_len // q_rows, q_rows)
        begins = jnp.arange(seq_len // q_rows, dtype=jnp.int32) * q_rows // k_rows
        first = tiled[:, :, 0] // k_rows
        full = jnp.minimum(begins[None, :], (tiled[:, :, -1] + k_rows - 1) // k_rows)
        return tiled, first, full

    _, first, full = ranges(Q_FORE, K_FORE)
    tiled, first_back, full_back = ranges(Q_BACK, K_BACK)

    both = jnp.stack([gain_attn, gain_ffn], axis=1)
    spare = jnp.zeros((both.shape[0], -(3 * width + 2) % 128), bf16)
    own_qkv = jnp.concatenate(
        [take(w, 1, rank, width) for w in (w_query, w_key, w_value)] + [both, spare], axis=1
    )

    def hidden_columns(weight):
        return [take(weight, 1, rank + z * groups, per_shard) for z in range(shards)]

    own_gate_up = jnp.concatenate(hidden_columns(w_gate) + hidden_columns(w_up), axis=1)
    own_down = take(w_down, 0, rank, per_shard)
    out_grid = w_out.reshape(-1, 2, width, feats)
    own_out = take(out_grid, 1, core, 1).reshape(-1, feats)

    merged = 2 * hidden_width == feats
    if merged:
        ffn_own = [jnp.concatenate([own_gate_up, own_down])]
    else:
        ffn_own = [own_gate_up, own_down]
    qkv_pieces = shard_pieces(own_qkv)
    x_spread_one = jnp.broadcast_to(x_one, (chips,) + x_one.shape)
    cot_all = [cotangent[:, b] for b in range(seqs)]
    (
        near_zero, qkv_pieces, start, tiled, first, full, first_back, full_back, rel_table, send_table,
        x_spread_one, cot_all, own_out, ffn_own,
    ) = hold(
        (
            near_zero, qkv_pieces, start, tiled, first, full, first_back, full_back, rel_table, send_table,
            x_spread_one, cot_all, own_out, ffn_own,
        )
    )
    qkv = in_order(qkv_pieces, ids[1])
    gain_one, gain_two = qkv[:, 3 * width][None, :], qkv[:, 3 * width + 1][None, :]
    def flat(*pair):
        return [value.reshape(tokens, feats) for value in pair]

    def by_chip(value):
        return value.reshape(chips, rows, feats)

    def spread_cot(own):
        return lax.all_gather(own, PLANE, axis=0).reshape(chips, 2, rows, feats)

    tables = [(rel_table, send_table, first[b], full[b]) for b in range(seqs)]
    tables_back = [(rel_table, send_table, first_back[b], full_back[b]) for b in range(seqs)]

    def forward(b, near, far):
        query, key, value, normed, fine, logsum, *sent = attend_forward(
            tables[b], *flat(near, far), qkv, gain_one, start[b][:, None], width, chips
        )
        return (query, key, value, fine, logsum), normed, sent

    def mid_norm(x_own, own, swapped):
        middle = x_own.astype(f32) + own + swapped
        return middle, (middle * row_scale(middle) * gain_two.astype(f32)).astype(bf16)

    near_one = exchange(x_spread_one)
    out_pieces = shard_pieces(own_out)
    ffn_pieces = [lax.all_gather(value, "fsdp", axis=0) for value in ffn_own]
    saved_zero, normed_zero, sent_zero = forward(0, near_zero, swap_core(near_zero))
    near_one, sent_zero, out_pieces, cot_zero, cot_one = hold(
        (near_one, sent_zero, out_pieces, cot_all[0], cot_all[1])
    )
    near_cot = spread(cot_zero)
    got_zero = exchange_pieces(sent_zero)
    saved_one, normed_one, sent_one = forward(1, near_one, swap_core(near_one))
    got_zero, sent_one, near_cot = hold((got_zero, sent_one, near_cot))
    got_one = exchange_pieces(sent_one)
    att_zero, own, other = mix(ids, got_zero, out_pieces)
    mid_zero, norm_zero = mid_norm(x_zero, own, swap_core(other))
    norm_zero, got_one = hold((norm_zero, got_one))
    near_zero = spread(norm_zero)
    att_one, own, other = mix(ids, hold(got_one, near_zero), out_pieces)
    mid_one, norm_one = mid_norm(x_one, own, swap_core(other))
    near_one = spread(norm_one)
    cots = (flat(near_cot, swap_core(near_cot)), [spread_cot(hold(cot_one, near_zero))])

    def ffn(b, near, far, split):
        mids = flat(near, far)
        *out_part, mid_near, mid_far, hidden, grad_pre = feed_forward(
            ids, mids, cots[b], ffn_pieces, hidden_width, split
        )
        return out_part, by_chip(mid_near), by_chip(mid_far), (*mids, hidden, grad_pre, *cots[b])

    out_zero, own_zero, far_zero, stream_zero = ffn(0, near_zero, swap_core(near_zero), False)
    near_one = hold(near_one, stream_zero[2])
    total_zero = core_sum(own_zero, swap_core(far_zero))
    near_far = hold((near_one, swap_core(near_one)), total_zero)
    out_one, own_one, far_one, stream_one = ffn(1, *near_far, True)
    sums_zero = hold(exchange(total_zero), stream_one[2])
    far_one = swap_core(far_one)
    ffn_sums = weight_sums(ids, (stream_zero, stream_one), shards)
    shares = [lax.psum_scatter(value, "fsdp", scatter_dimension=0) for value in ffn_sums]
    sums_zero, far_one = hold((sums_zero, far_one), ffn_sums[0])
    total_one = core_sum(own_one, far_one)

    out_sum_zero = lax.psum_scatter(
        out_zero[0].reshape(groups * rows, feats), PLANE, scatter_dimension=0, tiled=True
    )

    def mid_backward(b, grad_normed_mid, middle):
        scale_two = row_scale(middle)
        unit_two = middle * scale_two
        scaled_two = grad_normed_mid * gain_two.astype(f32)
        grad_middle = cot_all[b].astype(f32) + scale_two * (
            scaled_two - unit_two * jnp.mean(scaled_two * unit_two, axis=-1, keepdims=True)
        )
        return grad_middle, grad_middle.astype(bf16)

    def backward(b, saved, grad_got):
        return attend_backward(
            tables_back[b], saved, grad_got, qkv, tiled[b][:, None, :]
        )

    def qkv_stream(normed, grads):
        return normed.reshape(seq_len, feats), grads.reshape(seq_len, 3 * width)

    def in_backward(grad_normed_in, grad_middle, x_own):
        flat_in = x_own.astype(f32)
        scale_one = row_scale(flat_in)
        unit_one = flat_in * scale_one
        scaled_one = grad_normed_in * gain_one.astype(f32)
        return (
            grad_middle
            + scale_one
            * (scaled_one - unit_one * jnp.mean(scaled_one * unit_one, axis=-1, keepdims=True))
        ).astype(bf16)

    grad_mid_zero, branch = mid_backward(0, last_sum(sums_zero), mid_zero)
    grad_sent, grad_out_zero = unmix(ids, branch, swap_core(branch), att_zero, out_pieces, chips)
    total_one = hold(total_one, grad_sent)
    grad_got_zero = hold(exchange_pieces(grad_sent), out_sum_zero)
    sums_one = exchange(total_one)
    part_near, part_far, grads_zero = backward(0, saved_zero, grad_got_zero)
    sums_one = hold(sums_one, grads_zero)
    far_swapped = swap_core(by_chip(part_far))
    grad_mid_one, branch = mid_backward(1, last_sum(sums_one), mid_one)
    grad_sent, grad_out_one = unmix(ids, branch, swap_core(branch), att_one, out_pieces, chips)
    grad_got_one = exchange_pieces(grad_sent)
    far_swapped = hold(far_swapped, grad_sent)
    total_zero = core_sum(by_chip(part_near), far_swapped)
    sums_zero = exchange(total_zero)

    own_rows = feats // shards

    def rel_rows(value):
        value = value.astype(bf16)
        count = value.shape[0] // shards
        return [take(value, 0, ids[1] ^ r, count) for r in range(shards)]

    out_rel = rel_rows(grad_out_zero + grad_out_one)
    out_sent = send_pieces(out_rel)
    grad_got_one, shares = hold((grad_got_one, shares), total_zero)
    full_ffn = [lax.all_gather(share, PLANE, axis=0) for share in shares]
    part_near, part_far, grads_one = backward(1, saved_one, grad_got_one)
    part_near, part_far, grads_one, sums_zero, out_sent = hold(
        (part_near, part_far, grads_one, sums_zero, out_sent)
    )
    total_one = core_sum(by_chip(part_near), swap_core(by_chip(part_far)))
    qkv_one = qkv_first(*qkv_stream(normed_one, grads_one))
    total_one, qkv_one, grads_zero = hold((total_one, qkv_one, grads_zero))
    sums_one = exchange(total_one)
    grad_qkv = qkv_sums(ids, *qkv_stream(normed_zero, grads_zero), qkv_one, shards)
    own_rows = feats // shards
    g_gate_up, g_gain_two, (g_down,) = assemble(
        full_ffn[0],
        gain_ffn,
        (w_gate, w_up),
        shards,
        full_ffn[-1],
        own_rows if merged else 0,
        per_shard,
    )
    g_down = g_down.reshape(-1, feats)
    sums_one, g_gate_up, g_gain_two, g_down = hold((sums_one, g_gate_up, g_gain_two, g_down))
    out_near, out_far = [by_chip(part) for part in out_one]
    total_out = core_sum(out_near, swap_core(out_far))
    share_qkv = add_pieces(grad_qkv[0], send_pieces(grad_qkv))
    near_qkv = spread(hold(share_qkv, sums_one))
    sums_out = exchange(hold(total_out, near_qkv))
    share_out = lax.all_gather(add_pieces(out_rel[0], out_sent), PLANE, axis=0)
    share_out = share_out.astype(f32)

    outputs = [
        (mid_zero + out_sum_zero.astype(f32)).astype(bf16),
        (mid_one + last_sum(sums_out)).astype(bf16),
    ]
    grad_inputs = [
        in_backward(last_sum(sums_zero), grad_mid_zero, x_zero),
        in_backward(last_sum(sums_one), grad_mid_one, x_one),
    ]
    far_qkv = swap_core(near_qkv)
    full_qkv = jnp.stack(
        [jnp.where(core == 0, near_qkv, far_qkv), jnp.where(core == 0, far_qkv, near_qkv)], axis=1
    )
    full_qkv = full_qkv.reshape(groups, own_rows, 3 * width)
    g_qkv, g_gain_one, _ = assemble(full_qkv, gain_attn, (w_query, w_key, w_value), 1)
    share_out = share_out.reshape(chips, 2, -1, width, feats)
    g_out = jnp.sum(share_out, axis=0).transpose(1, 0, 2, 3).reshape(own_rows, feats)

    return (
        jnp.stack(outputs, axis=1),
        jnp.stack(grad_inputs, axis=1),
        *g_qkv,
        g_out,
        *g_gate_up,
        g_down,
        g_gain_one,
        g_gain_two,
    )


def solution(mesh):
    names = mesh.axis_names
    ctx, shards = mesh.shape[names[0]], mesh.shape[names[1]]
    fine_mesh = Mesh(mesh.devices.reshape(ctx // 2, 2, shards), ("chip", "core", "fsdp"))
    by_row = P("fsdp", None)
    by_token = P(PLANE, "fsdp", None)
    return jax.shard_map(
        per_device,
        mesh=fine_mesh,
        in_specs=(by_token,) + (by_row,) * 7 + (P("fsdp"), P("fsdp"), P(None, "fsdp"), P(), by_token),
        out_specs=(by_token, by_token) + (by_row,) * 7 + (P("fsdp"), P("fsdp")),
        check_vma=False,
    )
```

```python
import functools

import jax
import jax.numpy as jnp
from jax import lax
from jax.experimental import pallas as pl
from jax.experimental.pallas import tpu as pltpu
from jax.sharding import Mesh, PartitionSpec as P

HEAD_DIM = 64
EPSILON = 1e-05
MASKED = -1e30
TILE = 256
PROJ = 512
Q_FORE, K_FORE = 512, 512
Q_BACK, K_BACK = 512, 512
PLANE = ("chip", "core")

bf16 = jnp.bfloat16
f32 = jnp.float32


def dot_nn(left_op, right_op):
    return lax.dot_general(left_op, right_op, (((1,), (0,)), ((), ())), preferred_element_type=f32)


def dot_nt(left_op, right_op):
    return lax.dot_general(left_op, right_op, (((1,), (1,)), ((), ())), preferred_element_type=f32)


def dot_tn(left_op, right_op):
    return lax.dot_general(left_op, right_op, (((0,), (0,)), ((), ())), preferred_element_type=f32)


def row_scale(values):
    return lax.rsqrt(jnp.mean(values * values, axis=-1, keepdims=True) + EPSILON)


def swap_core(value):
    return lax.ppermute(value, "core", [(0, 1), (1, 0)])


def swap_chip(value, mask):
    count = lax.axis_size("chip")
    return lax.ppermute(value, "chip", [(i, i ^ mask) for i in range(count)])


def swap_shard(value, mask):
    count = lax.axis_size("fsdp")
    return lax.ppermute(value, "fsdp", [(i, i ^ mask) for i in range(count)])


def hold(value, *deps):
    return lax.optimization_barrier((value, deps))[0]


def spread(value):
    count = lax.axis_size("chip")
    return exchange(jnp.broadcast_to(value, (count,) + value.shape))


def exchange(value):
    return lax.all_to_all(value, "chip", 0, 0)


def arrange_kernel(ids, *refs):
    out = refs[-1]
    for r, piece in enumerate(refs[:-1]):
        out[ids[2] ^ r] = piece[...]


def arrange(ids, pieces):
    return pl.pallas_call(
        arrange_kernel,
        out_shape=jax.ShapeDtypeStruct((len(pieces),) + pieces[0].shape, bf16),
        in_specs=[smem()] + [vmem()] * len(pieces),
        out_specs=vmem(),
        compiler_params=LIMIT,
        cost_estimate=cost(3),
        name="arrange",
    )(ids, *pieces)


def send_copies(value):
    return exchange_pieces([value] * lax.axis_size("chip"))


def add_kernel(own, other, total):
    total[...] = (own[...].astype(f32) + other[...].astype(f32)).astype(bf16)


def exchange_pieces(pieces):
    return [pieces[0]] + [swap_chip(pieces[r], r) for r in range(1, len(pieces))]


def core_sum(own, swapped):
    chips, rows, width = own.shape
    block = pl.BlockSpec((chips // 2, rows, width), lambda t: (t, 0, 0))
    return pl.pallas_call(
        add_kernel,
        grid=(2,),
        out_shape=jax.ShapeDtypeStruct(own.shape, bf16),
        in_specs=[block, block],
        out_specs=block,
        cost_estimate=cost(3),
        name="core_sum",
    )(own, swapped)


def last_sum(value):
    return jnp.sum(value.astype(f32), axis=0)


def shard_pieces(value):
    return [value] + [swap_shard(value, r) for r in range(1, lax.axis_size("fsdp"))]


def shard_sum(pieces):
    return add_pieces(pieces[0], send_pieces(pieces))


def in_order(pieces, shard):
    stacked = jnp.stack(pieces)
    rows = [lax.dynamic_index_in_dim(stacked, shard ^ z, keepdims=False) for z in range(len(pieces))]
    return jnp.concatenate(rows)


def send_pieces(pieces):
    return [swap_shard(pieces[r], r) for r in range(1, len(pieces))]


def add_pieces(own, received):
    total = own.astype(f32)
    for piece in received:
        total = total + piece.astype(f32)
    return total.astype(bf16)


def head_masks(rows, width):
    lanes = lax.broadcasted_iota(jnp.int32, (rows, width), 1) // HEAD_DIM
    return [lanes == h for h in range(width // HEAD_DIM)]


def stack_heads(values, masks):
    zero = jnp.zeros_like(values)
    return jnp.concatenate([jnp.where(mask, values, zero) for mask in masks], axis=0)


def merge_heads(stacked, masks, rows):
    merged = stacked[:rows]
    for h in range(1, len(masks)):
        merged = jnp.where(masks[h], stacked[h * rows : (h + 1) * rows], merged)
    return merged


def forward_kernel(
    rel, send, first, full, x_near, x_far, weight, gain, start,
    query_out, key_out, value_out, normed, fine_out, logsum_out, *refs,
):
    attended, refs = refs[:-13], refs[-13:]
    query, key, value, fine, logsum, x_tiles, normed_tiles, scores, top, total = refs[:10]
    in_sems, normed_sems, out_sems = refs[10:]
    width = query.shape[1]
    seq_len = query.shape[0]
    heads = width // HEAD_DIM
    blk = TILE // 2
    tiles = x_near.shape[0] // PROJ
    blocks = PROJ // blk
    gain_row = gain[...].astype(f32)
    loads, stores = [], []
    for i in range(2 * tiles):
        rows = pl.ds(i % tiles * PROJ, PROJ)
        source = x_near if i < tiles else x_far
        loads.append(pltpu.make_async_copy(source.at[rows], x_tiles.at[i], in_sems.at[i]))
        stores.append(
            pltpu.make_async_copy(
                normed_tiles.at[i], normed.at[i // tiles, rows], normed_sems.at[i]
            )
        )
        loads[i].start()
    for i in range(2 * tiles):
        loads[i].wait()
        rows_in = x_tiles[i].astype(f32)
        tile = (rows_in * row_scale(rows_in) * gain_row).astype(bf16)
        normed_tiles[i] = tile
        stores[i].start()
        mixed = dot_nn(tile, weight[:, : 3 * width])
        for h in range(blocks):
            where = pl.ds(pl.multiple_of(rel[i * blocks + h] * blk, blk), blk)
            part = mixed[h * blk : (h + 1) * blk]
            query[where, :] = (part[:, :width].astype(bf16) * 0.125).astype(bf16)
            key[where, :] = part[:, width : 2 * width].astype(bf16)
            value[where, :] = part[:, 2 * width :].astype(bf16)
    for i, (source, target) in enumerate(
        ((query, query_out), (key, key_out), (value, value_out))
    ):
        stores.append(pltpu.make_async_copy(source, target, out_sems.at[i]))
        stores[-1].start()

    masks = head_masks(Q_FORE, width)
    big = heads * Q_FORE

    def query_tile(qb, _):
        rows = pl.ds(pl.multiple_of(qb * Q_FORE, Q_FORE), Q_FORE)
        stacked = stack_heads(query[rows, :], masks)
        top[...] = jnp.full_like(top, MASKED)
        begin = jnp.concatenate([start[rows, :]] * heads, axis=0)
        diagonal = qb * Q_FORE // K_FORE
        last = (qb * Q_FORE + Q_FORE + K_FORE - 1) // K_FORE

        def score(kb, masked):
            keys = key[pl.ds(pl.multiple_of(kb * K_FORE, K_FORE), K_FORE), :]
            raw = dot_nt(stacked, keys)
            if masked:
                k_pos = kb * K_FORE + lax.broadcasted_iota(jnp.int32, (big, K_FORE), 1)
                q_row = lax.broadcasted_iota(jnp.int32, (big, K_FORE), 0) & (Q_FORE - 1)
                allowed = (k_pos >= begin) & (k_pos <= qb * Q_FORE + q_row)
                raw = jnp.where(allowed, raw, MASKED)
            scores[kb] = raw
            best = raw[:, :128]
            for c in range(1, K_FORE // 128):
                best = jnp.maximum(best, raw[:, c * 128 : (c + 1) * 128])
            top[...] = jnp.maximum(top[...], best)

        def masked_step(kb, _):
            score(kb, True)
            return 0

        def plain_step(kb, _):
            score(kb, False)
            return 0

        lax.fori_loop(first[qb], full[qb], masked_step, 0)
        lax.fori_loop(full[qb], diagonal, plain_step, 0)
        lax.fori_loop(diagonal, last, masked_step, 0)
        peak = jnp.max(top[...], axis=1, keepdims=True)
        top[...] = jnp.broadcast_to(peak, top.shape)
        total[...] = jnp.zeros_like(total)

        def weigh(kb, carry):
            vals = value[pl.ds(pl.multiple_of(kb * K_FORE, K_FORE), K_FORE), :]
            pieces = []
            summed = total[...]
            for c in range(K_FORE // 128):
                piece = jnp.exp(scores[kb, :, c * 128 : (c + 1) * 128] - top[...])
                summed = summed + piece
                pieces.append(piece.astype(bf16))
            total[...] = summed
            return carry + dot_nn(jnp.concatenate(pieces, axis=1), vals)

        gathered = lax.fori_loop(first[qb], last, weigh, jnp.zeros((big, width), f32))
        denom = jnp.sum(total[...], axis=1, keepdims=True)
        fine[rows, :] = merge_heads(gathered / denom, masks, Q_FORE)
        logs = jnp.broadcast_to(peak + jnp.log(denom), (big, width))
        logsum[rows, :] = merge_heads(logs, masks, Q_FORE)
        return 0

    lax.fori_loop(0, seq_len // Q_FORE, query_tile, 0)
    for i, (source, target) in enumerate(((fine, fine_out), (logsum, logsum_out))):
        stores.append(pltpu.make_async_copy(source, target, out_sems.at[3 + i]))
        stores[-1].start()

    count = seq_len // blk // len(attended)
    for r, piece in enumerate(attended):
        for j in range(count):
            where = pl.ds(pl.multiple_of(send[r * count + j] * blk, blk), blk)
            piece[j * blk : (j + 1) * blk, :] = fine[where, :].astype(bf16)
    for copy in stores:
        copy.wait()


def backward_kernel(
    rel, send, first, full, query, key, value, fine, logsum, weight, start, *refs
):
    grad_in, refs = refs[:-13], refs[-13:]
    part_near, part_far, grads_out, grad_at, grad_q, grad_k, grad_v, grad_q2 = refs[:8]
    parts, grads, local_weight, sems, weight_sem = refs[8:]
    load = pltpu.make_async_copy(weight, local_weight, weight_sem)
    load.start()
    seq_len, width = query.shape
    heads = width // HEAD_DIM
    blk = TILE // 2
    big = heads * Q_BACK

    count = seq_len // blk // len(grad_in)
    for r, piece in enumerate(grad_in):
        for j in range(count):
            where = pl.ds(pl.multiple_of(send[r * count + j] * blk, blk), blk)
            grad_at[where, :] = piece[j * blk : (j + 1) * blk, :]
    grad_k[...] = jnp.zeros_like(grad_k)
    grad_v[...] = jnp.zeros_like(grad_v)
    masks = head_masks(Q_BACK, width)

    def flip(values):
        if width < 128:
            values = jnp.concatenate([values, jnp.zeros((Q_BACK, 128 - width), f32)], axis=1)
        return values.T

    def query_tile(qb, _):
        rows = pl.ds(pl.multiple_of(qb * Q_BACK, Q_BACK), Q_BACK)
        stacked = stack_heads(query[rows, :], masks)
        grad_rows = grad_at[rows, :]
        grad_stacked = stack_heads(grad_rows, masks)
        products = flip(grad_rows.astype(f32) * fine[rows, :])
        logs = flip(logsum[rows, :])
        delta = jnp.concatenate(
            [
                jnp.sum(products[h * HEAD_DIM : (h + 1) * HEAD_DIM], axis=0, keepdims=True)
                for h in range(heads)
            ],
            axis=1,
        )
        log_row = jnp.concatenate(
            [logs[h * HEAD_DIM : h * HEAD_DIM + 1] for h in range(heads)], axis=1
        )
        begin = jnp.concatenate([start[qb]] * heads, axis=1)
        grad_q2[...] = jnp.zeros_like(grad_q2)
        diagonal = qb * Q_BACK // K_BACK
        last = (qb * Q_BACK + Q_BACK + K_BACK - 1) // K_BACK

        def step(kb, masked):
            where = pl.ds(pl.multiple_of(kb * K_BACK, K_BACK), K_BACK)
            keys = key[where, :]
            probs = jnp.exp(dot_nt(keys, stacked) - log_row)
            if masked:
                k_pos = kb * K_BACK + lax.broadcasted_iota(jnp.int32, (K_BACK, big), 0)
                q_row = lax.broadcasted_iota(jnp.int32, (K_BACK, big), 1) & (Q_BACK - 1)
                allowed = (k_pos >= begin) & (k_pos <= qb * Q_BACK + q_row)
                probs = jnp.where(allowed, probs, 0.0)
            slope = (probs * (dot_nt(value[where, :], grad_stacked) - delta)).astype(bf16)
            grad_v[where, :] += dot_nn(probs.astype(bf16), grad_stacked)
            grad_k[where, :] += dot_nn(slope, stacked)
            grad_q2[...] += dot_tn(slope, keys)

        def masked_step(kb, _):
            step(kb, True)
            return 0

        def plain_step(kb, _):
            step(kb, False)
            return 0

        lax.fori_loop(first[qb], full[qb], masked_step, 0)
        lax.fori_loop(full[qb], diagonal, plain_step, 0)
        lax.fori_loop(diagonal, last, masked_step, 0)
        grad_q[rows, :] = (merge_heads(grad_q2[...], masks, Q_BACK) * 0.125).astype(bf16)
        return 0

    lax.fori_loop(0, seq_len // Q_BACK, query_tile, 0)

    tiles = seq_len // PROJ // 2
    blocks = PROJ // blk
    load.wait()
    stores = []
    for i in range(2 * tiles):
        rows = pl.ds(i % tiles * PROJ, PROJ)
        for h in range(blocks):
            where = pl.ds(pl.multiple_of(rel[i * blocks + h] * blk, blk), blk)
            here = pl.ds(h * blk, blk)
            grads[i, here, :width] = grad_q[where, :]
            grads[i, here, width : 2 * width] = grad_k[where, :].astype(bf16)
            grads[i, here, 2 * width :] = grad_v[where, :].astype(bf16)
        target = grads_out.at[i // tiles, rows]
        stores.append(pltpu.make_async_copy(grads.at[i], target, sems.at[0, i]))
        stores[-1].start()
        parts[i] = dot_nt(grads[i], local_weight[:, : 3 * width]).astype(bf16)
        target = (part_near if i < tiles else part_far).at[rows]
        stores.append(pltpu.make_async_copy(parts.at[i], target, sems.at[1, i]))
        stores[-1].start()
    for copy in stores:
        copy.wait()


def place_pieces(target, pieces, shard, begin, count):
    for r, piece in enumerate(pieces):
        at = pl.multiple_of((shard ^ r) * count, count)
        target[pl.ds(at, count), :] = piece[begin : begin + count, :]


def near_first(target, source, chip, count):
    for r in range(count):
        rows = target.shape[0] // count
        at = pl.multiple_of((chip ^ r) * rows, rows)
        target[r * rows : (r + 1) * rows, :] = source[pl.ds(at, rows), :]


def mix_kernel(ids, *refs, chips):
    got, pieces, (attended, own, other, whole, weight) = refs[:chips], refs[chips:-5], refs[-5:]
    rows = own.shape[0]
    place_pieces(whole, pieces, ids[1], 0, pieces[0].shape[0])
    near_first(weight, whole, ids[2], chips)
    joined = jnp.concatenate([piece[...] for piece in got], axis=1)
    attended[...] = joined
    own[...] = dot_nn(joined[:rows], weight[...])
    other[...] = dot_nn(joined[rows:], weight[...])


def unmix_kernel(ids, own, other, attended, *refs, chips):
    outs = chips + 3
    pieces, grad_sent, (grad_weight, whole, weight) = refs[:-outs], refs[-outs:-3], refs[-3:]
    place_pieces(whole, pieces, ids[1], 0, pieces[0].shape[0])
    near_first(weight, whole, ids[2], chips)
    branch = jnp.concatenate([own[...], other[...]], axis=0)
    mixed = dot_nt(branch, weight[...]).astype(bf16)
    sums = dot_tn(attended[...], branch)
    width = grad_sent[0].shape[1]
    for r in range(chips):
        grad_sent[r][...] = mixed[:, r * width : (r + 1) * width]
        at = pl.multiple_of((ids[2] ^ r) * width, width)
        grad_weight[pl.ds(at, width), :] = sums[r * width : (r + 1) * width]


def qkv_kernel(ids, *refs):
    normed, grads, before = refs[:3]
    outs, total = refs[3:-1], refs[-1]
    t = pl.program_id(0)

    @pl.when(t == 0)
    def _():
        total[...] = before[...]

    total[...] += dot_tn(normed[...], grads[...])

    @pl.when(t == pl.num_programs(0) - 1)
    def _():
        rows = outs[0].shape[0]
        for r, out in enumerate(outs):
            at = pl.multiple_of((ids[1] ^ r) * rows, rows)
            out[...] = total[pl.ds(at, rows), :].astype(bf16)


def ffn_kernel(ids, x_near, x_far, *refs, split, sides):
    cot_refs, refs = refs[:sides], refs[sides:]
    outs = 7 + split
    pieces, out_parts = refs[:-outs], refs[-outs : 1 + split - outs]
    mid_near, mid_far, hidden, grad_pre, gate_up, down = refs[-6:]
    t = pl.program_id(0)
    half = pl.num_programs(0) // 2
    feats, size = gate_up.shape[0], gate_up.shape[1] // 2
    shards = pieces[0].shape[0]
    rows, more = feats // shards, size // shards
    begin = rows if len(pieces) == 1 else 0

    @pl.when(t == 0)
    def _():
        for z in range(shards):
            gate_up[z * rows : (z + 1) * rows, :] = pieces[0][z, :rows, :]
            down[z * more : (z + 1) * more, :] = pieces[-1][z, begin : begin + more, :]

    tile = jnp.where(t < half, x_near[...], x_far[...])
    cot = cot_refs[0][...].reshape(tile.shape)
    if sides == 2:
        cot = jnp.where(t < half, cot, cot_refs[1][...])
    pre = dot_nn(tile, gate_up[...])
    gate_pre, up_pre = pre[:, :size], pre[:, size:]
    sigma = jax.nn.sigmoid(gate_pre)
    active = gate_pre * sigma
    low = (active * up_pre).astype(bf16)
    grad_hidden = dot_nt(cot, down[...])
    hidden[...] = low
    out_part = dot_nn(low, down[...]).astype(bf16)
    grad_gate = grad_hidden * up_pre * sigma * (1.0 + gate_pre * (1.0 - sigma))
    grad_up = grad_hidden * active
    grads = jnp.concatenate([grad_gate.astype(bf16), grad_up.astype(bf16)], axis=1)
    grad_pre[...] = grads
    mid_part = dot_nt(grads, gate_up[...]).astype(bf16)

    if not split:
        out_parts[0][...] = out_part.reshape(out_parts[0].shape)

    @pl.when(t < half)
    def _():
        mid_near[...] = mid_part
        if split:
            out_parts[0][...] = out_part

    @pl.when(t >= half)
    def _():
        mid_far[...] = mid_part
        if split:
            out_parts[1][...] = out_part


def weight_kernel(ids, *refs, counts, shards):
    streams = len(counts)
    ins, outs, (wide, down) = refs[: sum(counts)], refs[sum(counts) : -2], refs[-2:]
    t = pl.program_id(0)
    per = pl.num_programs(0) // streams

    @pl.when(t == 0)
    def _():
        wide[...] = jnp.zeros_like(wide)
        down[...] = jnp.zeros_like(down)

    for b in range(streams):
        mine = ins[sum(counts[:b]) : sum(counts[: b + 1])]

        @pl.when((t >= b * per) & (t < (b + 1) * per))
        def _(b=b, mine=mine):
            x_near, x_far, hidden, grad_pre = mine[:4]
            near = t < b * per + per // 2
            tile = jnp.where(near, x_near[...], x_far[...])
            cot = mine[4][...].reshape(tile.shape)
            if len(mine) == 6:
                cot = jnp.where(near, cot, mine[5][...])
            wide[...] += dot_tn(tile, grad_pre[...])
            down[...] += dot_tn(hidden[...], cot)

    @pl.when(t == pl.num_programs(0) - 1)
    def _():
        rows, more = wide.shape[0] // shards, down.shape[0] // shards
        begin = rows if len(outs) == 1 else 0
        for z in range(shards):
            outs[0][z, :rows, :] = wide[z * rows : (z + 1) * rows, :].astype(bf16)
            piece = down[z * more : (z + 1) * more, :]
            outs[-1][z, begin : begin + more, :] = piece.astype(bf16)


def assemble_kernel(*refs, kinds, shards, with_down, sides):
    sources, gain = refs[:sides], refs[sides]
    if sides == 1:
        parts = sources[0]
    else:
        ids, near, far = sources
        parts = []
        for p in range(near.shape[0]):
            own, other = near[p], far[p]
            parts.append(jnp.where(ids[0] == 0, own, other))
            parts.append(jnp.where(ids[0] == 0, other, own))
    refs = refs[sides - 1 :]
    weights = refs[2 : 2 + kinds]
    rest = refs[2 + kinds :]
    if with_down:
        down_part, rest = rest[0], rest[1:]
    outs, gain_out = rest[:kinds], rest[kinds]
    groups = len(parts) if sides > 1 else parts.shape[0]
    size = sources[-1].shape[2]
    pieces = size // kinds
    lanes = pieces // shards
    sums = 0.0
    for k in range(kinds):
        columns = []
        for z in range(shards):
            for i in range(groups):
                at = k * pieces + z * lanes
                columns.append(parts[i][:, at : at + lanes].astype(f32))
        full = jnp.concatenate(columns, axis=1)
        outs[k][...] = full
        sums = sums + jnp.sum(full * weights[k][...].astype(f32), axis=1, keepdims=True)
    gain_out[...] = sums / gain[...].astype(f32)
    if with_down:
        rest[kinds + 1][...] = down_part[...].astype(f32)


def smem():
    return pl.BlockSpec(memory_space=pltpu.SMEM)


def hbm():
    return pl.BlockSpec(memory_space=pl.ANY)


def vmem():
    return pl.BlockSpec(memory_space=pltpu.VMEM)


def cost(micros):
    return pl.CostEstimate(flops=micros * 10**9, bytes_accessed=2**20, transcendentals=0)


LIMIT = pltpu.CompilerParams(vmem_limit_bytes=56 * 2**20)


def attend_forward(tables, x_near, x_far, weight, gain, start, width, chips):
    half_rows, feats = x_near.shape
    seq_len = 2 * half_rows
    big = (width // HEAD_DIM) * Q_FORE
    shape = jax.ShapeDtypeStruct
    narrow = shape((seq_len, width), bf16)
    wide = shape((seq_len, width), f32)
    pairs = seq_len * seq_len * width // 2
    return pl.pallas_call(
        forward_kernel,
        out_shape=[narrow, narrow, narrow, shape((2, half_rows, feats), bf16), wide, wide]
        + [shape((seq_len // chips, width), bf16)] * chips,
        in_specs=[smem()] * 4 + [hbm()] * 2 + [vmem()] * 3,
        out_specs=[hbm()] * 6 + [vmem()] * chips,
        scratch_shapes=[
            pltpu.VMEM((seq_len, width), bf16),
            pltpu.VMEM((seq_len, width), bf16),
            pltpu.VMEM((seq_len, width), bf16),
            pltpu.VMEM((seq_len, width), f32),
            pltpu.VMEM((seq_len, width), f32),
            pltpu.VMEM((seq_len // PROJ, PROJ, feats), bf16),
            pltpu.VMEM((seq_len // PROJ, PROJ, feats), bf16),
            pltpu.VMEM((seq_len // K_FORE, big, K_FORE), f32),
            pltpu.VMEM((big, 128), f32),
            pltpu.VMEM((big, 128), f32),
            pltpu.SemaphoreType.DMA((seq_len // PROJ,)),
            pltpu.SemaphoreType.DMA((seq_len // PROJ,)),
            pltpu.SemaphoreType.DMA((5,)),
        ],
        compiler_params=LIMIT,
        cost_estimate=cost(31),
        name="attend_forward",
    )(*tables, x_near, x_far, weight, gain, start)


def attend_backward(tables, saved, grad_in, weight, start):
    query = saved[0]
    seq_len, width = query.shape
    feats = weight.shape[0]
    big = (width // HEAD_DIM) * Q_BACK
    shape = jax.ShapeDtypeStruct
    pairs = seq_len * seq_len * width // 2
    return pl.pallas_call(
        backward_kernel,
        out_shape=(
            shape((seq_len // 2, feats), bf16),
            shape((seq_len // 2, feats), bf16),
            shape((2, seq_len // 2, 3 * width), bf16),
        ),
        in_specs=[smem()] * 4 + [vmem()] * 5 + [hbm()] + [vmem()] * (1 + len(grad_in)),
        out_specs=[hbm()] * 3,
        scratch_shapes=[
            pltpu.VMEM((seq_len, width), bf16),
            pltpu.VMEM((seq_len, width), bf16),
            pltpu.VMEM((seq_len, width), f32),
            pltpu.VMEM((seq_len, width), f32),
            pltpu.VMEM((big, width), f32),
            pltpu.VMEM((seq_len // PROJ, PROJ, feats), bf16),
            pltpu.VMEM((seq_len // PROJ, PROJ, 3 * width), bf16),
            pltpu.VMEM(weight.shape, bf16),
            pltpu.SemaphoreType.DMA((2, seq_len // PROJ)),
            pltpu.SemaphoreType.DMA,
        ],
        compiler_params=LIMIT,
        cost_estimate=cost(31),
        name="attend_backward",
    )(*tables, *saved, weight, start, *grad_in)


def mix(ids, got, pieces):
    chips = len(got)
    doubled, width = got[0].shape
    feats = pieces[0].shape[1]
    size = chips * width
    shape = jax.ShapeDtypeStruct
    return pl.pallas_call(
        functools.partial(mix_kernel, chips=chips),
        out_shape=(
            shape((doubled, size), bf16),
            shape((doubled // 2, feats), f32),
            shape((doubled // 2, feats), f32),
        ),
        in_specs=[smem()] + [vmem()] * (chips + len(pieces)),
        out_specs=[vmem()] * 3,
        scratch_shapes=[pltpu.VMEM((size, feats), bf16)] * 2,
        compiler_params=LIMIT,
        cost_estimate=cost(3),
        name="mix",
    )(ids, *got, *pieces)


def unmix(ids, own, other, attended, pieces, chips):
    rows, feats = own.shape
    size = attended.shape[1]
    shape = jax.ShapeDtypeStruct
    outs = pl.pallas_call(
        functools.partial(unmix_kernel, chips=chips),
        out_shape=[shape((2 * rows, size // chips), bf16)] * chips + [shape((size, feats), f32)],
        in_specs=[smem()] + [vmem()] * (3 + len(pieces)),
        out_specs=[vmem()] * (chips + 1),
        scratch_shapes=[pltpu.VMEM((size, feats), bf16)] * 2,
        compiler_params=LIMIT,
        cost_estimate=cost(4),
        name="unmix",
    )(ids, own, other, attended, *pieces)
    return outs[:-1], outs[-1]


ROWS = 512


def feed_forward(ids, mids, cot, pieces, size, split):
    tokens, feats = mids[0].shape
    rows = ROWS // 2
    chips = tokens // rows
    half = tokens // ROWS
    shape = jax.ShapeDtypeStruct
    near = pl.BlockSpec((ROWS, feats), lambda t, ids: (jnp.minimum(t, half - 1), 0))
    far = pl.BlockSpec((ROWS, feats), lambda t, ids: (jnp.maximum(t - half, 0), 0))
    by_device = pl.BlockSpec(
        (ROWS // rows, None, rows, feats),
        lambda t, ids: (lax.rem(t, half), ids[0] ^ lax.div(t, half), 0, 0),
    )
    cot_specs = [by_device] if len(cot) == 1 else [near, far]

    def tiles(width):
        return pl.BlockSpec((ROWS, width), lambda t, ids: (t, 0))

    side = shape((tokens, feats), bf16)
    return pl.pallas_call(
        functools.partial(ffn_kernel, split=split, sides=len(cot)),
        grid_spec=pltpu.PrefetchScalarGridSpec(
            num_scalar_prefetch=1,
            grid=(2 * half,),
            in_specs=[near, far, *cot_specs]
            + [pl.BlockSpec(piece.shape, lambda t, ids: (0, 0, 0)) for piece in pieces],
            out_specs=([near, far] if split else [by_device])
            + [near, far, tiles(size), tiles(2 * size)],
            scratch_shapes=[
                pltpu.VMEM((feats, 2 * size), bf16),
                pltpu.VMEM((size, feats), bf16),
            ],
        ),
        out_shape=([side, side] if split else [shape((chips, 2, rows, feats), bf16)])
        + [
            side,
            side,
            shape((2 * tokens, size), bf16),
            shape((2 * tokens, 2 * size), bf16),
        ],
        compiler_params=LIMIT,
        cost_estimate=cost(20),
        name="feed_forward",
    )(ids, *mids, *cot, *pieces)


def weight_sums(ids, streams, shards):
    tokens, feats = streams[0][0].shape
    size = streams[0][2].shape[1]
    rows = ROWS // 2
    half = tokens // ROWS
    per = 2 * half
    shape = jax.ShapeDtypeStruct
    specs = []
    for b in range(len(streams)):

        def local(t, b=b):
            return jnp.clip(t - b * per, 0, per - 1)

        near = pl.BlockSpec(
            (ROWS, feats), lambda t, ids, f=local: (jnp.minimum(f(t), half - 1), 0)
        )
        far = pl.BlockSpec(
            (ROWS, feats), lambda t, ids, f=local: (jnp.maximum(f(t) - half, 0), 0)
        )
        by_device = pl.BlockSpec(
            (ROWS // rows, None, rows, feats),
            lambda t, ids, f=local: (lax.rem(f(t), half), ids[0] ^ lax.div(f(t), half), 0, 0),
        )
        specs += [
            near,
            far,
            pl.BlockSpec((ROWS, size), lambda t, ids, f=local: (f(t), 0)),
            pl.BlockSpec((ROWS, 2 * size), lambda t, ids, f=local: (f(t), 0)),
        ]
        specs += [by_device] if len(streams[b]) == 5 else [near, far]
    if 2 * size == feats:
        outs = [(shards, (feats + size) // shards, feats)]
    else:
        outs = [(shards, feats // shards, 2 * size), (shards, size // shards, feats)]
    return pl.pallas_call(
        functools.partial(weight_kernel, counts=[len(v) for v in streams], shards=shards),
        grid_spec=pltpu.PrefetchScalarGridSpec(
            num_scalar_prefetch=1,
            grid=(per * len(streams),),
            in_specs=specs,
            out_specs=[pl.BlockSpec(out, lambda t, ids: (0, 0, 0)) for out in outs],
            scratch_shapes=[pltpu.VMEM((feats, 2 * size), f32), pltpu.VMEM((size, feats), f32)],
        ),
        out_shape=[shape(out, bf16) for out in outs],
        compiler_params=LIMIT,
        cost_estimate=cost(23),
        name="weight_sums",
    )(ids, *[value for stream in streams for value in stream])


def qkv_first(normed, grads):
    tokens, feats = normed.shape
    size = grads.shape[1]

    def kernel(normed_ref, grads_ref, total):
        @pl.when(pl.program_id(0) == 0)
        def _():
            total[...] = jnp.zeros_like(total)

        total[...] += dot_tn(normed_ref[...], grads_ref[...])

    return pl.pallas_call(
        kernel,
        grid=(tokens // ROWS,),
        out_shape=jax.ShapeDtypeStruct((feats, size), f32),
        in_specs=[
            pl.BlockSpec((ROWS, feats), lambda t: (t, 0)),
            pl.BlockSpec((ROWS, size), lambda t: (t, 0)),
        ],
        out_specs=pl.BlockSpec((feats, size), lambda t: (0, 0)),
        compiler_params=LIMIT,
        cost_estimate=cost(6),
        name="qkv_first",
    )(normed, grads)


def qkv_sums(ids, normed, grads, before, shards):
    tokens, feats = normed.shape
    size = grads.shape[1]
    out = (feats // shards, size)
    return pl.pallas_call(
        qkv_kernel,
        grid_spec=pltpu.PrefetchScalarGridSpec(
            num_scalar_prefetch=1,
            grid=(tokens // ROWS,),
            in_specs=[
                pl.BlockSpec((ROWS, feats), lambda t, ids: (t, 0)),
                pl.BlockSpec((ROWS, size), lambda t, ids: (t, 0)),
                pl.BlockSpec((feats, size), lambda t, ids: (0, 0)),
            ],
            out_specs=[pl.BlockSpec(out, lambda t, ids: (0, 0))] * shards,
            scratch_shapes=[pltpu.VMEM((feats, size), f32)],
        ),
        out_shape=[jax.ShapeDtypeStruct(out, bf16)] * shards,
        compiler_params=LIMIT,
        cost_estimate=cost(6),
        name="qkv_sums",
    )(ids, normed, grads, before)


STEPS = 4


def assemble(parts, gain, weights, shards, downs=None, begin=0, down_rows=0):
    rows, columns = weights[0].shape
    step = rows // STEPS
    shape = jax.ShapeDtypeStruct
    sides = len(parts)
    groups, size = parts[-1].shape[0] * min(2, sides), parts[-1].shape[2]
    row_block = pl.BlockSpec((step, columns), lambda t: (t, 0))
    thin = pl.BlockSpec((step, 1), lambda t: (t, 0))
    count = len(weights)
    args = [*parts, gain[:, None], *weights]
    share_spec = pl.BlockSpec((parts[-1].shape[0], step, size), lambda t: (0, t, 0))
    in_specs = [share_spec] if sides == 1 else [smem(), share_spec, share_spec]
    in_specs += [thin] + [row_block] * count
    out_shape = [shape((rows, columns), f32)] * count + [shape((rows, 1), f32)]
    out_specs = [row_block] * count + [thin]
    if down_rows:
        share, feats = groups // STEPS, downs.shape[2]
        args.append(downs)
        in_specs.append(
            pl.BlockSpec((share, down_rows, feats), lambda t: (t, begin // down_rows, 0))
        )
        out_shape.append(shape((groups, down_rows, feats), f32))
        out_specs.append(pl.BlockSpec((share, down_rows, feats), lambda t: (t, 0, 0)))
    outs = pl.pallas_call(
        functools.partial(
            assemble_kernel, kinds=count, shards=shards, with_down=bool(down_rows), sides=sides
        ),
        grid=(STEPS,),
        out_shape=out_shape,
        in_specs=in_specs,
        out_specs=out_specs,
        compiler_params=LIMIT,
        name="assemble",
    )(*args)
    return outs[:count], outs[count][:, 0], outs[count + 1 :]


def per_device(
    inputs, w_query, w_key, w_value, w_out, w_gate, w_up, w_down,
    gain_attn, gain_ffn, segments, deal_order, cotangent,
):
    rows, seqs, feats = inputs.shape
    chips = lax.axis_size("chip")
    groups = 2 * chips
    shards = lax.axis_size("fsdp")
    chip = lax.axis_index("chip")
    core = lax.axis_index("core")
    rank = chip * 2 + core
    width = feats // groups
    hidden_width = w_gate.shape[1] // groups
    per_shard = hidden_width // shards
    seq_len = rows * groups
    blocks = deal_order.shape[0]
    blk = rows // 2
    tokens = chips * rows

    def take(weight, axis, index, size):
        return lax.dynamic_slice_in_dim(weight, index * size, size, axis)

    x_zero, x_one = [inputs[:, b] for b in range(seqs)]
    x_spread = jnp.broadcast_to(x_zero, (chips,) + x_zero.shape)
    near_zero = exchange(x_spread)
    w_query, w_key, w_value, w_out, w_gate, w_up, w_down, segments, deal_order = hold(
        (w_query, w_key, w_value, w_out, w_gate, w_up, w_down, segments, deal_order), x_spread
    )

    ids = jnp.stack([core, lax.axis_index("fsdp"), chip]).astype(jnp.int32)
    pair = jnp.arange(2, dtype=jnp.int32)
    rel_dev = (jnp.arange(chips, dtype=jnp.int32)[None, :] * 2) + (pair[:, None] ^ core)
    rel_slot = (rel_dev[:, :, None] * 2 + pair[None, None, :]).reshape(-1)
    near_chips = jnp.arange(chips, dtype=jnp.int32) ^ chip
    send_dev = near_chips[:, None] * 2 + (pair[None, :] ^ core)
    send_slot = (send_dev[:, :, None] * 2 + pair[None, None, :]).reshape(-1)
    spots = jnp.arange(blocks, dtype=jnp.int32)

    def look_up(slots):
        return jnp.sum(
            jnp.where(slots[:, None] == spots[None, :], deal_order[None, :], 0), axis=1
        ).astype(jnp.int32)

    rel_table = look_up(rel_slot)
    send_table = look_up(send_slot)
    earlier = (segments[None, :, :] < segments[:, None, :]).astype(jnp.int32)
    slot_start = jnp.sum(earlier, axis=1).astype(jnp.int32).reshape(blocks, blk, seqs)
    start = jnp.sum(
        jnp.where((deal_order[None, :] == spots[:, None])[:, :, None, None], slot_start[None], 0),
        axis=1,
    ).astype(jnp.int32)
    start = start.transpose(2, 0, 1).reshape(seqs, seq_len)

    def ranges(q_rows, k_rows):
        tiled = start.reshape(seqs, seq_len // q_rows, q_rows)
        begins = jnp.arange(seq_len // q_rows, dtype=jnp.int32) * q_rows // k_rows
        first = tiled[:, :, 0] // k_rows
        full = jnp.minimum(begins[None, :], (tiled[:, :, -1] + k_rows - 1) // k_rows)
        return tiled, first, full

    _, first, full = ranges(Q_FORE, K_FORE)
    tiled, first_back, full_back = ranges(Q_BACK, K_BACK)

    both = jnp.stack([gain_attn, gain_ffn], axis=1)
    spare = jnp.zeros((both.shape[0], -(3 * width + 2) % 128), bf16)
    own_qkv = jnp.concatenate(
        [take(w, 1, rank, width) for w in (w_query, w_key, w_value)] + [both, spare], axis=1
    )

    def hidden_columns(weight):
        return [take(weight, 1, rank + z * groups, per_shard) for z in range(shards)]

    own_gate_up = jnp.concatenate(hidden_columns(w_gate) + hidden_columns(w_up), axis=1)
    own_down = take(w_down, 0, rank, per_shard)
    out_grid = w_out.reshape(-1, 2, width, feats)
    own_out = take(out_grid, 1, core, 1).reshape(-1, feats)

    merged = 2 * hidden_width == feats
    if merged:
        ffn_own = [jnp.concatenate([own_gate_up, own_down])]
    else:
        ffn_own = [own_gate_up, own_down]
    qkv_pieces = shard_pieces(own_qkv)
    x_spread_one = jnp.broadcast_to(x_one, (chips,) + x_one.shape)
    cot_all = [cotangent[:, b] for b in range(seqs)]
    (
        near_zero, qkv_pieces, start, tiled, first, full, first_back, full_back, rel_table, send_table,
        x_spread_one, cot_all, own_out, ffn_own,
    ) = hold(
        (
            near_zero, qkv_pieces, start, tiled, first, full, first_back, full_back, rel_table, send_table,
            x_spread_one, cot_all, own_out, ffn_own,
        )
    )
    qkv = in_order(qkv_pieces, ids[1])
    gain_one, gain_two = qkv[:, 3 * width][None, :], qkv[:, 3 * width + 1][None, :]
    def flat(*pair):
        return [value.reshape(tokens, feats) for value in pair]

    def by_chip(value):
        return value.reshape(chips, rows, feats)

    def spread_cot(own):
        return lax.all_gather(own, PLANE, axis=0).reshape(chips, 2, rows, feats)

    tables = [(rel_table, send_table, first[b], full[b]) for b in range(seqs)]
    tables_back = [(rel_table, send_table, first_back[b], full_back[b]) for b in range(seqs)]

    def forward(b, near, far):
        query, key, value, normed, fine, logsum, *sent = attend_forward(
            tables[b], *flat(near, far), qkv, gain_one, start[b][:, None], width, chips
        )
        return (query, key, value, fine, logsum), normed, sent

    def mid_norm(x_own, own, swapped):
        middle = x_own.astype(f32) + own + swapped
        return middle, (middle * row_scale(middle) * gain_two.astype(f32)).astype(bf16)

    near_one = exchange(x_spread_one)
    out_pieces = shard_pieces(own_out)
    ffn_pieces = [lax.all_gather(value, "fsdp", axis=0) for value in ffn_own]
    saved_zero, normed_zero, sent_zero = forward(0, near_zero, swap_core(near_zero))
    near_one, sent_zero, out_pieces, cot_zero, cot_one = hold(
        (near_one, sent_zero, out_pieces, cot_all[0], cot_all[1])
    )
    near_cot = spread(cot_zero)
    got_zero = exchange_pieces(sent_zero)
    saved_one, normed_one, sent_one = forward(1, near_one, swap_core(near_one))
    got_zero, sent_one, near_cot = hold((got_zero, sent_one, near_cot))
    got_one = exchange_pieces(sent_one)
    att_zero, own, other = mix(ids, got_zero, out_pieces)
    mid_zero, norm_zero = mid_norm(x_zero, own, swap_core(other))
    norm_zero, got_one = hold((norm_zero, got_one))
    pieces_zero = send_copies(norm_zero)
    pieces_zero, got_one = hold((pieces_zero, got_one))
    near_zero = arrange(ids, pieces_zero)
    att_one, own, other = mix(ids, hold(got_one, near_zero), out_pieces)
    mid_one, norm_one = mid_norm(x_one, own, swap_core(other))
    cot_one, near_zero = hold((cot_one, near_zero))
    pieces_one = send_copies(norm_one)
    cots = (flat(near_cot, swap_core(near_cot)), [spread_cot(cot_one)])

    def ffn(b, near, far, split):
        mids = flat(near, far)
        *out_part, mid_near, mid_far, hidden, grad_pre = feed_forward(
            ids, mids, cots[b], ffn_pieces, hidden_width, split
        )
        return out_part, by_chip(mid_near), by_chip(mid_far), (*mids, hidden, grad_pre, *cots[b])

    out_zero, own_zero, far_zero, stream_zero = ffn(0, near_zero, swap_core(near_zero), False)
    near_one = arrange(ids, hold(pieces_one, stream_zero[2]))
    total_zero = core_sum(own_zero, swap_core(far_zero))
    near_far = hold((near_one, swap_core(near_one)), total_zero)
    out_one, own_one, far_one, stream_one = ffn(1, *near_far, False)
    sums_zero = hold(exchange(total_zero), stream_one[2])
    far_one = swap_core(far_one)
    ffn_sums = weight_sums(ids, (stream_zero, stream_one), shards)
    shares = [lax.psum_scatter(value, "fsdp", scatter_dimension=0) for value in ffn_sums]
    sums_zero, far_one = hold((sums_zero, far_one), ffn_sums[0])
    total_one = core_sum(own_one, far_one)

    def collect_out(part):
        flat_part = part.reshape(groups * rows, feats)
        return lax.psum_scatter(flat_part, PLANE, scatter_dimension=0, tiled=True)

    out_sum_zero = collect_out(out_zero[0])

    def mid_backward(b, grad_normed_mid, middle):
        scale_two = row_scale(middle)
        unit_two = middle * scale_two
        scaled_two = grad_normed_mid * gain_two.astype(f32)
        grad_middle = cot_all[b].astype(f32) + scale_two * (
            scaled_two - unit_two * jnp.mean(scaled_two * unit_two, axis=-1, keepdims=True)
        )
        return grad_middle, grad_middle.astype(bf16)

    def backward(b, saved, grad_got):
        return attend_backward(
            tables_back[b], saved, grad_got, qkv, tiled[b][:, None, :]
        )

    def qkv_stream(normed, grads):
        return normed.reshape(seq_len, feats), grads.reshape(seq_len, 3 * width)

    def in_backward(grad_normed_in, grad_middle, x_own):
        flat_in = x_own.astype(f32)
        scale_one = row_scale(flat_in)
        unit_one = flat_in * scale_one
        scaled_one = grad_normed_in * gain_one.astype(f32)
        return (
            grad_middle
            + scale_one
            * (scaled_one - unit_one * jnp.mean(scaled_one * unit_one, axis=-1, keepdims=True))
        ).astype(bf16)

    grad_mid_zero, branch = mid_backward(0, last_sum(sums_zero), mid_zero)
    grad_sent, grad_out_zero = unmix(ids, branch, swap_core(branch), att_zero, out_pieces, chips)
    total_one = hold(total_one, grad_sent)
    grad_got_zero = hold(exchange_pieces(grad_sent), out_sum_zero)
    sums_one = exchange(total_one)
    part_near, part_far, grads_zero = backward(0, saved_zero, grad_got_zero)
    sums_one = hold(sums_one, grads_zero)
    far_swapped = swap_core(by_chip(part_far))
    grad_mid_one, branch = mid_backward(1, last_sum(sums_one), mid_one)
    grad_sent, grad_out_one = unmix(ids, branch, swap_core(branch), att_one, out_pieces, chips)
    grad_got_one = exchange_pieces(grad_sent)
    far_swapped = hold(far_swapped, grad_sent)
    total_zero = core_sum(by_chip(part_near), far_swapped)
    sums_zero = exchange(total_zero)

    own_rows = feats // shards

    def rel_rows(value):
        value = value.astype(bf16)
        count = value.shape[0] // shards
        return [take(value, 0, ids[1] ^ r, count) for r in range(shards)]

    out_rel = rel_rows(grad_out_zero + grad_out_one)
    out_sent = send_pieces(out_rel)
    grad_got_one, shares = hold((grad_got_one, shares), total_zero)
    full_ffn = [lax.all_gather(share, PLANE, axis=0) for share in shares]
    part_near, part_far, grads_one = backward(1, saved_one, grad_got_one)
    part_near, part_far, grads_one, sums_zero, out_sent = hold(
        (part_near, part_far, grads_one, sums_zero, out_sent)
    )
    total_one = core_sum(by_chip(part_near), swap_core(by_chip(part_far)))
    qkv_one = qkv_first(*qkv_stream(normed_one, grads_one))
    total_one, qkv_one, grads_zero = hold((total_one, qkv_one, grads_zero))
    sums_one = exchange(total_one)
    grad_qkv = qkv_sums(ids, *qkv_stream(normed_zero, grads_zero), qkv_one, shards)
    own_rows = feats // shards
    g_gate_up, g_gain_two, (g_down,) = assemble(
        [full_ffn[0]],
        gain_ffn,
        (w_gate, w_up),
        shards,
        full_ffn[-1],
        own_rows if merged else 0,
        per_shard,
    )
    g_down = g_down.reshape(-1, feats)
    sent_qkv = send_pieces(grad_qkv)
    sent_qkv, g_gate_up, g_gain_two, g_down = hold((sent_qkv, g_gate_up, g_gain_two, g_down))
    share_qkv = add_pieces(grad_qkv[0], sent_qkv)
    out_sum_one = collect_out(hold(out_one[0], full_ffn, grad_qkv))
    share_out = add_pieces(out_rel[0], out_sent)
    spare = share_out.size // rows
    if share_qkv.shape[0] == rows and spare % 128 == 0:
        beside = jnp.concatenate([share_qkv, share_out.reshape(rows, spare)], axis=1)
        mixed = spread(hold(beside, sums_one))
        near_qkv = mixed[:, :, : 3 * width]
        own_sum = last_sum(mixed[:, :, 3 * width :]).reshape(-1, width, feats)
        other_sum = swap_core(own_sum)
        sides = (own_sum, other_sum)
        g_out = jnp.stack(
            [jnp.where(core == 0, *sides), jnp.where(core == 0, *sides[::-1])], axis=1
        ).reshape(own_rows, feats)
    else:
        near_qkv = spread(hold(share_qkv, sums_one))
        all_out = lax.all_gather(share_out, PLANE, axis=0).astype(f32)
        all_out = all_out.reshape(chips, 2, -1, width, feats)
        g_out = jnp.sum(all_out, axis=0).transpose(1, 0, 2, 3).reshape(own_rows, feats)

    outputs = [
        (mid_zero + out_sum_zero.astype(f32)).astype(bf16),
        (mid_one + out_sum_one.astype(f32)).astype(bf16),
    ]
    grad_inputs = [
        in_backward(last_sum(sums_zero), grad_mid_zero, x_zero),
        in_backward(last_sum(sums_one), grad_mid_one, x_one),
    ]
    far_qkv = swap_core(near_qkv)
    g_qkv, g_gain_one, _ = assemble(
        [ids, near_qkv, far_qkv], gain_attn, (w_query, w_key, w_value), 1
    )

    return (
        jnp.stack(outputs, axis=1),
        jnp.stack(grad_inputs, axis=1),
        *g_qkv,
        g_out,
        *g_gate_up,
        g_down,
        g_gain_one,
        g_gain_two,
    )


def solution(mesh):
    names = mesh.axis_names
    ctx, shards = mesh.shape[names[0]], mesh.shape[names[1]]
    fine_mesh = Mesh(mesh.devices.reshape(ctx // 2, 2, shards), ("chip", "core", "fsdp"))
    by_row = P("fsdp", None)
    by_token = P(PLANE, "fsdp", None)
    return jax.shard_map(
        per_device,
        mesh=fine_mesh,
        in_specs=(by_token,) + (by_row,) * 7 + (P("fsdp"), P("fsdp"), P(None, "fsdp"), P(), by_token),
        out_specs=(by_token, by_token) + (by_row,) * 7 + (P("fsdp"), P("fsdp")),
        check_vma=False,
    )
```

```python
import functools

import jax
import jax.numpy as jnp
from jax import lax
from jax.experimental import pallas as pl
from jax.experimental.pallas import tpu as pltpu
from jax.sharding import Mesh, PartitionSpec as P

HEAD_DIM = 64
EPSILON = 1e-05
MASKED = -1e30
TILE = 256
PROJ = 512
Q_FORE, K_FORE = 512, 512
Q_BACK, K_BACK = 512, 512
PLANE = ("chip", "core")

bf16 = jnp.bfloat16
f32 = jnp.float32


def dot_nn(left_op, right_op):
    return lax.dot_general(left_op, right_op, (((1,), (0,)), ((), ())), preferred_element_type=f32)


def dot_nt(left_op, right_op):
    return lax.dot_general(left_op, right_op, (((1,), (1,)), ((), ())), preferred_element_type=f32)


def dot_tn(left_op, right_op):
    return lax.dot_general(left_op, right_op, (((0,), (0,)), ((), ())), preferred_element_type=f32)


def row_scale(values):
    return lax.rsqrt(jnp.mean(values * values, axis=-1, keepdims=True) + EPSILON)


def swap_core(value):
    return lax.ppermute(value, "core", [(0, 1), (1, 0)])


def swap_chip(value, mask):
    count = lax.axis_size("chip")
    return lax.ppermute(value, "chip", [(i, i ^ mask) for i in range(count)])


def swap_shard(value, mask):
    count = lax.axis_size("fsdp")
    return lax.ppermute(value, "fsdp", [(i, i ^ mask) for i in range(count)])


def hold(value, *deps):
    return lax.optimization_barrier((value, deps))[0]


def spread(value):
    count = lax.axis_size("chip")
    return exchange(jnp.broadcast_to(value, (count,) + value.shape))


def exchange(value):
    return lax.all_to_all(value, "chip", 0, 0)


def arrange_kernel(ids, *refs):
    out = refs[-1]
    for r, piece in enumerate(refs[:-1]):
        out[ids[2] ^ r] = piece[...]


def arrange(ids, pieces):
    return pl.pallas_call(
        arrange_kernel,
        out_shape=jax.ShapeDtypeStruct((len(pieces),) + pieces[0].shape, bf16),
        in_specs=[smem()] + [vmem()] * len(pieces),
        out_specs=vmem(),
        compiler_params=LIMIT,
        cost_estimate=cost(3),
        name="arrange",
    )(ids, *pieces)


def send_copies(value):
    return exchange_pieces([value] * lax.axis_size("chip"))


def add_kernel(own, other, total):
    total[...] = (own[...].astype(f32) + other[...].astype(f32)).astype(bf16)


def exchange_pieces(pieces):
    return [pieces[0]] + [swap_chip(pieces[r], r) for r in range(1, len(pieces))]


def core_sum(own, swapped):
    chips, rows, width = own.shape
    block = pl.BlockSpec((chips // 2, rows, width), lambda t: (t, 0, 0))
    return pl.pallas_call(
        add_kernel,
        grid=(2,),
        out_shape=jax.ShapeDtypeStruct(own.shape, bf16),
        in_specs=[block, block],
        out_specs=block,
        cost_estimate=cost(3),
        name="core_sum",
    )(own, swapped)


def last_sum(value):
    return jnp.sum(value.astype(f32), axis=0)


def shard_pieces(value):
    return [value] + [swap_shard(value, r) for r in range(1, lax.axis_size("fsdp"))]


def shard_sum(pieces):
    return add_pieces(pieces[0], send_pieces(pieces))


def in_order(pieces, shard):
    stacked = jnp.stack(pieces)
    rows = [lax.dynamic_index_in_dim(stacked, shard ^ z, keepdims=False) for z in range(len(pieces))]
    return jnp.concatenate(rows)


def send_pieces(pieces):
    return [swap_shard(pieces[r], r) for r in range(1, len(pieces))]


def add_pieces(own, received):
    total = own.astype(f32)
    for piece in received:
        total = total + piece.astype(f32)
    return total.astype(bf16)


def head_masks(rows, width):
    lanes = lax.broadcasted_iota(jnp.int32, (rows, width), 1) // HEAD_DIM
    return [lanes == h for h in range(width // HEAD_DIM)]


def stack_heads(values, masks):
    zero = jnp.zeros_like(values)
    return jnp.concatenate([jnp.where(mask, values, zero) for mask in masks], axis=0)


def merge_heads(stacked, masks, rows):
    merged = stacked[:rows]
    for h in range(1, len(masks)):
        merged = jnp.where(masks[h], stacked[h * rows : (h + 1) * rows], merged)
    return merged


def forward_kernel(
    rel, send, first, full, x_near, x_far, weight, gain, start,
    query_out, key_out, value_out, normed, fine_out, logsum_out, *refs,
):
    attended, refs = refs[:-13], refs[-13:]
    query, key, value, fine, logsum, x_tiles, normed_tiles, scores, top, total = refs[:10]
    in_sems, normed_sems, out_sems = refs[10:]
    width = query.shape[1]
    seq_len = query.shape[0]
    heads = width // HEAD_DIM
    blk = TILE // 2
    tiles = x_near.shape[0] // PROJ
    blocks = PROJ // blk
    gain_row = gain[...].astype(f32)
    loads, stores = [], []
    for i in range(2 * tiles):
        rows = pl.ds(i % tiles * PROJ, PROJ)
        source = x_near if i < tiles else x_far
        loads.append(pltpu.make_async_copy(source.at[rows], x_tiles.at[i], in_sems.at[i]))
        stores.append(
            pltpu.make_async_copy(
                normed_tiles.at[i], normed.at[i // tiles, rows], normed_sems.at[i]
            )
        )
        loads[i].start()
    for i in range(2 * tiles):
        loads[i].wait()
        rows_in = x_tiles[i].astype(f32)
        tile = (rows_in * row_scale(rows_in) * gain_row).astype(bf16)
        normed_tiles[i] = tile
        stores[i].start()
        mixed = dot_nn(tile, weight[:, : 3 * width])
        for h in range(blocks):
            where = pl.ds(pl.multiple_of(rel[i * blocks + h] * blk, blk), blk)
            part = mixed[h * blk : (h + 1) * blk]
            query[where, :] = (part[:, :width].astype(bf16) * 0.125).astype(bf16)
            key[where, :] = part[:, width : 2 * width].astype(bf16)
            value[where, :] = part[:, 2 * width :].astype(bf16)
    for i, (source, target) in enumerate(
        ((query, query_out), (key, key_out), (value, value_out))
    ):
        stores.append(pltpu.make_async_copy(source, target, out_sems.at[i]))
        stores[-1].start()

    masks = head_masks(Q_FORE, width)
    big = heads * Q_FORE

    def query_tile(qb, _):
        rows = pl.ds(pl.multiple_of(qb * Q_FORE, Q_FORE), Q_FORE)
        stacked = stack_heads(query[rows, :], masks)
        top[...] = jnp.full_like(top, MASKED)
        begin = jnp.concatenate([start[rows, :]] * heads, axis=0)
        diagonal = qb * Q_FORE // K_FORE
        last = (qb * Q_FORE + Q_FORE + K_FORE - 1) // K_FORE

        def score(kb, masked):
            keys = key[pl.ds(pl.multiple_of(kb * K_FORE, K_FORE), K_FORE), :]
            raw = dot_nt(stacked, keys)
            if masked:
                k_pos = kb * K_FORE + lax.broadcasted_iota(jnp.int32, (big, K_FORE), 1)
                q_row = lax.broadcasted_iota(jnp.int32, (big, K_FORE), 0) & (Q_FORE - 1)
                allowed = (k_pos >= begin) & (k_pos <= qb * Q_FORE + q_row)
                raw = jnp.where(allowed, raw, MASKED)
            scores[kb] = raw
            best = raw[:, :128]
            for c in range(1, K_FORE // 128):
                best = jnp.maximum(best, raw[:, c * 128 : (c + 1) * 128])
            top[...] = jnp.maximum(top[...], best)

        def masked_step(kb, _):
            score(kb, True)
            return 0

        def plain_step(kb, _):
            score(kb, False)
            return 0

        lax.fori_loop(first[qb], full[qb], masked_step, 0)
        lax.fori_loop(full[qb], diagonal, plain_step, 0)
        lax.fori_loop(diagonal, last, masked_step, 0)
        peak = jnp.max(top[...], axis=1, keepdims=True)
        top[...] = jnp.broadcast_to(peak, top.shape)
        total[...] = jnp.zeros_like(total)

        def weigh(kb, carry):
            vals = value[pl.ds(pl.multiple_of(kb * K_FORE, K_FORE), K_FORE), :]
            pieces = []
            summed = total[...]
            for c in range(K_FORE // 128):
                piece = jnp.exp(scores[kb, :, c * 128 : (c + 1) * 128] - top[...])
                summed = summed + piece
                pieces.append(piece.astype(bf16))
            total[...] = summed
            return carry + dot_nn(jnp.concatenate(pieces, axis=1), vals)

        gathered = lax.fori_loop(first[qb], last, weigh, jnp.zeros((big, width), f32))
        denom = jnp.sum(total[...], axis=1, keepdims=True)
        fine[rows, :] = merge_heads(gathered / denom, masks, Q_FORE)
        logs = jnp.broadcast_to(peak + jnp.log(denom), (big, width))
        logsum[rows, :] = merge_heads(logs, masks, Q_FORE)
        return 0

    lax.fori_loop(0, seq_len // Q_FORE, query_tile, 0)
    for i, (source, target) in enumerate(((fine, fine_out), (logsum, logsum_out))):
        stores.append(pltpu.make_async_copy(source, target, out_sems.at[3 + i]))
        stores[-1].start()

    count = seq_len // blk // len(attended)
    for r, piece in enumerate(attended):
        for j in range(count):
            where = pl.ds(pl.multiple_of(send[r * count + j] * blk, blk), blk)
            piece[j * blk : (j + 1) * blk, :] = fine[where, :].astype(bf16)
    for copy in stores:
        copy.wait()


def backward_kernel(
    rel, send, first, full, query, key, value, fine, logsum, weight, start, *refs
):
    grad_in, refs = refs[:-13], refs[-13:]
    part_near, part_far, grads_out, grad_at, grad_q, grad_k, grad_v, grad_q2 = refs[:8]
    parts, grads, local_weight, sems, weight_sem = refs[8:]
    load = pltpu.make_async_copy(weight, local_weight, weight_sem)
    load.start()
    seq_len, width = query.shape
    heads = width // HEAD_DIM
    blk = TILE // 2
    big = heads * Q_BACK

    count = seq_len // blk // len(grad_in)
    for r, piece in enumerate(grad_in):
        for j in range(count):
            where = pl.ds(pl.multiple_of(send[r * count + j] * blk, blk), blk)
            grad_at[where, :] = piece[j * blk : (j + 1) * blk, :]
    grad_k[...] = jnp.zeros_like(grad_k)
    grad_v[...] = jnp.zeros_like(grad_v)
    masks = head_masks(Q_BACK, width)

    def flip(values):
        if width < 128:
            values = jnp.concatenate([values, jnp.zeros((Q_BACK, 128 - width), f32)], axis=1)
        return values.T

    def query_tile(qb, _):
        rows = pl.ds(pl.multiple_of(qb * Q_BACK, Q_BACK), Q_BACK)
        stacked = stack_heads(query[rows, :], masks)
        grad_rows = grad_at[rows, :]
        grad_stacked = stack_heads(grad_rows, masks)
        products = flip(grad_rows.astype(f32) * fine[rows, :])
        logs = flip(logsum[rows, :])
        delta = jnp.concatenate(
            [
                jnp.sum(products[h * HEAD_DIM : (h + 1) * HEAD_DIM], axis=0, keepdims=True)
                for h in range(heads)
            ],
            axis=1,
        )
        log_row = jnp.concatenate(
            [logs[h * HEAD_DIM : h * HEAD_DIM + 1] for h in range(heads)], axis=1
        )
        begin = jnp.concatenate([start[qb]] * heads, axis=1)
        grad_q2[...] = jnp.zeros_like(grad_q2)
        diagonal = qb * Q_BACK // K_BACK
        last = (qb * Q_BACK + Q_BACK + K_BACK - 1) // K_BACK

        def step(kb, masked):
            where = pl.ds(pl.multiple_of(kb * K_BACK, K_BACK), K_BACK)
            keys = key[where, :]
            probs = jnp.exp(dot_nt(keys, stacked) - log_row)
            if masked:
                k_pos = kb * K_BACK + lax.broadcasted_iota(jnp.int32, (K_BACK, big), 0)
                q_row = lax.broadcasted_iota(jnp.int32, (K_BACK, big), 1) & (Q_BACK - 1)
                allowed = (k_pos >= begin) & (k_pos <= qb * Q_BACK + q_row)
                probs = jnp.where(allowed, probs, 0.0)
            slope = (probs * (dot_nt(value[where, :], grad_stacked) - delta)).astype(bf16)
            grad_v[where, :] += dot_nn(probs.astype(bf16), grad_stacked)
            grad_k[where, :] += dot_nn(slope, stacked)
            grad_q2[...] += dot_tn(slope, keys)

        def masked_step(kb, _):
            step(kb, True)
            return 0

        def plain_step(kb, _):
            step(kb, False)
            return 0

        lax.fori_loop(first[qb], full[qb], masked_step, 0)
        lax.fori_loop(full[qb], diagonal, plain_step, 0)
        lax.fori_loop(diagonal, last, masked_step, 0)
        grad_q[rows, :] = (merge_heads(grad_q2[...], masks, Q_BACK) * 0.125).astype(bf16)
        return 0

    lax.fori_loop(0, seq_len // Q_BACK, query_tile, 0)

    tiles = seq_len // PROJ // 2
    blocks = PROJ // blk
    load.wait()
    stores = []
    for i in range(2 * tiles):
        rows = pl.ds(i % tiles * PROJ, PROJ)
        for h in range(blocks):
            where = pl.ds(pl.multiple_of(rel[i * blocks + h] * blk, blk), blk)
            here = pl.ds(h * blk, blk)
            grads[i, here, :width] = grad_q[where, :]
            grads[i, here, width : 2 * width] = grad_k[where, :].astype(bf16)
            grads[i, here, 2 * width :] = grad_v[where, :].astype(bf16)
        target = grads_out.at[i // tiles, rows]
        stores.append(pltpu.make_async_copy(grads.at[i], target, sems.at[0, i]))
        stores[-1].start()
        parts[i] = dot_nt(grads[i], local_weight[:, : 3 * width]).astype(bf16)
        target = (part_near if i < tiles else part_far).at[rows]
        stores.append(pltpu.make_async_copy(parts.at[i], target, sems.at[1, i]))
        stores[-1].start()
    for copy in stores:
        copy.wait()


def place_pieces(target, pieces, shard, begin, count):
    for r, piece in enumerate(pieces):
        at = pl.multiple_of((shard ^ r) * count, count)
        target[pl.ds(at, count), :] = piece[begin : begin + count, :]


def near_first(target, source, chip, count):
    for r in range(count):
        rows = target.shape[0] // count
        at = pl.multiple_of((chip ^ r) * rows, rows)
        target[r * rows : (r + 1) * rows, :] = source[pl.ds(at, rows), :]


def mix_kernel(ids, *refs, chips):
    got, pieces, (attended, own, other, whole, weight) = refs[:chips], refs[chips:-5], refs[-5:]
    rows = own.shape[0]
    place_pieces(whole, pieces, ids[1], 0, pieces[0].shape[0])
    near_first(weight, whole, ids[2], chips)
    joined = jnp.concatenate([piece[...] for piece in got], axis=1)
    attended[...] = joined
    own[...] = dot_nn(joined[:rows], weight[...])
    other[...] = dot_nn(joined[rows:], weight[...])


def unmix_kernel(ids, own, other, attended, *refs, chips):
    outs = chips + 3
    pieces, grad_sent, (grad_weight, whole, weight) = refs[:-outs], refs[-outs:-3], refs[-3:]
    place_pieces(whole, pieces, ids[1], 0, pieces[0].shape[0])
    near_first(weight, whole, ids[2], chips)
    branch = jnp.concatenate([own[...], other[...]], axis=0)
    mixed = dot_nt(branch, weight[...]).astype(bf16)
    sums = dot_tn(attended[...], branch)
    width = grad_sent[0].shape[1]
    for r in range(chips):
        grad_sent[r][...] = mixed[:, r * width : (r + 1) * width]
        at = pl.multiple_of((ids[2] ^ r) * width, width)
        grad_weight[pl.ds(at, width), :] = sums[r * width : (r + 1) * width]


def qkv_kernel(ids, *refs):
    normed, grads, before = refs[:3]
    outs, total = refs[3:-1], refs[-1]
    t = pl.program_id(0)

    @pl.when(t == 0)
    def _():
        total[...] = before[...]

    total[...] += dot_tn(normed[...], grads[...])

    @pl.when(t == pl.num_programs(0) - 1)
    def _():
        rows = outs[0].shape[0]
        for r, out in enumerate(outs):
            at = pl.multiple_of((ids[1] ^ r) * rows, rows)
            out[...] = total[pl.ds(at, rows), :].astype(bf16)


def ffn_kernel(ids, x_near, x_far, *refs, split, sides):
    cot_refs, refs = refs[:sides], refs[sides:]
    outs = 7 + split
    pieces, out_parts = refs[:-outs], refs[-outs : 1 + split - outs]
    mid_near, mid_far, hidden, grad_pre, gate_up, down = refs[-6:]
    t = pl.program_id(0)
    half = pl.num_programs(0) // 2
    feats, size = gate_up.shape[0], gate_up.shape[1] // 2
    shards = pieces[0].shape[0]
    rows, more = feats // shards, size // shards
    begin = rows if len(pieces) == 1 else 0

    @pl.when(t == 0)
    def _():
        for z in range(shards):
            gate_up[z * rows : (z + 1) * rows, :] = pieces[0][z, :rows, :]
            down[z * more : (z + 1) * more, :] = pieces[-1][z, begin : begin + more, :]

    tile = jnp.where(t < half, x_near[...], x_far[...])
    cot = cot_refs[0][...].reshape(tile.shape)
    if sides == 2:
        cot = jnp.where(t < half, cot, cot_refs[1][...])
    pre = dot_nn(tile, gate_up[...])
    gate_pre, up_pre = pre[:, :size], pre[:, size:]
    sigma = 0.5 * jnp.tanh(0.5 * gate_pre) + 0.5
    active = gate_pre * sigma
    low = (active * up_pre).astype(bf16)
    grad_hidden = dot_nt(cot, down[...])
    hidden[...] = low
    out_part = dot_nn(low, down[...]).astype(bf16)
    grad_gate = grad_hidden * up_pre * sigma * (1.0 + gate_pre * (1.0 - sigma))
    grad_up = grad_hidden * active
    grads = jnp.concatenate([grad_gate.astype(bf16), grad_up.astype(bf16)], axis=1)
    grad_pre[...] = grads
    mid_part = dot_nt(grads, gate_up[...]).astype(bf16)

    if not split:
        out_parts[0][...] = out_part.reshape(out_parts[0].shape)

    @pl.when(t < half)
    def _():
        mid_near[...] = mid_part
        if split:
            out_parts[0][...] = out_part

    @pl.when(t >= half)
    def _():
        mid_far[...] = mid_part
        if split:
            out_parts[1][...] = out_part


def weight_kernel(ids, *refs, counts, shards):
    streams = len(counts)
    ins, outs, (wide, down) = refs[: sum(counts)], refs[sum(counts) : -2], refs[-2:]
    t = pl.program_id(0)
    per = pl.num_programs(0) // streams

    @pl.when(t == 0)
    def _():
        wide[...] = jnp.zeros_like(wide)
        down[...] = jnp.zeros_like(down)

    for b in range(streams):
        mine = ins[sum(counts[:b]) : sum(counts[: b + 1])]

        @pl.when((t >= b * per) & (t < (b + 1) * per))
        def _(b=b, mine=mine):
            x_near, x_far, hidden, grad_pre = mine[:4]
            near = t < b * per + per // 2
            tile = jnp.where(near, x_near[...], x_far[...])
            cot = mine[4][...].reshape(tile.shape)
            if len(mine) == 6:
                cot = jnp.where(near, cot, mine[5][...])
            wide[...] += dot_tn(tile, grad_pre[...])
            down[...] += dot_tn(hidden[...], cot)

    @pl.when(t == pl.num_programs(0) - 1)
    def _():
        rows, more = wide.shape[0] // shards, down.shape[0] // shards
        begin = rows if len(outs) == 1 else 0
        for z in range(shards):
            outs[0][z, :rows, :] = wide[z * rows : (z + 1) * rows, :].astype(bf16)
            piece = down[z * more : (z + 1) * more, :]
            outs[-1][z, begin : begin + more, :] = piece.astype(bf16)


def assemble_kernel(*refs, kinds, shards, with_down, sides):
    sources, gain = refs[:sides], refs[sides]
    if sides == 1:
        parts = sources[0]
    else:
        ids, near, far = sources
        parts = []
        for p in range(near.shape[0]):
            own, other = near[p], far[p]
            parts.append(jnp.where(ids[0] == 0, own, other))
            parts.append(jnp.where(ids[0] == 0, other, own))
    refs = refs[sides - 1 :]
    weights = refs[2 : 2 + kinds]
    rest = refs[2 + kinds :]
    if with_down:
        down_part, rest = rest[0], rest[1:]
    outs, gain_out = rest[:kinds], rest[kinds]
    groups = len(parts) if sides > 1 else parts.shape[0]
    size = sources[-1].shape[2]
    pieces = size // kinds
    lanes = pieces // shards
    sums = 0.0
    for k in range(kinds):
        columns = []
        for z in range(shards):
            for i in range(groups):
                at = k * pieces + z * lanes
                columns.append(parts[i][:, at : at + lanes].astype(f32))
        full = jnp.concatenate(columns, axis=1)
        outs[k][...] = full
        sums = sums + jnp.sum(full * weights[k][...].astype(f32), axis=1, keepdims=True)
    gain_out[...] = sums / gain[...].astype(f32)
    if with_down:
        rest[kinds + 1][...] = down_part[...].astype(f32)


def smem():
    return pl.BlockSpec(memory_space=pltpu.SMEM)


def hbm():
    return pl.BlockSpec(memory_space=pl.ANY)


def vmem():
    return pl.BlockSpec(memory_space=pltpu.VMEM)


def cost(micros):
    return pl.CostEstimate(flops=micros * 10**9, bytes_accessed=2**20, transcendentals=0)


LIMIT = pltpu.CompilerParams(vmem_limit_bytes=56 * 2**20)


def attend_forward(tables, x_near, x_far, weight, gain, start, width, chips):
    half_rows, feats = x_near.shape
    seq_len = 2 * half_rows
    big = (width // HEAD_DIM) * Q_FORE
    shape = jax.ShapeDtypeStruct
    narrow = shape((seq_len, width), bf16)
    wide = shape((seq_len, width), f32)
    pairs = seq_len * seq_len * width // 2
    return pl.pallas_call(
        forward_kernel,
        out_shape=[narrow, narrow, narrow, shape((2, half_rows, feats), bf16), wide, wide]
        + [shape((seq_len // chips, width), bf16)] * chips,
        in_specs=[smem()] * 4 + [hbm()] * 2 + [vmem()] * 3,
        out_specs=[hbm()] * 6 + [vmem()] * chips,
        scratch_shapes=[
            pltpu.VMEM((seq_len, width), bf16),
            pltpu.VMEM((seq_len, width), bf16),
            pltpu.VMEM((seq_len, width), bf16),
            pltpu.VMEM((seq_len, width), f32),
            pltpu.VMEM((seq_len, width), f32),
            pltpu.VMEM((seq_len // PROJ, PROJ, feats), bf16),
            pltpu.VMEM((seq_len // PROJ, PROJ, feats), bf16),
            pltpu.VMEM((seq_len // K_FORE, big, K_FORE), f32),
            pltpu.VMEM((big, 128), f32),
            pltpu.VMEM((big, 128), f32),
            pltpu.SemaphoreType.DMA((seq_len // PROJ,)),
            pltpu.SemaphoreType.DMA((seq_len // PROJ,)),
            pltpu.SemaphoreType.DMA((5,)),
        ],
        compiler_params=LIMIT,
        cost_estimate=cost(31),
        name="attend_forward",
    )(*tables, x_near, x_far, weight, gain, start)


def attend_backward(tables, saved, grad_in, weight, start):
    query = saved[0]
    seq_len, width = query.shape
    feats = weight.shape[0]
    big = (width // HEAD_DIM) * Q_BACK
    shape = jax.ShapeDtypeStruct
    pairs = seq_len * seq_len * width // 2
    return pl.pallas_call(
        backward_kernel,
        out_shape=(
            shape((seq_len // 2, feats), bf16),
            shape((seq_len // 2, feats), bf16),
            shape((2, seq_len // 2, 3 * width), bf16),
        ),
        in_specs=[smem()] * 4 + [vmem()] * 5 + [hbm()] + [vmem()] * (1 + len(grad_in)),
        out_specs=[hbm()] * 3,
        scratch_shapes=[
            pltpu.VMEM((seq_len, width), bf16),
            pltpu.VMEM((seq_len, width), bf16),
            pltpu.VMEM((seq_len, width), f32),
            pltpu.VMEM((seq_len, width), f32),
            pltpu.VMEM((big, width), f32),
            pltpu.VMEM((seq_len // PROJ, PROJ, feats), bf16),
            pltpu.VMEM((seq_len // PROJ, PROJ, 3 * width), bf16),
            pltpu.VMEM(weight.shape, bf16),
            pltpu.SemaphoreType.DMA((2, seq_len // PROJ)),
            pltpu.SemaphoreType.DMA,
        ],
        compiler_params=LIMIT,
        cost_estimate=cost(31),
        name="attend_backward",
    )(*tables, *saved, weight, start, *grad_in)


def mix(ids, got, pieces):
    chips = len(got)
    doubled, width = got[0].shape
    feats = pieces[0].shape[1]
    size = chips * width
    shape = jax.ShapeDtypeStruct
    return pl.pallas_call(
        functools.partial(mix_kernel, chips=chips),
        out_shape=(
            shape((doubled, size), bf16),
            shape((doubled // 2, feats), f32),
            shape((doubled // 2, feats), f32),
        ),
        in_specs=[smem()] + [vmem()] * (chips + len(pieces)),
        out_specs=[vmem()] * 3,
        scratch_shapes=[pltpu.VMEM((size, feats), bf16)] * 2,
        compiler_params=LIMIT,
        cost_estimate=cost(3),
        name="mix",
    )(ids, *got, *pieces)


def unmix(ids, own, other, attended, pieces, chips):
    rows, feats = own.shape
    size = attended.shape[1]
    shape = jax.ShapeDtypeStruct
    outs = pl.pallas_call(
        functools.partial(unmix_kernel, chips=chips),
        out_shape=[shape((2 * rows, size // chips), bf16)] * chips + [shape((size, feats), f32)],
        in_specs=[smem()] + [vmem()] * (3 + len(pieces)),
        out_specs=[vmem()] * (chips + 1),
        scratch_shapes=[pltpu.VMEM((size, feats), bf16)] * 2,
        compiler_params=LIMIT,
        cost_estimate=cost(4),
        name="unmix",
    )(ids, own, other, attended, *pieces)
    return outs[:-1], outs[-1]


ROWS = 512


def feed_forward(ids, mids, cot, pieces, size, split):
    tokens, feats = mids[0].shape
    rows = ROWS // 2
    chips = tokens // rows
    half = tokens // ROWS
    shape = jax.ShapeDtypeStruct
    near = pl.BlockSpec((ROWS, feats), lambda t, ids: (jnp.minimum(t, half - 1), 0))
    far = pl.BlockSpec((ROWS, feats), lambda t, ids: (jnp.maximum(t - half, 0), 0))
    by_device = pl.BlockSpec(
        (ROWS // rows, None, rows, feats),
        lambda t, ids: (lax.rem(t, half), ids[0] ^ lax.div(t, half), 0, 0),
    )
    cot_specs = [by_device] if len(cot) == 1 else [near, far]

    def tiles(width):
        return pl.BlockSpec((ROWS, width), lambda t, ids: (t, 0))

    side = shape((tokens, feats), bf16)
    return pl.pallas_call(
        functools.partial(ffn_kernel, split=split, sides=len(cot)),
        grid_spec=pltpu.PrefetchScalarGridSpec(
            num_scalar_prefetch=1,
            grid=(2 * half,),
            in_specs=[near, far, *cot_specs]
            + [pl.BlockSpec(piece.shape, lambda t, ids: (0, 0, 0)) for piece in pieces],
            out_specs=([near, far] if split else [by_device])
            + [near, far, tiles(size), tiles(2 * size)],
            scratch_shapes=[
                pltpu.VMEM((feats, 2 * size), bf16),
                pltpu.VMEM((size, feats), bf16),
            ],
        ),
        out_shape=([side, side] if split else [shape((chips, 2, rows, feats), bf16)])
        + [
            side,
            side,
            shape((2 * tokens, size), bf16),
            shape((2 * tokens, 2 * size), bf16),
        ],
        compiler_params=LIMIT,
        cost_estimate=cost(20),
        name="feed_forward",
    )(ids, *mids, *cot, *pieces)


def weight_sums(ids, streams, shards):
    tokens, feats = streams[0][0].shape
    size = streams[0][2].shape[1]
    rows = ROWS // 2
    half = tokens // ROWS
    per = 2 * half
    shape = jax.ShapeDtypeStruct
    specs = []
    for b in range(len(streams)):

        def local(t, b=b):
            return jnp.clip(t - b * per, 0, per - 1)

        near = pl.BlockSpec(
            (ROWS, feats), lambda t, ids, f=local: (jnp.minimum(f(t), half - 1), 0)
        )
        far = pl.BlockSpec(
            (ROWS, feats), lambda t, ids, f=local: (jnp.maximum(f(t) - half, 0), 0)
        )
        by_device = pl.BlockSpec(
            (ROWS // rows, None, rows, feats),
            lambda t, ids, f=local: (lax.rem(f(t), half), ids[0] ^ lax.div(f(t), half), 0, 0),
        )
        specs += [
            near,
            far,
            pl.BlockSpec((ROWS, size), lambda t, ids, f=local: (f(t), 0)),
            pl.BlockSpec((ROWS, 2 * size), lambda t, ids, f=local: (f(t), 0)),
        ]
        specs += [by_device] if len(streams[b]) == 5 else [near, far]
    if 2 * size == feats:
        outs = [(shards, (feats + size) // shards, feats)]
    else:
        outs = [(shards, feats // shards, 2 * size), (shards, size // shards, feats)]
    return pl.pallas_call(
        functools.partial(weight_kernel, counts=[len(v) for v in streams], shards=shards),
        grid_spec=pltpu.PrefetchScalarGridSpec(
            num_scalar_prefetch=1,
            grid=(per * len(streams),),
            in_specs=specs,
            out_specs=[pl.BlockSpec(out, lambda t, ids: (0, 0, 0)) for out in outs],
            scratch_shapes=[pltpu.VMEM((feats, 2 * size), f32), pltpu.VMEM((size, feats), f32)],
        ),
        out_shape=[shape(out, bf16) for out in outs],
        compiler_params=LIMIT,
        cost_estimate=cost(23),
        name="weight_sums",
    )(ids, *[value for stream in streams for value in stream])


def qkv_first(normed, grads):
    tokens, feats = normed.shape
    size = grads.shape[1]

    def kernel(normed_ref, grads_ref, total):
        @pl.when(pl.program_id(0) == 0)
        def _():
            total[...] = jnp.zeros_like(total)

        total[...] += dot_tn(normed_ref[...], grads_ref[...])

    return pl.pallas_call(
        kernel,
        grid=(tokens // ROWS,),
        out_shape=jax.ShapeDtypeStruct((feats, size), f32),
        in_specs=[
            pl.BlockSpec((ROWS, feats), lambda t: (t, 0)),
            pl.BlockSpec((ROWS, size), lambda t: (t, 0)),
        ],
        out_specs=pl.BlockSpec((feats, size), lambda t: (0, 0)),
        compiler_params=LIMIT,
        cost_estimate=cost(6),
        name="qkv_first",
    )(normed, grads)


def qkv_sums(ids, normed, grads, before, shards):
    tokens, feats = normed.shape
    size = grads.shape[1]
    out = (feats // shards, size)
    return pl.pallas_call(
        qkv_kernel,
        grid_spec=pltpu.PrefetchScalarGridSpec(
            num_scalar_prefetch=1,
            grid=(tokens // ROWS,),
            in_specs=[
                pl.BlockSpec((ROWS, feats), lambda t, ids: (t, 0)),
                pl.BlockSpec((ROWS, size), lambda t, ids: (t, 0)),
                pl.BlockSpec((feats, size), lambda t, ids: (0, 0)),
            ],
            out_specs=[pl.BlockSpec(out, lambda t, ids: (0, 0))] * shards,
            scratch_shapes=[pltpu.VMEM((feats, size), f32)],
        ),
        out_shape=[jax.ShapeDtypeStruct(out, bf16)] * shards,
        compiler_params=LIMIT,
        cost_estimate=cost(6),
        name="qkv_sums",
    )(ids, normed, grads, before)


STEPS = 4


def assemble(parts, gain, weights, shards, downs=None, begin=0, down_rows=0):
    rows, columns = weights[0].shape
    step = rows // STEPS
    shape = jax.ShapeDtypeStruct
    sides = len(parts)
    groups, size = parts[-1].shape[0] * min(2, sides), parts[-1].shape[2]
    row_block = pl.BlockSpec((step, columns), lambda t: (t, 0))
    thin = pl.BlockSpec((step, 1), lambda t: (t, 0))
    count = len(weights)
    args = [*parts, gain[:, None], *weights]
    share_spec = pl.BlockSpec((parts[-1].shape[0], step, size), lambda t: (0, t, 0))
    in_specs = [share_spec] if sides == 1 else [smem(), share_spec, share_spec]
    in_specs += [thin] + [row_block] * count
    out_shape = [shape((rows, columns), f32)] * count + [shape((rows, 1), f32)]
    out_specs = [row_block] * count + [thin]
    if down_rows:
        share, feats = groups // STEPS, downs.shape[2]
        args.append(downs)
        in_specs.append(
            pl.BlockSpec((share, down_rows, feats), lambda t: (t, begin // down_rows, 0))
        )
        out_shape.append(shape((groups, down_rows, feats), f32))
        out_specs.append(pl.BlockSpec((share, down_rows, feats), lambda t: (t, 0, 0)))
    outs = pl.pallas_call(
        functools.partial(
            assemble_kernel, kinds=count, shards=shards, with_down=bool(down_rows), sides=sides
        ),
        grid=(STEPS,),
        out_shape=out_shape,
        in_specs=in_specs,
        out_specs=out_specs,
        compiler_params=LIMIT,
        cost_estimate=cost(2),
        name="assemble",
    )(*args)
    return outs[:count], outs[count][:, 0], outs[count + 1 :]


def per_device(
    inputs, w_query, w_key, w_value, w_out, w_gate, w_up, w_down,
    gain_attn, gain_ffn, segments, deal_order, cotangent,
):
    rows, seqs, feats = inputs.shape
    chips = lax.axis_size("chip")
    groups = 2 * chips
    shards = lax.axis_size("fsdp")
    chip = lax.axis_index("chip")
    core = lax.axis_index("core")
    rank = chip * 2 + core
    width = feats // groups
    hidden_width = w_gate.shape[1] // groups
    per_shard = hidden_width // shards
    seq_len = rows * groups
    blocks = deal_order.shape[0]
    blk = rows // 2
    tokens = chips * rows

    def take(weight, axis, index, size):
        return lax.dynamic_slice_in_dim(weight, index * size, size, axis)

    x_zero, x_one = [inputs[:, b] for b in range(seqs)]
    x_spread = jnp.broadcast_to(x_zero, (chips,) + x_zero.shape)
    near_zero = exchange(x_spread)
    w_query, w_key, w_value, w_out, w_gate, w_up, w_down, segments, deal_order = hold(
        (w_query, w_key, w_value, w_out, w_gate, w_up, w_down, segments, deal_order), x_spread
    )

    ids = jnp.stack([core, lax.axis_index("fsdp"), chip]).astype(jnp.int32)
    pair = jnp.arange(2, dtype=jnp.int32)
    rel_dev = (jnp.arange(chips, dtype=jnp.int32)[None, :] * 2) + (pair[:, None] ^ core)
    rel_slot = (rel_dev[:, :, None] * 2 + pair[None, None, :]).reshape(-1)
    near_chips = jnp.arange(chips, dtype=jnp.int32) ^ chip
    send_dev = near_chips[:, None] * 2 + (pair[None, :] ^ core)
    send_slot = (send_dev[:, :, None] * 2 + pair[None, None, :]).reshape(-1)
    spots = jnp.arange(blocks, dtype=jnp.int32)

    def look_up(slots):
        return jnp.sum(
            jnp.where(slots[:, None] == spots[None, :], deal_order[None, :], 0), axis=1
        ).astype(jnp.int32)

    rel_table = look_up(rel_slot)
    send_table = look_up(send_slot)
    earlier = (segments[None, :, :] < segments[:, None, :]).astype(jnp.int32)
    slot_start = jnp.sum(earlier, axis=1).astype(jnp.int32).reshape(blocks, blk, seqs)
    start = jnp.sum(
        jnp.where((deal_order[None, :] == spots[:, None])[:, :, None, None], slot_start[None], 0),
        axis=1,
    ).astype(jnp.int32)
    start = start.transpose(2, 0, 1).reshape(seqs, seq_len)

    def ranges(q_rows, k_rows):
        tiled = start.reshape(seqs, seq_len // q_rows, q_rows)
        begins = jnp.arange(seq_len // q_rows, dtype=jnp.int32) * q_rows // k_rows
        first = tiled[:, :, 0] // k_rows
        full = jnp.minimum(begins[None, :], (tiled[:, :, -1] + k_rows - 1) // k_rows)
        return tiled, first, full

    _, first, full = ranges(Q_FORE, K_FORE)
    tiled, first_back, full_back = ranges(Q_BACK, K_BACK)

    both = jnp.stack([gain_attn, gain_ffn], axis=1)
    spare = jnp.zeros((both.shape[0], -(3 * width + 2) % 128), bf16)
    own_qkv = jnp.concatenate(
        [take(w, 1, rank, width) for w in (w_query, w_key, w_value)] + [both, spare], axis=1
    )

    def hidden_columns(weight):
        return [take(weight, 1, rank + z * groups, per_shard) for z in range(shards)]

    own_gate_up = jnp.concatenate(hidden_columns(w_gate) + hidden_columns(w_up), axis=1)
    own_down = take(w_down, 0, rank, per_shard)
    out_grid = w_out.reshape(-1, 2, width, feats)
    own_out = take(out_grid, 1, core, 1).reshape(-1, feats)

    merged = 2 * hidden_width == feats
    if merged:
        ffn_own = [jnp.concatenate([own_gate_up, own_down])]
    else:
        ffn_own = [own_gate_up, own_down]
    qkv_pieces = shard_pieces(own_qkv)
    x_spread_one = jnp.broadcast_to(x_one, (chips,) + x_one.shape)
    cot_all = [cotangent[:, b] for b in range(seqs)]
    (
        near_zero, qkv_pieces, start, tiled, first, full, first_back, full_back, rel_table, send_table,
        x_spread_one, cot_all, own_out, ffn_own,
    ) = hold(
        (
            near_zero, qkv_pieces, start, tiled, first, full, first_back, full_back, rel_table, send_table,
            x_spread_one, cot_all, own_out, ffn_own,
        )
    )
    qkv = in_order(qkv_pieces, ids[1])
    gain_one, gain_two = qkv[:, 3 * width][None, :], qkv[:, 3 * width + 1][None, :]
    def flat(*pair):
        return [value.reshape(tokens, feats) for value in pair]

    def by_chip(value):
        return value.reshape(chips, rows, feats)

    def spread_cot(own):
        return lax.all_gather(own, PLANE, axis=0).reshape(chips, 2, rows, feats)

    tables = [(rel_table, send_table, first[b], full[b]) for b in range(seqs)]
    tables_back = [(rel_table, send_table, first_back[b], full_back[b]) for b in range(seqs)]

    def forward(b, near, far):
        query, key, value, normed, fine, logsum, *sent = attend_forward(
            tables[b], *flat(near, far), qkv, gain_one, start[b][:, None], width, chips
        )
        return (query, key, value, fine, logsum), normed, sent

    def mid_norm(x_own, own, swapped):
        middle = x_own.astype(f32) + own + swapped
        return middle, (middle * row_scale(middle) * gain_two.astype(f32)).astype(bf16)

    near_one = exchange(x_spread_one)
    out_pieces = shard_pieces(own_out)
    ffn_pieces = [lax.all_gather(value, "fsdp", axis=0) for value in ffn_own]
    saved_zero, normed_zero, sent_zero = forward(0, near_zero, swap_core(near_zero))
    near_one, sent_zero, out_pieces, cot_zero, cot_one = hold(
        (near_one, sent_zero, out_pieces, cot_all[0], cot_all[1])
    )
    near_cot = spread(cot_zero)
    got_zero = exchange_pieces(sent_zero)
    saved_one, normed_one, sent_one = forward(1, near_one, swap_core(near_one))
    got_zero, sent_one, near_cot = hold((got_zero, sent_one, near_cot))
    got_one = exchange_pieces(sent_one)
    att_zero, own, other = mix(ids, got_zero, out_pieces)
    mid_zero, norm_zero = mid_norm(x_zero, own, swap_core(other))
    norm_zero, got_one = hold((norm_zero, got_one))
    pieces_zero = send_copies(norm_zero)
    pieces_zero, got_one = hold((pieces_zero, got_one))
    near_zero = arrange(ids, pieces_zero)
    att_one, own, other = mix(ids, hold(got_one, near_zero), out_pieces)
    mid_one, norm_one = mid_norm(x_one, own, swap_core(other))
    cot_one, near_zero = hold((cot_one, near_zero))
    pieces_one = send_copies(norm_one)
    cots = (flat(near_cot, swap_core(near_cot)), [spread_cot(cot_one)])

    def ffn(b, near, far, split):
        mids = flat(near, far)
        *out_part, mid_near, mid_far, hidden, grad_pre = feed_forward(
            ids, mids, cots[b], ffn_pieces, hidden_width, split
        )
        return out_part, by_chip(mid_near), by_chip(mid_far), (*mids, hidden, grad_pre, *cots[b])

    out_zero, own_zero, far_zero, stream_zero = ffn(0, near_zero, swap_core(near_zero), False)
    near_one = arrange(ids, hold(pieces_one, stream_zero[2]))
    total_zero = core_sum(own_zero, swap_core(far_zero))
    near_far = hold((near_one, swap_core(near_one)), total_zero)
    out_one, own_one, far_one, stream_one = ffn(1, *near_far, False)
    sums_zero = hold(exchange(total_zero), stream_one[2])
    far_one = swap_core(far_one)
    ffn_sums = weight_sums(ids, (stream_zero, stream_one), shards)
    shares = [lax.psum_scatter(value, "fsdp", scatter_dimension=0) for value in ffn_sums]
    sums_zero, far_one = hold((sums_zero, far_one), ffn_sums[0])
    total_one = core_sum(own_one, far_one)

    def collect_out(part):
        flat_part = part.reshape(groups * rows, feats)
        return lax.psum_scatter(flat_part, PLANE, scatter_dimension=0, tiled=True)

    out_sum_zero = collect_out(out_zero[0])

    def mid_backward(b, grad_normed_mid, middle):
        scale_two = row_scale(middle)
        unit_two = middle * scale_two
        scaled_two = grad_normed_mid * gain_two.astype(f32)
        grad_middle = cot_all[b].astype(f32) + scale_two * (
            scaled_two - unit_two * jnp.mean(scaled_two * unit_two, axis=-1, keepdims=True)
        )
        return grad_middle, grad_middle.astype(bf16)

    def backward(b, saved, grad_got):
        return attend_backward(
            tables_back[b], saved, grad_got, qkv, tiled[b][:, None, :]
        )

    def qkv_stream(normed, grads):
        return normed.reshape(seq_len, feats), grads.reshape(seq_len, 3 * width)

    def in_backward(grad_normed_in, grad_middle, x_own):
        flat_in = x_own.astype(f32)
        scale_one = row_scale(flat_in)
        unit_one = flat_in * scale_one
        scaled_one = grad_normed_in * gain_one.astype(f32)
        return (
            grad_middle
            + scale_one
            * (scaled_one - unit_one * jnp.mean(scaled_one * unit_one, axis=-1, keepdims=True))
        ).astype(bf16)

    grad_mid_zero, branch = mid_backward(0, last_sum(sums_zero), mid_zero)
    grad_sent, grad_out_zero = unmix(ids, branch, swap_core(branch), att_zero, out_pieces, chips)
    total_one = hold(total_one, grad_sent)
    grad_got_zero = hold(exchange_pieces(grad_sent), out_sum_zero)
    sums_one = exchange(total_one)
    part_near, part_far, grads_zero = backward(0, saved_zero, grad_got_zero)
    sums_one = hold(sums_one, grads_zero)
    far_swapped = swap_core(by_chip(part_far))
    grad_mid_one, branch = mid_backward(1, last_sum(sums_one), mid_one)
    grad_sent, grad_out_one = unmix(ids, branch, swap_core(branch), att_one, out_pieces, chips)
    grad_got_one = exchange_pieces(grad_sent)
    far_swapped = hold(far_swapped, grad_sent)
    total_zero = core_sum(by_chip(part_near), far_swapped)
    sums_zero = exchange(total_zero)

    own_rows = feats // shards

    def rel_rows(value):
        value = value.astype(bf16)
        count = value.shape[0] // shards
        return [take(value, 0, ids[1] ^ r, count) for r in range(shards)]

    out_rel = rel_rows(grad_out_zero + grad_out_one)
    out_sent = send_pieces(out_rel)
    grad_got_one, shares = hold((grad_got_one, shares), total_zero)
    full_ffn = [lax.all_gather(share, PLANE, axis=0) for share in shares]
    part_near, part_far, grads_one = backward(1, saved_one, grad_got_one)
    qkv_one = qkv_first(*qkv_stream(normed_one, grads_one))
    part_near, part_far, qkv_one, sums_zero, out_sent = hold(
        (part_near, part_far, qkv_one, sums_zero, out_sent)
    )
    far_swapped = swap_core(by_chip(part_far))
    grad_qkv = qkv_sums(ids, *qkv_stream(normed_zero, grads_zero), qkv_one, shards)
    part_near, far_swapped = hold((part_near, far_swapped), grad_qkv)
    total_one = core_sum(by_chip(part_near), far_swapped)
    sums_one = exchange(total_one)
    full_ffn = hold(full_ffn, total_one)
    own_rows = feats // shards
    g_gate_up, g_gain_two, (g_down,) = assemble(
        [full_ffn[0]],
        gain_ffn,
        (w_gate, w_up),
        shards,
        full_ffn[-1],
        own_rows if merged else 0,
        per_shard,
    )
    g_down = g_down.reshape(-1, feats)
    sent_qkv = send_pieces(grad_qkv)
    sums_one, g_gate_up, g_gain_two, g_down = hold((sums_one, g_gate_up, g_gain_two, g_down))
    share_qkv = add_pieces(grad_qkv[0], sent_qkv)
    out_sum_one = collect_out(hold(out_one[0], g_down, sent_qkv))
    share_out = add_pieces(out_rel[0], out_sent)
    spare = share_out.size // rows
    if share_qkv.shape[0] == rows and spare % 128 == 0:
        beside = jnp.concatenate([share_qkv, share_out.reshape(rows, spare)], axis=1)
        mixed = spread(hold(beside, sums_one))
        near_qkv = mixed[:, :, : 3 * width]
        own_sum = last_sum(mixed[:, :, 3 * width :]).reshape(-1, width, feats)
        other_sum = swap_core(own_sum)
        sides = (own_sum, other_sum)
        g_out = jnp.stack(
            [jnp.where(core == 0, *sides), jnp.where(core == 0, *sides[::-1])], axis=1
        ).reshape(own_rows, feats)
    else:
        near_qkv = spread(hold(share_qkv, sums_one))
        all_out = lax.all_gather(share_out, PLANE, axis=0).astype(f32)
        all_out = all_out.reshape(chips, 2, -1, width, feats)
        g_out = jnp.sum(all_out, axis=0).transpose(1, 0, 2, 3).reshape(own_rows, feats)

    outputs = [
        (mid_zero + out_sum_zero.astype(f32)).astype(bf16),
        (mid_one + out_sum_one.astype(f32)).astype(bf16),
    ]
    grad_inputs = [
        in_backward(last_sum(sums_zero), grad_mid_zero, x_zero),
        in_backward(last_sum(sums_one), grad_mid_one, x_one),
    ]
    far_qkv = swap_core(near_qkv)
    g_qkv, g_gain_one, _ = assemble(
        [ids, near_qkv, far_qkv], gain_attn, (w_query, w_key, w_value), 1
    )

    return (
        jnp.stack(outputs, axis=1),
        jnp.stack(grad_inputs, axis=1),
        *g_qkv,
        g_out,
        *g_gate_up,
        g_down,
        g_gain_one,
        g_gain_two,
    )


def solution(mesh):
    names = mesh.axis_names
    ctx, shards = mesh.shape[names[0]], mesh.shape[names[1]]
    fine_mesh = Mesh(mesh.devices.reshape(ctx // 2, 2, shards), ("chip", "core", "fsdp"))
    by_row = P("fsdp", None)
    by_token = P(PLANE, "fsdp", None)
    return jax.shard_map(
        per_device,
        mesh=fine_mesh,
        in_specs=(by_token,) + (by_row,) * 7 + (P("fsdp"), P("fsdp"), P(None, "fsdp"), P(), by_token),
        out_specs=(by_token, by_token) + (by_row,) * 7 + (P("fsdp"), P("fsdp")),
        check_vma=False,
    )
```

```python
import functools

import jax
import jax.numpy as jnp
from jax import lax
from jax.experimental import pallas as pl
from jax.experimental.pallas import tpu as pltpu
from jax.sharding import Mesh, PartitionSpec as P

HEAD_DIM = 64
EPSILON = 1e-05
MASKED = -1e30
TILE = 256
PROJ = 512
Q_FORE, K_FORE = 512, 512
Q_BACK, K_BACK = 512, 512
PLANE = ("chip", "core")

bf16 = jnp.bfloat16
f32 = jnp.float32


def dot_nn(left_op, right_op):
    return lax.dot_general(left_op, right_op, (((1,), (0,)), ((), ())), preferred_element_type=f32)


def dot_nt(left_op, right_op):
    return lax.dot_general(left_op, right_op, (((1,), (1,)), ((), ())), preferred_element_type=f32)


def dot_tn(left_op, right_op):
    return lax.dot_general(left_op, right_op, (((0,), (0,)), ((), ())), preferred_element_type=f32)


def row_scale(values):
    return lax.rsqrt(jnp.mean(values * values, axis=-1, keepdims=True) + EPSILON)


def swap_core(value):
    return lax.ppermute(value, "core", [(0, 1), (1, 0)])


def swap_chip(value, mask):
    count = lax.axis_size("chip")
    return lax.ppermute(value, "chip", [(i, i ^ mask) for i in range(count)])


def swap_shard(value, mask):
    count = lax.axis_size("fsdp")
    return lax.ppermute(value, "fsdp", [(i, i ^ mask) for i in range(count)])


def hold(value, *deps):
    return lax.optimization_barrier((value, deps))[0]


def spread(value):
    count = lax.axis_size("chip")
    return exchange(jnp.broadcast_to(value, (count,) + value.shape))


def exchange(value):
    return lax.all_to_all(value, "chip", 0, 0)


def arrange_kernel(ids, *refs):
    out = refs[-1]
    for r, piece in enumerate(refs[:-1]):
        out[ids[2] ^ r] = piece[...]


def arrange(ids, pieces):
    return pl.pallas_call(
        arrange_kernel,
        out_shape=jax.ShapeDtypeStruct((len(pieces),) + pieces[0].shape, bf16),
        in_specs=[smem()] + [vmem()] * len(pieces),
        out_specs=vmem(),
        compiler_params=LIMIT,
        cost_estimate=cost(3),
        name="arrange",
    )(ids, *pieces)


def send_copies(value):
    return exchange_pieces([value] * lax.axis_size("chip"))


def add_kernel(own, other, total):
    total[...] = (own[...].astype(f32) + other[...].astype(f32)).astype(bf16)


def exchange_pieces(pieces):
    return [pieces[0]] + [swap_chip(pieces[r], r) for r in range(1, len(pieces))]


def core_sum(own, swapped):
    chips, rows, width = own.shape
    block = pl.BlockSpec((chips // 2, rows, width), lambda t: (t, 0, 0))
    return pl.pallas_call(
        add_kernel,
        grid=(2,),
        out_shape=jax.ShapeDtypeStruct(own.shape, bf16),
        in_specs=[block, block],
        out_specs=block,
        cost_estimate=cost(3),
        name="core_sum",
    )(own, swapped)


def last_sum(value):
    return jnp.sum(value.astype(f32), axis=0)


def shard_pieces(value):
    return [value] + [swap_shard(value, r) for r in range(1, lax.axis_size("fsdp"))]


def shard_sum(pieces):
    return add_pieces(pieces[0], send_pieces(pieces))


def in_order(pieces, shard):
    stacked = jnp.stack(pieces)
    rows = [lax.dynamic_index_in_dim(stacked, shard ^ z, keepdims=False) for z in range(len(pieces))]
    return jnp.concatenate(rows)


def send_pieces(pieces):
    return [swap_shard(pieces[r], r) for r in range(1, len(pieces))]


def add_pieces(own, received):
    total = own.astype(f32)
    for piece in received:
        total = total + piece.astype(f32)
    return total.astype(bf16)


def head_masks(rows, width):
    lanes = lax.broadcasted_iota(jnp.int32, (rows, width), 1) // HEAD_DIM
    return [lanes == h for h in range(width // HEAD_DIM)]


def stack_heads(values, masks):
    zero = jnp.zeros_like(values)
    return jnp.concatenate([jnp.where(mask, values, zero) for mask in masks], axis=0)


def merge_heads(stacked, masks, rows):
    merged = stacked[:rows]
    for h in range(1, len(masks)):
        merged = jnp.where(masks[h], stacked[h * rows : (h + 1) * rows], merged)
    return merged


def forward_kernel(
    rel, send, first, full, x_near, x_far, weight, gain, start,
    query_out, key_out, value_out, normed, fine_out, logsum_out, *refs,
):
    attended, refs = refs[:-13], refs[-13:]
    query, key, value, fine, logsum, x_tiles, normed_tiles, scores, top, total = refs[:10]
    in_sems, normed_sems, out_sems = refs[10:]
    width = query.shape[1]
    seq_len = query.shape[0]
    heads = width // HEAD_DIM
    blk = TILE // 2
    tiles = x_near.shape[0] // PROJ
    blocks = PROJ // blk
    gain_row = gain[...].astype(f32)
    loads, stores = [], []
    for i in range(2 * tiles):
        rows = pl.ds(i % tiles * PROJ, PROJ)
        source = x_near if i < tiles else x_far
        loads.append(pltpu.make_async_copy(source.at[rows], x_tiles.at[i], in_sems.at[i]))
        stores.append(
            pltpu.make_async_copy(
                normed_tiles.at[i], normed.at[i // tiles, rows], normed_sems.at[i]
            )
        )
        loads[i].start()
    for i in range(2 * tiles):
        loads[i].wait()
        rows_in = x_tiles[i].astype(f32)
        tile = (rows_in * row_scale(rows_in) * gain_row).astype(bf16)
        normed_tiles[i] = tile
        stores[i].start()
        mixed = dot_nn(tile, weight[:, : 3 * width])
        for h in range(blocks):
            where = pl.ds(pl.multiple_of(rel[i * blocks + h] * blk, blk), blk)
            part = mixed[h * blk : (h + 1) * blk]
            query[where, :] = (part[:, :width].astype(bf16) * 0.125).astype(bf16)
            key[where, :] = part[:, width : 2 * width].astype(bf16)
            value[where, :] = part[:, 2 * width :].astype(bf16)
    for i, (source, target) in enumerate(
        ((query, query_out), (key, key_out), (value, value_out))
    ):
        stores.append(pltpu.make_async_copy(source, target, out_sems.at[i]))
        stores[-1].start()

    masks = head_masks(Q_FORE, width)
    big = heads * Q_FORE

    def query_tile(qb, _):
        rows = pl.ds(pl.multiple_of(qb * Q_FORE, Q_FORE), Q_FORE)
        stacked = stack_heads(query[rows, :], masks)
        top[...] = jnp.full_like(top, MASKED)
        begin = jnp.concatenate([start[rows, :]] * heads, axis=0)
        diagonal = qb * Q_FORE // K_FORE
        last = (qb * Q_FORE + Q_FORE + K_FORE - 1) // K_FORE

        def score(kb, masked):
            keys = key[pl.ds(pl.multiple_of(kb * K_FORE, K_FORE), K_FORE), :]
            raw = dot_nt(stacked, keys)
            if masked:
                k_pos = kb * K_FORE + lax.broadcasted_iota(jnp.int32, (big, K_FORE), 1)
                q_row = lax.broadcasted_iota(jnp.int32, (big, K_FORE), 0) & (Q_FORE - 1)
                allowed = (k_pos >= begin) & (k_pos <= qb * Q_FORE + q_row)
                raw = jnp.where(allowed, raw, MASKED)
            scores[kb] = raw
            best = raw[:, :128]
            for c in range(1, K_FORE // 128):
                best = jnp.maximum(best, raw[:, c * 128 : (c + 1) * 128])
            top[...] = jnp.maximum(top[...], best)

        def masked_step(kb, _):
            score(kb, True)
            return 0

        def plain_step(kb, _):
            score(kb, False)
            return 0

        lax.fori_loop(first[qb], full[qb], masked_step, 0)
        lax.fori_loop(full[qb], diagonal, plain_step, 0)
        lax.fori_loop(diagonal, last, masked_step, 0)
        peak = jnp.max(top[...], axis=1, keepdims=True)
        top[...] = jnp.broadcast_to(peak, top.shape)
        total[...] = jnp.zeros_like(total)

        def weigh(kb, carry):
            vals = value[pl.ds(pl.multiple_of(kb * K_FORE, K_FORE), K_FORE), :]
            pieces = []
            summed = total[...]
            for c in range(K_FORE // 128):
                piece = jnp.exp(scores[kb, :, c * 128 : (c + 1) * 128] - top[...])
                summed = summed + piece
                pieces.append(piece.astype(bf16))
            total[...] = summed
            return carry + dot_nn(jnp.concatenate(pieces, axis=1), vals)

        gathered = lax.fori_loop(first[qb], last, weigh, jnp.zeros((big, width), f32))
        denom = jnp.sum(total[...], axis=1, keepdims=True)
        fine[rows, :] = merge_heads(gathered / denom, masks, Q_FORE)
        logs = jnp.broadcast_to(peak + jnp.log(denom), (big, width))
        logsum[rows, :] = merge_heads(logs, masks, Q_FORE)
        return 0

    lax.fori_loop(0, seq_len // Q_FORE, query_tile, 0)
    for i, (source, target) in enumerate(((fine, fine_out), (logsum, logsum_out))):
        stores.append(pltpu.make_async_copy(source, target, out_sems.at[3 + i]))
        stores[-1].start()

    count = seq_len // blk // len(attended)
    for r, piece in enumerate(attended):
        for j in range(count):
            where = pl.ds(pl.multiple_of(send[r * count + j] * blk, blk), blk)
            piece[j * blk : (j + 1) * blk, :] = fine[where, :].astype(bf16)
    for copy in stores:
        copy.wait()


def backward_kernel(
    rel, send, first, full, query, key, value, fine, logsum, weight, start, *refs
):
    grad_in, refs = refs[:-13], refs[-13:]
    part_near, part_far, grads_out, grad_at, grad_q, grad_k, grad_v, grad_q2 = refs[:8]
    parts, grads, local_weight, sems, weight_sem = refs[8:]
    load = pltpu.make_async_copy(weight, local_weight, weight_sem)
    load.start()
    seq_len, width = query.shape
    heads = width // HEAD_DIM
    blk = TILE // 2
    big = heads * Q_BACK

    count = seq_len // blk // len(grad_in)
    for r, piece in enumerate(grad_in):
        for j in range(count):
            where = pl.ds(pl.multiple_of(send[r * count + j] * blk, blk), blk)
            grad_at[where, :] = piece[j * blk : (j + 1) * blk, :]
    grad_k[...] = jnp.zeros_like(grad_k)
    grad_v[...] = jnp.zeros_like(grad_v)
    masks = head_masks(Q_BACK, width)

    def flip(values):
        if width < 128:
            values = jnp.concatenate([values, jnp.zeros((Q_BACK, 128 - width), f32)], axis=1)
        return values.T

    def query_tile(qb, _):
        rows = pl.ds(pl.multiple_of(qb * Q_BACK, Q_BACK), Q_BACK)
        stacked = stack_heads(query[rows, :], masks)
        grad_rows = grad_at[rows, :]
        grad_stacked = stack_heads(grad_rows, masks)
        products = flip(grad_rows.astype(f32) * fine[rows, :])
        logs = flip(logsum[rows, :])
        delta = jnp.concatenate(
            [
                jnp.sum(products[h * HEAD_DIM : (h + 1) * HEAD_DIM], axis=0, keepdims=True)
                for h in range(heads)
            ],
            axis=1,
        )
        log_row = jnp.concatenate(
            [logs[h * HEAD_DIM : h * HEAD_DIM + 1] for h in range(heads)], axis=1
        )
        begin = jnp.concatenate([start[qb]] * heads, axis=1)
        grad_q2[...] = jnp.zeros_like(grad_q2)
        diagonal = qb * Q_BACK // K_BACK
        last = (qb * Q_BACK + Q_BACK + K_BACK - 1) // K_BACK

        def step(kb, masked):
            where = pl.ds(pl.multiple_of(kb * K_BACK, K_BACK), K_BACK)
            keys = key[where, :]
            probs = jnp.exp(dot_nt(keys, stacked) - log_row)
            if masked:
                k_pos = kb * K_BACK + lax.broadcasted_iota(jnp.int32, (K_BACK, big), 0)
                q_row = lax.broadcasted_iota(jnp.int32, (K_BACK, big), 1) & (Q_BACK - 1)
                allowed = (k_pos >= begin) & (k_pos <= qb * Q_BACK + q_row)
                probs = jnp.where(allowed, probs, 0.0)
            slope = (probs * (dot_nt(value[where, :], grad_stacked) - delta)).astype(bf16)
            grad_v[where, :] += dot_nn(probs.astype(bf16), grad_stacked)
            grad_k[where, :] += dot_nn(slope, stacked)
            grad_q2[...] += dot_tn(slope, keys)

        def masked_step(kb, _):
            step(kb, True)
            return 0

        def plain_step(kb, _):
            step(kb, False)
            return 0

        lax.fori_loop(first[qb], full[qb], masked_step, 0)
        lax.fori_loop(full[qb], diagonal, plain_step, 0)
        lax.fori_loop(diagonal, last, masked_step, 0)
        grad_q[rows, :] = (merge_heads(grad_q2[...], masks, Q_BACK) * 0.125).astype(bf16)
        return 0

    lax.fori_loop(0, seq_len // Q_BACK, query_tile, 0)

    tiles = seq_len // PROJ // 2
    blocks = PROJ // blk
    load.wait()
    stores = []
    for i in range(2 * tiles):
        rows = pl.ds(i % tiles * PROJ, PROJ)
        for h in range(blocks):
            where = pl.ds(pl.multiple_of(rel[i * blocks + h] * blk, blk), blk)
            here = pl.ds(h * blk, blk)
            grads[i, here, :width] = grad_q[where, :]
            grads[i, here, width : 2 * width] = grad_k[where, :].astype(bf16)
            grads[i, here, 2 * width :] = grad_v[where, :].astype(bf16)
        target = grads_out.at[i // tiles, rows]
        stores.append(pltpu.make_async_copy(grads.at[i], target, sems.at[0, i]))
        stores[-1].start()
        parts[i] = dot_nt(grads[i], local_weight[:, : 3 * width]).astype(bf16)
        target = (part_near if i < tiles else part_far).at[rows]
        stores.append(pltpu.make_async_copy(parts.at[i], target, sems.at[1, i]))
        stores[-1].start()
    for copy in stores:
        copy.wait()


def place_pieces(target, pieces, shard, begin, count):
    for r, piece in enumerate(pieces):
        at = pl.multiple_of((shard ^ r) * count, count)
        target[pl.ds(at, count), :] = piece[begin : begin + count, :]


def near_first(target, source, chip, count):
    for r in range(count):
        rows = target.shape[0] // count
        at = pl.multiple_of((chip ^ r) * rows, rows)
        target[r * rows : (r + 1) * rows, :] = source[pl.ds(at, rows), :]


def mix_kernel(ids, *refs, chips):
    got, pieces, (attended, own, other, whole, weight) = refs[:chips], refs[chips:-5], refs[-5:]
    rows = own.shape[0]
    place_pieces(whole, pieces, ids[1], 0, pieces[0].shape[0])
    near_first(weight, whole, ids[2], chips)
    joined = jnp.concatenate([piece[...] for piece in got], axis=1)
    attended[...] = joined
    own[...] = dot_nn(joined[:rows], weight[...])
    other[...] = dot_nn(joined[rows:], weight[...])


def unmix_kernel(ids, own, other, attended, *refs, chips):
    outs = chips + 3
    pieces, grad_sent, (grad_weight, whole, weight) = refs[:-outs], refs[-outs:-3], refs[-3:]
    place_pieces(whole, pieces, ids[1], 0, pieces[0].shape[0])
    near_first(weight, whole, ids[2], chips)
    branch = jnp.concatenate([own[...], other[...]], axis=0)
    mixed = dot_nt(branch, weight[...]).astype(bf16)
    sums = dot_tn(attended[...], branch)
    width = grad_sent[0].shape[1]
    for r in range(chips):
        grad_sent[r][...] = mixed[:, r * width : (r + 1) * width]
        at = pl.multiple_of((ids[2] ^ r) * width, width)
        grad_weight[pl.ds(at, width), :] = sums[r * width : (r + 1) * width]


def qkv_kernel(ids, *refs):
    normed, grads, before = refs[:3]
    outs, total = refs[3:-1], refs[-1]
    t = pl.program_id(0)

    @pl.when(t == 0)
    def _():
        total[...] = before[...]

    total[...] += dot_tn(normed[...], grads[...])

    @pl.when(t == pl.num_programs(0) - 1)
    def _():
        rows = outs[0].shape[0]
        for r, out in enumerate(outs):
            at = pl.multiple_of((ids[1] ^ r) * rows, rows)
            out[...] = total[pl.ds(at, rows), :].astype(bf16)


def ffn_kernel(ids, x_near, x_far, *refs, split, sides):
    cot_refs, refs = refs[:sides], refs[sides:]
    outs = 7 + split
    pieces, out_parts = refs[:-outs], refs[-outs : 1 + split - outs]
    mid_near, mid_far, hidden, grad_pre, gate_up, down = refs[-6:]
    t = pl.program_id(0)
    half = pl.num_programs(0) // 2
    feats, size = gate_up.shape[0], gate_up.shape[1] // 2
    shards = pieces[0].shape[0]
    rows, more = feats // shards, size // shards
    begin = rows if len(pieces) == 1 else 0

    @pl.when(t == 0)
    def _():
        for z in range(shards):
            gate_up[z * rows : (z + 1) * rows, :] = pieces[0][z, :rows, :]
            down[z * more : (z + 1) * more, :] = pieces[-1][z, begin : begin + more, :]

    tile = jnp.where(t < half, x_near[...], x_far[...])
    cot = cot_refs[0][...].reshape(tile.shape)
    if sides == 2:
        cot = jnp.where(t < half, cot, cot_refs[1][...])
    pre = dot_nn(tile, gate_up[...])
    gate_pre, up_pre = pre[:, :size], pre[:, size:]
    sigma = 0.5 * jnp.tanh(0.5 * gate_pre) + 0.5
    active = gate_pre * sigma
    low = (active * up_pre).astype(bf16)
    grad_hidden = dot_nt(cot, down[...])
    hidden[...] = low
    out_part = dot_nn(low, down[...]).astype(bf16)
    grad_gate = grad_hidden * up_pre * sigma * (1.0 + gate_pre * (1.0 - sigma))
    grad_up = grad_hidden * active
    grads = jnp.concatenate([grad_gate.astype(bf16), grad_up.astype(bf16)], axis=1)
    grad_pre[...] = grads
    mid_part = dot_nt(grads, gate_up[...]).astype(bf16)

    if not split:
        out_parts[0][...] = out_part.reshape(out_parts[0].shape)

    @pl.when(t < half)
    def _():
        mid_near[...] = mid_part
        if split:
            out_parts[0][...] = out_part

    @pl.when(t >= half)
    def _():
        mid_far[...] = mid_part
        if split:
            out_parts[1][...] = out_part


def weight_kernel(ids, *refs, counts, shards):
    streams = len(counts)
    ins, outs, (wide, down) = refs[: sum(counts)], refs[sum(counts) : -2], refs[-2:]
    t = pl.program_id(0)
    per = pl.num_programs(0) // streams

    @pl.when(t == 0)
    def _():
        wide[...] = jnp.zeros_like(wide)
        down[...] = jnp.zeros_like(down)

    for b in range(streams):
        mine = ins[sum(counts[:b]) : sum(counts[: b + 1])]

        @pl.when((t >= b * per) & (t < (b + 1) * per))
        def _(b=b, mine=mine):
            x_near, x_far, hidden, grad_pre = mine[:4]
            near = t < b * per + per // 2
            tile = jnp.where(near, x_near[...], x_far[...])
            cot = mine[4][...].reshape(tile.shape)
            if len(mine) == 6:
                cot = jnp.where(near, cot, mine[5][...])
            wide[...] += dot_tn(tile, grad_pre[...])
            down[...] += dot_tn(hidden[...], cot)

    @pl.when(t == pl.num_programs(0) - 1)
    def _():
        rows, more = wide.shape[0] // shards, down.shape[0] // shards
        begin = rows if len(outs) == 1 else 0
        for z in range(shards):
            outs[0][z, :rows, :] = wide[z * rows : (z + 1) * rows, :].astype(bf16)
            piece = down[z * more : (z + 1) * more, :]
            outs[-1][z, begin : begin + more, :] = piece.astype(bf16)


def assemble_kernel(*refs, kinds, shards, with_down, sides):
    sources, gain = refs[:sides], refs[sides]
    if sides == 1:
        parts = sources[0]
    else:
        ids, near, far = sources
        parts = []
        for p in range(near.shape[0]):
            own, other = near[p], far[p]
            parts.append(jnp.where(ids[0] == 0, own, other))
            parts.append(jnp.where(ids[0] == 0, other, own))
    refs = refs[sides - 1 :]
    weights = refs[2 : 2 + kinds]
    rest = refs[2 + kinds :]
    if with_down:
        down_part, rest = rest[0], rest[1:]
    outs, gain_out = rest[:kinds], rest[kinds]
    groups = len(parts) if sides > 1 else parts.shape[0]
    size = sources[-1].shape[2]
    pieces = size // kinds
    lanes = pieces // shards
    sums = 0.0
    for k in range(kinds):
        columns = []
        for z in range(shards):
            for i in range(groups):
                at = k * pieces + z * lanes
                columns.append(parts[i][:, at : at + lanes].astype(f32))
        full = jnp.concatenate(columns, axis=1)
        outs[k][...] = full
        sums = sums + jnp.sum(full * weights[k][...].astype(f32), axis=1, keepdims=True)
    gain_out[...] = sums / gain[...].astype(f32)
    if with_down:
        rest[kinds + 1][...] = down_part[...].astype(f32)


def smem():
    return pl.BlockSpec(memory_space=pltpu.SMEM)


def hbm():
    return pl.BlockSpec(memory_space=pl.ANY)


def vmem():
    return pl.BlockSpec(memory_space=pltpu.VMEM)


def cost(micros):
    return pl.CostEstimate(flops=micros * 10**9, bytes_accessed=2**20, transcendentals=0)


LIMIT = pltpu.CompilerParams(vmem_limit_bytes=56 * 2**20)


def attend_forward(tables, x_near, x_far, weight, gain, start, width, chips):
    half_rows, feats = x_near.shape
    seq_len = 2 * half_rows
    big = (width // HEAD_DIM) * Q_FORE
    shape = jax.ShapeDtypeStruct
    narrow = shape((seq_len, width), bf16)
    wide = shape((seq_len, width), f32)
    pairs = seq_len * seq_len * width // 2
    return pl.pallas_call(
        forward_kernel,
        out_shape=[narrow, narrow, narrow, shape((2, half_rows, feats), bf16), wide, wide]
        + [shape((seq_len // chips, width), bf16)] * chips,
        in_specs=[smem()] * 4 + [hbm()] * 2 + [vmem()] * 3,
        out_specs=[hbm()] * 6 + [vmem()] * chips,
        scratch_shapes=[
            pltpu.VMEM((seq_len, width), bf16),
            pltpu.VMEM((seq_len, width), bf16),
            pltpu.VMEM((seq_len, width), bf16),
            pltpu.VMEM((seq_len, width), f32),
            pltpu.VMEM((seq_len, width), f32),
            pltpu.VMEM((seq_len // PROJ, PROJ, feats), bf16),
            pltpu.VMEM((seq_len // PROJ, PROJ, feats), bf16),
            pltpu.VMEM((seq_len // K_FORE, big, K_FORE), f32),
            pltpu.VMEM((big, 128), f32),
            pltpu.VMEM((big, 128), f32),
            pltpu.SemaphoreType.DMA((seq_len // PROJ,)),
            pltpu.SemaphoreType.DMA((seq_len // PROJ,)),
            pltpu.SemaphoreType.DMA((5,)),
        ],
        compiler_params=LIMIT,
        cost_estimate=cost(31),
        name="attend_forward",
    )(*tables, x_near, x_far, weight, gain, start)


def attend_backward(tables, saved, grad_in, weight, start):
    query = saved[0]
    seq_len, width = query.shape
    feats = weight.shape[0]
    big = (width // HEAD_DIM) * Q_BACK
    shape = jax.ShapeDtypeStruct
    pairs = seq_len * seq_len * width // 2
    return pl.pallas_call(
        backward_kernel,
        out_shape=(
            shape((seq_len // 2, feats), bf16),
            shape((seq_len // 2, feats), bf16),
            shape((2, seq_len // 2, 3 * width), bf16),
        ),
        in_specs=[smem()] * 4 + [vmem()] * 5 + [hbm()] + [vmem()] * (1 + len(grad_in)),
        out_specs=[hbm()] * 3,
        scratch_shapes=[
            pltpu.VMEM((seq_len, width), bf16),
            pltpu.VMEM((seq_len, width), bf16),
            pltpu.VMEM((seq_len, width), f32),
            pltpu.VMEM((seq_len, width), f32),
            pltpu.VMEM((big, width), f32),
            pltpu.VMEM((seq_len // PROJ, PROJ, feats), bf16),
            pltpu.VMEM((seq_len // PROJ, PROJ, 3 * width), bf16),
            pltpu.VMEM(weight.shape, bf16),
            pltpu.SemaphoreType.DMA((2, seq_len // PROJ)),
            pltpu.SemaphoreType.DMA,
        ],
        compiler_params=LIMIT,
        cost_estimate=cost(31),
        name="attend_backward",
    )(*tables, *saved, weight, start, *grad_in)


def mix(ids, got, pieces):
    chips = len(got)
    doubled, width = got[0].shape
    feats = pieces[0].shape[1]
    size = chips * width
    shape = jax.ShapeDtypeStruct
    return pl.pallas_call(
        functools.partial(mix_kernel, chips=chips),
        out_shape=(
            shape((doubled, size), bf16),
            shape((doubled // 2, feats), f32),
            shape((doubled // 2, feats), f32),
        ),
        in_specs=[smem()] + [vmem()] * (chips + len(pieces)),
        out_specs=[vmem()] * 3,
        scratch_shapes=[pltpu.VMEM((size, feats), bf16)] * 2,
        compiler_params=LIMIT,
        cost_estimate=cost(3),
        name="mix",
    )(ids, *got, *pieces)


def unmix(ids, own, other, attended, pieces, chips):
    rows, feats = own.shape
    size = attended.shape[1]
    shape = jax.ShapeDtypeStruct
    outs = pl.pallas_call(
        functools.partial(unmix_kernel, chips=chips),
        out_shape=[shape((2 * rows, size // chips), bf16)] * chips + [shape((size, feats), f32)],
        in_specs=[smem()] + [vmem()] * (3 + len(pieces)),
        out_specs=[vmem()] * (chips + 1),
        scratch_shapes=[pltpu.VMEM((size, feats), bf16)] * 2,
        compiler_params=LIMIT,
        cost_estimate=cost(4),
        name="unmix",
    )(ids, own, other, attended, *pieces)
    return outs[:-1], outs[-1]


ROWS = 512


def feed_forward(ids, mids, cot, pieces, size, split):
    tokens, feats = mids[0].shape
    rows = ROWS // 2
    chips = tokens // rows
    half = tokens // ROWS
    shape = jax.ShapeDtypeStruct
    near = pl.BlockSpec((ROWS, feats), lambda t, ids: (jnp.minimum(t, half - 1), 0))
    far = pl.BlockSpec((ROWS, feats), lambda t, ids: (jnp.maximum(t - half, 0), 0))
    by_device = pl.BlockSpec(
        (ROWS // rows, None, rows, feats),
        lambda t, ids: (lax.rem(t, half), ids[0] ^ lax.div(t, half), 0, 0),
    )
    cot_specs = [by_device] if len(cot) == 1 else [near, far]

    def tiles(width):
        return pl.BlockSpec((ROWS, width), lambda t, ids: (t, 0))

    side = shape((tokens, feats), bf16)
    return pl.pallas_call(
        functools.partial(ffn_kernel, split=split, sides=len(cot)),
        grid_spec=pltpu.PrefetchScalarGridSpec(
            num_scalar_prefetch=1,
            grid=(2 * half,),
            in_specs=[near, far, *cot_specs]
            + [pl.BlockSpec(piece.shape, lambda t, ids: (0, 0, 0)) for piece in pieces],
            out_specs=([near, far] if split else [by_device])
            + [near, far, tiles(size), tiles(2 * size)],
            scratch_shapes=[
                pltpu.VMEM((feats, 2 * size), bf16),
                pltpu.VMEM((size, feats), bf16),
            ],
        ),
        out_shape=([side, side] if split else [shape((chips, 2, rows, feats), bf16)])
        + [
            side,
            side,
            shape((2 * tokens, size), bf16),
            shape((2 * tokens, 2 * size), bf16),
        ],
        compiler_params=LIMIT,
        cost_estimate=cost(20),
        name="feed_forward",
    )(ids, *mids, *cot, *pieces)


def weight_sums(ids, streams, shards):
    tokens, feats = streams[0][0].shape
    size = streams[0][2].shape[1]
    rows = ROWS // 2
    half = tokens // ROWS
    per = 2 * half
    shape = jax.ShapeDtypeStruct
    specs = []
    for b in range(len(streams)):

        def local(t, b=b):
            return jnp.clip(t - b * per, 0, per - 1)

        near = pl.BlockSpec(
            (ROWS, feats), lambda t, ids, f=local: (jnp.minimum(f(t), half - 1), 0)
        )
        far = pl.BlockSpec(
            (ROWS, feats), lambda t, ids, f=local: (jnp.maximum(f(t) - half, 0), 0)
        )
        by_device = pl.BlockSpec(
            (ROWS // rows, None, rows, feats),
            lambda t, ids, f=local: (lax.rem(f(t), half), ids[0] ^ lax.div(f(t), half), 0, 0),
        )
        specs += [
            near,
            far,
            pl.BlockSpec((ROWS, size), lambda t, ids, f=local: (f(t), 0)),
            pl.BlockSpec((ROWS, 2 * size), lambda t, ids, f=local: (f(t), 0)),
        ]
        specs += [by_device] if len(streams[b]) == 5 else [near, far]
    if 2 * size == feats:
        outs = [(shards, (feats + size) // shards, feats)]
    else:
        outs = [(shards, feats // shards, 2 * size), (shards, size // shards, feats)]
    return pl.pallas_call(
        functools.partial(weight_kernel, counts=[len(v) for v in streams], shards=shards),
        grid_spec=pltpu.PrefetchScalarGridSpec(
            num_scalar_prefetch=1,
            grid=(per * len(streams),),
            in_specs=specs,
            out_specs=[pl.BlockSpec(out, lambda t, ids: (0, 0, 0)) for out in outs],
            scratch_shapes=[pltpu.VMEM((feats, 2 * size), f32), pltpu.VMEM((size, feats), f32)],
        ),
        out_shape=[shape(out, bf16) for out in outs],
        compiler_params=LIMIT,
        cost_estimate=cost(23),
        name="weight_sums",
    )(ids, *[value for stream in streams for value in stream])


def qkv_first(normed, grads):
    tokens, feats = normed.shape
    size = grads.shape[1]

    def kernel(normed_ref, grads_ref, total):
        @pl.when(pl.program_id(0) == 0)
        def _():
            total[...] = jnp.zeros_like(total)

        total[...] += dot_tn(normed_ref[...], grads_ref[...])

    return pl.pallas_call(
        kernel,
        grid=(tokens // ROWS,),
        out_shape=jax.ShapeDtypeStruct((feats, size), f32),
        in_specs=[
            pl.BlockSpec((ROWS, feats), lambda t: (t, 0)),
            pl.BlockSpec((ROWS, size), lambda t: (t, 0)),
        ],
        out_specs=pl.BlockSpec((feats, size), lambda t: (0, 0)),
        compiler_params=LIMIT,
        cost_estimate=cost(6),
        name="qkv_first",
    )(normed, grads)


def qkv_sums(ids, normed, grads, before, shards):
    tokens, feats = normed.shape
    size = grads.shape[1]
    out = (feats // shards, size)
    return pl.pallas_call(
        qkv_kernel,
        grid_spec=pltpu.PrefetchScalarGridSpec(
            num_scalar_prefetch=1,
            grid=(tokens // ROWS,),
            in_specs=[
                pl.BlockSpec((ROWS, feats), lambda t, ids: (t, 0)),
                pl.BlockSpec((ROWS, size), lambda t, ids: (t, 0)),
                pl.BlockSpec((feats, size), lambda t, ids: (0, 0)),
            ],
            out_specs=[pl.BlockSpec(out, lambda t, ids: (0, 0))] * shards,
            scratch_shapes=[pltpu.VMEM((feats, size), f32)],
        ),
        out_shape=[jax.ShapeDtypeStruct(out, bf16)] * shards,
        compiler_params=LIMIT,
        cost_estimate=cost(6),
        name="qkv_sums",
    )(ids, normed, grads, before)


STEPS = 4


def assemble(parts, gain, weights, shards, downs=None, begin=0, down_rows=0):
    rows, columns = weights[0].shape
    step = rows // STEPS
    shape = jax.ShapeDtypeStruct
    sides = len(parts)
    groups, size = parts[-1].shape[0] * min(2, sides), parts[-1].shape[2]
    row_block = pl.BlockSpec((step, columns), lambda t: (t, 0))
    thin = pl.BlockSpec((step, 1), lambda t: (t, 0))
    count = len(weights)
    args = [*parts, gain[:, None], *weights]
    share_spec = pl.BlockSpec((parts[-1].shape[0], step, size), lambda t: (0, t, 0))
    in_specs = [share_spec] if sides == 1 else [smem(), share_spec, share_spec]
    in_specs += [thin] + [row_block] * count
    out_shape = [shape((rows, columns), f32)] * count + [shape((rows, 1), f32)]
    out_specs = [row_block] * count + [thin]
    if down_rows:
        share, feats = groups // STEPS, downs.shape[2]
        args.append(downs)
        in_specs.append(
            pl.BlockSpec((share, down_rows, feats), lambda t: (t, begin // down_rows, 0))
        )
        out_shape.append(shape((groups, down_rows, feats), f32))
        out_specs.append(pl.BlockSpec((share, down_rows, feats), lambda t: (t, 0, 0)))
    outs = pl.pallas_call(
        functools.partial(
            assemble_kernel, kinds=count, shards=shards, with_down=bool(down_rows), sides=sides
        ),
        grid=(STEPS,),
        out_shape=out_shape,
        in_specs=in_specs,
        out_specs=out_specs,
        compiler_params=LIMIT,
        cost_estimate=cost(2),
        name="assemble",
    )(*args)
    return outs[:count], outs[count][:, 0], outs[count + 1 :]


def per_device(
    inputs, w_query, w_key, w_value, w_out, w_gate, w_up, w_down,
    gain_attn, gain_ffn, segments, deal_order, cotangent,
):
    rows, seqs, feats = inputs.shape
    chips = lax.axis_size("chip")
    groups = 2 * chips
    shards = lax.axis_size("fsdp")
    chip = lax.axis_index("chip")
    core = lax.axis_index("core")
    rank = chip * 2 + core
    width = feats // groups
    hidden_width = w_gate.shape[1] // groups
    per_shard = hidden_width // shards
    seq_len = rows * groups
    blocks = deal_order.shape[0]
    blk = rows // 2
    tokens = chips * rows

    def take(weight, axis, index, size):
        return lax.dynamic_slice_in_dim(weight, index * size, size, axis)

    x_zero, x_one = [inputs[:, b] for b in range(seqs)]
    x_spread = jnp.broadcast_to(x_zero, (chips,) + x_zero.shape)
    near_zero = exchange(x_spread)
    w_query, w_key, w_value, w_out, w_gate, w_up, w_down, segments, deal_order = hold(
        (w_query, w_key, w_value, w_out, w_gate, w_up, w_down, segments, deal_order), x_spread
    )

    ids = jnp.stack([core, lax.axis_index("fsdp"), chip]).astype(jnp.int32)
    pair = jnp.arange(2, dtype=jnp.int32)
    rel_dev = (jnp.arange(chips, dtype=jnp.int32)[None, :] * 2) + (pair[:, None] ^ core)
    rel_slot = (rel_dev[:, :, None] * 2 + pair[None, None, :]).reshape(-1)
    near_chips = jnp.arange(chips, dtype=jnp.int32) ^ chip
    send_dev = near_chips[:, None] * 2 + (pair[None, :] ^ core)
    send_slot = (send_dev[:, :, None] * 2 + pair[None, None, :]).reshape(-1)
    spots = jnp.arange(blocks, dtype=jnp.int32)

    def look_up(slots):
        return jnp.sum(
            jnp.where(slots[:, None] == spots[None, :], deal_order[None, :], 0), axis=1
        ).astype(jnp.int32)

    rel_table = look_up(rel_slot)
    send_table = look_up(send_slot)
    earlier = (segments[None, :, :] < segments[:, None, :]).astype(jnp.int32)
    slot_start = jnp.sum(earlier, axis=1).astype(jnp.int32).reshape(blocks, blk, seqs)
    start = jnp.sum(
        jnp.where((deal_order[None, :] == spots[:, None])[:, :, None, None], slot_start[None], 0),
        axis=1,
    ).astype(jnp.int32)
    start = start.transpose(2, 0, 1).reshape(seqs, seq_len)

    def ranges(q_rows, k_rows):
        tiled = start.reshape(seqs, seq_len // q_rows, q_rows)
        begins = jnp.arange(seq_len // q_rows, dtype=jnp.int32) * q_rows // k_rows
        first = tiled[:, :, 0] // k_rows
        full = jnp.minimum(begins[None, :], (tiled[:, :, -1] + k_rows - 1) // k_rows)
        return tiled, first, full

    _, first, full = ranges(Q_FORE, K_FORE)
    tiled, first_back, full_back = ranges(Q_BACK, K_BACK)

    both = jnp.stack([gain_attn, gain_ffn], axis=1)
    spare = jnp.zeros((both.shape[0], -(3 * width + 2) % 128), bf16)
    own_qkv = jnp.concatenate(
        [take(w, 1, rank, width) for w in (w_query, w_key, w_value)] + [both, spare], axis=1
    )

    def hidden_columns(weight):
        return [take(weight, 1, rank + z * groups, per_shard) for z in range(shards)]

    own_gate_up = jnp.concatenate(hidden_columns(w_gate) + hidden_columns(w_up), axis=1)
    own_down = take(w_down, 0, rank, per_shard)
    out_grid = w_out.reshape(-1, 2, width, feats)
    own_out = take(out_grid, 1, core, 1).reshape(-1, feats)

    merged = 2 * hidden_width == feats
    if merged:
        ffn_own = [jnp.concatenate([own_gate_up, own_down])]
    else:
        ffn_own = [own_gate_up, own_down]
    qkv_pieces = shard_pieces(own_qkv)
    x_spread_one = jnp.broadcast_to(x_one, (chips,) + x_one.shape)
    cot_all = [cotangent[:, b] for b in range(seqs)]
    (
        near_zero, qkv_pieces, start, tiled, first, full, first_back, full_back, rel_table, send_table,
        x_spread_one, cot_all, own_out, ffn_own,
    ) = hold(
        (
            near_zero, qkv_pieces, start, tiled, first, full, first_back, full_back, rel_table, send_table,
            x_spread_one, cot_all, own_out, ffn_own,
        )
    )
    qkv = in_order(qkv_pieces, ids[1])
    gain_one, gain_two = qkv[:, 3 * width][None, :], qkv[:, 3 * width + 1][None, :]
    def flat(*pair):
        return [value.reshape(tokens, feats) for value in pair]

    def by_chip(value):
        return value.reshape(chips, rows, feats)

    def spread_cot(own):
        return lax.all_gather(own, PLANE, axis=0).reshape(chips, 2, rows, feats)

    tables = [(rel_table, send_table, first[b], full[b]) for b in range(seqs)]
    tables_back = [(rel_table, send_table, first_back[b], full_back[b]) for b in range(seqs)]

    def forward(b, near, far):
        query, key, value, normed, fine, logsum, *sent = attend_forward(
            tables[b], *flat(near, far), qkv, gain_one, start[b][:, None], width, chips
        )
        return (query, key, value, fine, logsum), normed, sent

    def mid_norm(x_own, own, swapped):
        middle = x_own.astype(f32) + own + swapped
        return middle, (middle * row_scale(middle) * gain_two.astype(f32)).astype(bf16)

    near_one = exchange(x_spread_one)
    out_pieces = shard_pieces(own_out)
    ffn_pieces = [lax.all_gather(value, "fsdp", axis=0) for value in ffn_own]
    saved_zero, normed_zero, sent_zero = forward(0, near_zero, swap_core(near_zero))
    near_one, sent_zero, out_pieces, cot_zero, cot_one = hold(
        (near_one, sent_zero, out_pieces, cot_all[0], cot_all[1])
    )
    near_cot = spread(cot_zero)
    got_zero = exchange_pieces(sent_zero)
    saved_one, normed_one, sent_one = forward(1, near_one, swap_core(near_one))
    got_zero, sent_one, near_cot = hold((got_zero, sent_one, near_cot))
    got_one = exchange_pieces(sent_one)
    att_zero, own, other = mix(ids, got_zero, out_pieces)
    mid_zero, norm_zero = mid_norm(x_zero, own, swap_core(other))
    norm_zero, got_one = hold((norm_zero, got_one))
    pieces_zero = send_copies(norm_zero)
    pieces_zero, got_one = hold((pieces_zero, got_one))
    near_zero = arrange(ids, pieces_zero)
    att_one, own, other = mix(ids, hold(got_one, near_zero), out_pieces)
    mid_one, norm_one = mid_norm(x_one, own, swap_core(other))
    cot_one, near_zero = hold((cot_one, near_zero))
    pieces_one = send_copies(norm_one)
    cots = (flat(near_cot, swap_core(near_cot)), [spread_cot(cot_one)])

    def ffn(b, near, far, split):
        mids = flat(near, far)
        *out_part, mid_near, mid_far, hidden, grad_pre = feed_forward(
            ids, mids, cots[b], ffn_pieces, hidden_width, split
        )
        return out_part, by_chip(mid_near), by_chip(mid_far), (*mids, hidden, grad_pre, *cots[b])

    out_zero, own_zero, far_zero, stream_zero = ffn(0, near_zero, swap_core(near_zero), False)
    near_one = arrange(ids, hold(pieces_one, stream_zero[2]))
    total_zero = core_sum(own_zero, swap_core(far_zero))
    near_far = hold((near_one, swap_core(near_one)), total_zero)
    out_one, own_one, far_one, stream_one = ffn(1, *near_far, False)
    sums_zero = hold(exchange(total_zero), stream_one[2])
    far_one = swap_core(far_one)
    ffn_sums = weight_sums(ids, (stream_zero, stream_one), shards)
    shares = [lax.psum_scatter(value, "fsdp", scatter_dimension=0) for value in ffn_sums]
    sums_zero, far_one = hold((sums_zero, far_one), ffn_sums[0])
    total_one = core_sum(own_one, far_one)

    def collect_out(part):
        flat_part = part.reshape(groups * rows, feats)
        return lax.psum_scatter(flat_part, PLANE, scatter_dimension=0, tiled=True)

    out_sum_zero = collect_out(out_zero[0])

    def mid_backward(b, grad_normed_mid, middle):
        scale_two = row_scale(middle)
        unit_two = middle * scale_two
        scaled_two = grad_normed_mid * gain_two.astype(f32)
        grad_middle = cot_all[b].astype(f32) + scale_two * (
            scaled_two - unit_two * jnp.mean(scaled_two * unit_two, axis=-1, keepdims=True)
        )
        return grad_middle, grad_middle.astype(bf16)

    def backward(b, saved, grad_got):
        return attend_backward(
            tables_back[b], saved, grad_got, qkv, tiled[b][:, None, :]
        )

    def qkv_stream(normed, grads):
        return normed.reshape(seq_len, feats), grads.reshape(seq_len, 3 * width)

    def in_backward(grad_normed_in, grad_middle, x_own):
        flat_in = x_own.astype(f32)
        scale_one = row_scale(flat_in)
        unit_one = flat_in * scale_one
        scaled_one = grad_normed_in * gain_one.astype(f32)
        return (
            grad_middle
            + scale_one
            * (scaled_one - unit_one * jnp.mean(scaled_one * unit_one, axis=-1, keepdims=True))
        ).astype(bf16)

    grad_mid_zero, branch = mid_backward(0, last_sum(sums_zero), mid_zero)
    grad_sent, grad_out_zero = unmix(ids, branch, swap_core(branch), att_zero, out_pieces, chips)
    total_one = hold(total_one, grad_sent)
    grad_got_zero = hold(exchange_pieces(grad_sent), out_sum_zero)
    sums_one = exchange(total_one)
    part_near, part_far, grads_zero = backward(0, saved_zero, grad_got_zero)
    sums_one = hold(sums_one, grads_zero)
    far_swapped = swap_core(by_chip(part_far))
    grad_mid_one, branch = mid_backward(1, last_sum(sums_one), mid_one)
    grad_sent, grad_out_one = unmix(ids, branch, swap_core(branch), att_one, out_pieces, chips)
    grad_got_one = exchange_pieces(grad_sent)
    far_swapped = hold(far_swapped, grad_sent)
    total_zero = core_sum(by_chip(part_near), far_swapped)
    sums_zero = exchange(total_zero)

    own_rows = feats // shards

    def rel_rows(value):
        value = value.astype(bf16)
        count = value.shape[0] // shards
        return [take(value, 0, ids[1] ^ r, count) for r in range(shards)]

    out_rel = rel_rows(grad_out_zero + grad_out_one)
    out_sent = send_pieces(out_rel)
    grad_got_one, shares = hold((grad_got_one, shares), total_zero)
    full_ffn = [lax.all_gather(share, PLANE, axis=0) for share in shares]
    part_near, part_far, grads_one = backward(1, saved_one, grad_got_one)
    qkv_one = qkv_first(*qkv_stream(normed_one, grads_one))
    part_near, part_far, qkv_one, sums_zero, out_sent = hold(
        (part_near, part_far, qkv_one, sums_zero, out_sent)
    )
    far_swapped = swap_core(by_chip(part_far))
    grad_qkv = qkv_sums(ids, *qkv_stream(normed_zero, grads_zero), qkv_one, shards)
    part_near, far_swapped = hold((part_near, far_swapped), grad_qkv)
    total_one = core_sum(by_chip(part_near), far_swapped)
    sums_one = exchange(total_one)
    full_ffn = hold(full_ffn, total_one)
    own_rows = feats // shards
    g_gate_up, g_gain_two, (g_down,) = assemble(
        [full_ffn[0]],
        gain_ffn,
        (w_gate, w_up),
        shards,
        full_ffn[-1],
        own_rows if merged else 0,
        per_shard,
    )
    g_down = g_down.reshape(-1, feats)
    sent_qkv = send_pieces(grad_qkv)
    share_qkv = add_pieces(grad_qkv[0], sent_qkv)
    share_out = add_pieces(out_rel[0], out_sent)
    spare = share_out.size // rows
    together = share_qkv.shape[0] == rows and spare % 128 == 0
    beside = share_qkv
    if together:
        beside = jnp.concatenate([share_qkv, share_out.reshape(rows, spare)], axis=1)
        beside = jnp.broadcast_to(beside, (chips,) + beside.shape)
    sums_one, g_gate_up, g_gain_two, g_down, beside = hold(
        (sums_one, g_gate_up, g_gain_two, g_down, beside)
    )
    out_sum_one = collect_out(hold(out_one[0], g_down, sent_qkv))
    if together:
        mixed = exchange(beside)
        near_qkv = mixed[:, :, : 3 * width]
        own_sum = last_sum(mixed[:, :, 3 * width :]).reshape(-1, width, feats)
        other_sum = swap_core(own_sum)
        sides = (own_sum, other_sum)
        g_out = jnp.stack(
            [jnp.where(core == 0, *sides), jnp.where(core == 0, *sides[::-1])], axis=1
        ).reshape(own_rows, feats)
    else:
        near_qkv = spread(hold(share_qkv, sums_one))
        all_out = lax.all_gather(share_out, PLANE, axis=0).astype(f32)
        all_out = all_out.reshape(chips, 2, -1, width, feats)
        g_out = jnp.sum(all_out, axis=0).transpose(1, 0, 2, 3).reshape(own_rows, feats)

    outputs = [
        (mid_zero + out_sum_zero.astype(f32)).astype(bf16),
        (mid_one + out_sum_one.astype(f32)).astype(bf16),
    ]
    grad_inputs = [
        in_backward(last_sum(sums_zero), grad_mid_zero, x_zero),
        in_backward(last_sum(sums_one), grad_mid_one, x_one),
    ]
    far_qkv = swap_core(near_qkv)
    g_qkv, g_gain_one, _ = assemble(
        [ids, near_qkv, far_qkv], gain_attn, (w_query, w_key, w_value), 1
    )

    return (
        jnp.stack(outputs, axis=1),
        jnp.stack(grad_inputs, axis=1),
        *g_qkv,
        g_out,
        *g_gate_up,
        g_down,
        g_gain_one,
        g_gain_two,
    )


def solution(mesh):
    names = mesh.axis_names
    ctx, shards = mesh.shape[names[0]], mesh.shape[names[1]]
    fine_mesh = Mesh(mesh.devices.reshape(ctx // 2, 2, shards), ("chip", "core", "fsdp"))
    by_row = P("fsdp", None)
    by_token = P(PLANE, "fsdp", None)
    return jax.shard_map(
        per_device,
        mesh=fine_mesh,
        in_specs=(by_token,) + (by_row,) * 7 + (P("fsdp"), P("fsdp"), P(None, "fsdp"), P(), by_token),
        out_specs=(by_token, by_token) + (by_row,) * 7 + (P("fsdp"), P("fsdp")),
        check_vma=False,
    )
```
